32 devices in a mesh: dp: 8 (over z, y), mp: 4 (over x, core).
Axes of the slice: x: 2, y: 2, z: 4, core: 2. Of those that a mesh axis runs over, the one named last changes fastest.
Arguments:
- inputs: bfloat16 [4, 40, 197, 768], P(None, 'dp'), may hold values from -6 to 6
- cotangent: bfloat16 [4, 40, 197, 768], P(None, 'dp'), may hold values from -6 to 6
- counts: int32 [4, 8], P(None, 'dp'), may hold values from 3 to 5, as said below
- norm_gain: float32 [768], replicated, may hold values from 0.5 to 1.5
- norm_shift: float32 [768], replicated, may hold values from -1.75 to 1.75
- qkv_weight: bfloat16 [768, 2304], P('dp', 'mp'), may hold values from -0.21875 to 0.21875
- query_bias: float32 [768], P('mp'), may hold values from -1.75 to 1.75
- value_bias: float32 [768], P('mp'), may hold values from -1.75 to 1.75
- out_weight: bfloat16 [768, 768], P('mp', 'dp'), may hold values from -0.875 to 0.875
- out_bias: float32 [768], replicated, may hold values from -1.75 to 1.75
- mlp_gain: float32 [768], replicated, may hold values from 0.5 to 1.5
- mlp_shift: float32 [768], replicated, may hold values from -1.75 to 1.75
- hidden_weight: bfloat16 [768, 3072], P('dp', 'mp'), may hold values from -0.21875 to 0.21875
- hidden_bias: float32 [3072], P('mp'), may hold values from -1.75 to 1.75
- down_weight: bfloat16 [3072, 768], P('mp', 'dp'), may hold values from -0.109375 to 0.109375
- down_bias: float32 [768], replicated, may hold values from -1.75 to 1.75
Outputs:
- block_out: bfloat16 [4, 40, 197, 768], P(None, 'dp')
- input_grad: bfloat16 [4, 40, 197, 768], P(None, 'dp')
- grad_norm_gain: float32 [768], replicated
- grad_norm_shift: float32 [768], replicated
- grad_qkv_weight: float32 [768, 2304], P('dp', 'mp')
- grad_query_bias: float32 [768], P('mp')
- grad_value_bias: float32 [768], P('mp')
- grad_out_weight: float32 [768, 768], P('mp', 'dp')
- grad_out_bias: float32 [768], replicated
- grad_mlp_gain: float32 [768], replicated
- grad_mlp_shift: float32 [768], replicated
- grad_hidden_weight: float32 [768, 3072], P('dp', 'mp')
- grad_hidden_bias: float32 [3072], P('mp')
- grad_down_weight: float32 [3072, 768], P('mp', 'dp')
- grad_down_bias: float32 [768], replicated
The draws below stay inside these ranges and needn't reach their ends.
Inputs may be any that keep to these rules, and one draw needn't show every extreme that they name: Live images fill the first counts[m, b] slots of block b; in every micro-batch some block holds 5 live images.
All inputs are finite; a program needn't handle non-finite values.
Results may differ from the reference program's by a relative error of at most 0.019.
Values may be sent and summed in bfloat16 or wider, within the bound.
No kernel may reach another device: no remote copies, remote signals or barrier semaphores. Data moves between devices by JAX's collectives and lax.ppermute only.
A program may use at most 256 MiB of HBM per device.

```python
import jax
import jax.numpy as jnp
from jax import lax

D = 768
HEADS = 12
HEAD_DIM = 64
FF = 3072
SEQ = 197
IMG_DEV = 5
MICRO = 4
IMAGES = 40
N_DP = 8
N_MP = 4


def draw_counts(key, part):
    count_key, pick_key = jax.random.split(key)
    fewest = (IMG_DEV + 1) // 2
    drawn = jax.random.randint(count_key, (MICRO, N_DP), fewest, IMG_DEV + 1)
    busiest = jax.random.randint(pick_key, (MICRO, 1), 0, N_DP)
    is_full = jnp.arange(N_DP)[None, :] == busiest
    return jnp.where(is_full, IMG_DEV, drawn).astype(jnp.int32)


def shard_levels(stream_key, dims, shards, smallest, high):
    gain, own = 1.0, jax.random.fold_in(stream_key, 6)
    for position, parts in shards:
        draws = jnp.exp(jax.random.uniform(jax.random.fold_in(own, position), (parts,), jnp.float32, smallest / len(shards), high / len(shards)))
        gain = gain * jnp.repeat(draws, dims[position] // parts).reshape([-1 if axis == position else 1 for axis in range(len(dims))])
    return gain


def centred(stream_key, shape, deviation, most, pieces=(), kind=jnp.bfloat16):
    values = jax.random.normal(stream_key, shape, jnp.float32) * deviation
    if len(pieces) > 0:
        values = shard_levels(stream_key, shape, pieces, -0.22, 0.18) * values
    return jnp.clip(values, min=-most, max=most).astype(kind)


def setup_inputs(seed: int = 0) -> dict:
    streams_of = jax.random.split(jax.random.key(seed), 17)
    inputs = centred(streams_of[0], (MICRO, IMAGES, SEQ, D), 1.0, 6.0, ((1, 8),))
    cotangent = centred(streams_of[1], (MICRO, IMAGES, SEQ, D), 1.0, 6.0, ((1, 8),))
    counts = draw_counts(jax.random.fold_in(streams_of[16], 71), 0)
    norm_gain = jnp.clip(1.0 + 0.1 * jax.random.normal(streams_of[3], (D,), jnp.float32), 0.5, 1.5)
    norm_shift = centred(streams_of[4], (D,), 0.3, 1.75, (), jnp.float32)
    qkv_weight = centred(streams_of[5], (D, 3 * D), D ** -0.5, 0.21875, ((0, 8), (1, 4)))
    query_bias = centred(streams_of[6], (D,), 0.3, 1.75, ((0, 4),), jnp.float32)
    value_bias = centred(streams_of[7], (D,), 0.3, 1.75, ((0, 4),), jnp.float32)
    out_weight = centred(streams_of[8], (D, D), (D // 16) ** -0.5, 0.875, ((0, 4), (1, 8)))
    out_bias = centred(streams_of[9], (D,), 0.3, 1.75, (), jnp.float32)
    mlp_gain = jnp.clip(1.0 + 0.1 * jax.random.normal(streams_of[10], (D,), jnp.float32), 0.5, 1.5)
    mlp_shift = centred(streams_of[11], (D,), 0.3, 1.75, (), jnp.float32)
    hidden_weight = centred(streams_of[12], (D, FF), D ** -0.5, 0.21875, ((0, 8), (1, 4)))
    hidden_bias = centred(streams_of[13], (FF,), 0.3, 1.75, ((0, 4),), jnp.float32)
    down_weight = centred(streams_of[14], (FF, D), FF ** -0.5, 0.109375, ((0, 4), (1, 8)))
    down_bias = centred(streams_of[15], (D,), 0.3, 1.75, (), jnp.float32)
    return dict(inputs=inputs, cotangent=cotangent, counts=counts, norm_gain=norm_gain, norm_shift=norm_shift, qkv_weight=qkv_weight, query_bias=query_bias, value_bias=value_bias, out_weight=out_weight, out_bias=out_bias, mlp_gain=mlp_gain, mlp_shift=mlp_shift, hidden_weight=hidden_weight, hidden_bias=hidden_bias, down_weight=down_weight, down_bias=down_bias)


NORM_EPS = 1e-06
EXACT = lax.Precision.HIGHEST

@jax.custom_vjp
def low(v):
    return lax.optimization_barrier(v.astype(jnp.bfloat16)).astype(jnp.float32)

@jax.custom_vjp
def low_back(v):
    return v

def low_keep(v):
    return (low(v), None)

def low_pass(kept, grad):
    return (grad,)

def back_keep(v):
    return (v, None)

def back_low(kept, grad):
    return (low(grad),)
low.defvjp(low_keep, low_pass)
low_back.defvjp(back_keep, back_low)

def layer_norm(values, gain_vec, shift_vec):
    center = lax.optimization_barrier(jnp.mean(values, axis=-1, keepdims=True))
    offset = values - center
    spread = lax.optimization_barrier(jnp.mean(offset * offset, axis=-1, keepdims=True))
    return offset * lax.rsqrt(spread + NORM_EPS) * gain_vec + shift_vec

def gelu_exact(values):
    return 0.5 * values * (1.0 + lax.erf(values * 0.7071067811865476))

def block_forward(params, images, count_now):
    norm_gain, norm_shift, qkv_weight, query_bias, value_bias, out_weight, out_bias, mlp_gain, mlp_shift, hidden_weight, hidden_bias, down_weight, down_bias = params
    groups = N_MP
    per_group = HEADS // N_MP
    normed = low(layer_norm(images, norm_gain, norm_shift))
    shared = low_back(jnp.broadcast_to(normed[None], (groups,) + normed.shape))
    qkv_split = qkv_weight.reshape(D, groups, 3, per_group, HEAD_DIM)
    projected = jnp.einsum('gisd,dgtlh->gistlh', shared, qkv_split, precision=EXACT)
    key_zeros = jnp.zeros((groups, per_group, HEAD_DIM), jnp.float32)
    biases = jnp.stack([query_bias.reshape(groups, per_group, HEAD_DIM), key_zeros, value_bias.reshape(groups, per_group, HEAD_DIM)], axis=1)
    projected = low(low_back(projected + biases[:, None, None]))
    queries = projected[:, :, :, 0]
    key_vecs = projected[:, :, :, 1]
    value_vecs = projected[:, :, :, 2]
    scores = low_back(jnp.einsum('gislh,gitlh->gilst', queries, key_vecs, precision=EXACT) * 0.125)
    row_max = lax.optimization_barrier(jnp.max(scores, axis=-1, keepdims=True))
    exp_scores = jnp.exp(scores - row_max)
    attn_probs = exp_scores / lax.optimization_barrier(jnp.sum(exp_scores, axis=-1, keepdims=True))
    mixed_heads = jnp.einsum('gilst,gitlh->gislh', low(attn_probs), value_vecs, precision=EXACT)
    mixed_heads = low(low_back(mixed_heads))
    out_split = out_weight.reshape(groups, per_group, HEAD_DIM, D)
    partial_value = jnp.einsum('gislh,glhd->gisd', mixed_heads, out_split, precision=EXACT)
    attended = low_back(lax.optimization_barrier(jnp.sum(low(partial_value), axis=0))) + out_bias
    middle = images + attended
    normed_two = low(layer_norm(middle, mlp_gain, mlp_shift))
    shared_two = low_back(jnp.broadcast_to(normed_two[None], (groups,) + normed_two.shape))
    hidden_split = hidden_weight.reshape(D, groups, FF // groups)
    pre_act = jnp.einsum('gisd,dgf->gisf', shared_two, hidden_split, precision=EXACT)
    pre_act = low_back(pre_act + hidden_bias.reshape(groups, 1, 1, FF // groups))
    activated = low(gelu_exact(pre_act))
    down_split = down_weight.reshape(groups, FF // groups, D)
    partial_two = jnp.einsum('gisf,gfd->gisd', activated, down_split, precision=EXACT)
    result = middle + low_back(lax.optimization_barrier(jnp.sum(low(partial_two), axis=0))) + down_bias
    live_mask = (jnp.arange(IMG_DEV, dtype=jnp.int32) < count_now).astype(jnp.float32)
    return result * live_mask[:, None, None]

def reference(inputs, cotangent, counts, norm_gain, norm_shift, qkv_weight, query_bias, value_bias, out_weight, out_bias, mlp_gain, mlp_shift, hidden_weight, hidden_bias, down_weight, down_bias):
    params = tuple((weight.astype(jnp.float32) for weight in (norm_gain, norm_shift, qkv_weight, query_bias, value_bias, out_weight, out_bias, mlp_gain, mlp_shift, hidden_weight, hidden_bias, down_weight, down_bias)))
    blocks = inputs.astype(jnp.float32).reshape(MICRO * N_DP, IMG_DEV, SEQ, D)
    cot_blocks = cotangent.astype(jnp.float32).reshape(MICRO * N_DP, IMG_DEV, SEQ, D)
    flat_counts = counts.reshape(MICRO * N_DP).astype(jnp.int32)

    def whole(block_inputs, weights):

        def one_block(packed):
            return block_forward(weights, packed[0], packed[1])
        return lax.map(jax.checkpoint(one_block), (block_inputs, flat_counts))
    outputs, pullback = jax.vjp(whole, blocks, params)
    grad_blocks, weight_grads = pullback(cot_blocks)
    g_norm_gain, g_norm_shift, g_qkv, g_query, g_value, g_out, g_out_bias, g_mlp_gain, g_mlp_shift, g_hidden, g_hidden_bias, g_down, g_down_bias = weight_grads
    block_out = outputs.reshape(MICRO, IMAGES, SEQ, D).astype(jnp.bfloat16)
    input_grad = grad_blocks.reshape(MICRO, IMAGES, SEQ, D).astype(jnp.bfloat16)
    return (block_out, input_grad, g_norm_gain, g_norm_shift, g_qkv, g_query, g_value, g_out, g_out_bias, g_mlp_gain, g_mlp_shift, g_hidden, g_hidden_bias, g_down, g_down_bias)
```

```python
import functools
import jax
import jax.numpy as jnp
from jax import lax
from jax.experimental import pallas as pl
from jax.experimental.pallas import tpu as pltpu
from jax.sharding import PartitionSpec as P

HEAD_DIM = 64
NORM_EPS = 1e-06
SLOT_ROWS = 200
ROWS = 1024
BF = jnp.bfloat16
F32 = jnp.float32
NT = (((1,), (1,)), ((), ()))
NN = (((1,), (0,)), ((), ()))
TN = (((0,), (0,)), ((), ()))


def dot(a, b, dims=NN):
    return lax.dot_general(a, b, dims, preferred_element_type=F32)


def norm_stats(values):
    center = jnp.mean(values, axis=-1, keepdims=True)
    offset = values - center
    spread = jnp.mean(offset * offset, axis=-1, keepdims=True)
    scale_inv = lax.rsqrt(spread + NORM_EPS)
    return offset * scale_inv, scale_inv


def norm_back(upstream, normal, scale_inv, gain_vec):
    scaled = upstream * gain_vec
    return scale_inv * (
        scaled
        - jnp.mean(scaled, axis=-1, keepdims=True)
        - normal * jnp.mean(scaled * normal, axis=-1, keepdims=True)
    )


def colsum(values):
    return jnp.sum(values, axis=0, keepdims=True)


def call(body, outs, ins, in_specs=None, out_specs=None, grid=None, scratch=(), flops=0, nbytes=0, limit=60, **kw):
    full = lambda a: pl.BlockSpec(a.shape, (lambda *_: (0,) * len(a.shape)))
    if in_specs is None:
        in_specs = [None] * len(ins)
    if out_specs is None:
        out_specs = [None] * len(outs)
    in_specs = [full(a) if s is None else s for a, s in zip(ins, in_specs)]
    out_specs = [full(a) if s is None else s for a, s in zip(outs, out_specs)]
    nbytes = sum(a.size * a.dtype.itemsize for a in ins) + sum(a.size * a.dtype.itemsize for a in outs)
    return pl.pallas_call(
        body,
        out_shape=tuple(outs),
        grid=(1,) if grid is None else grid,
        in_specs=in_specs,
        out_specs=tuple(out_specs),
        scratch_shapes=list(scratch),
        compiler_params=pltpu.CompilerParams(vmem_limit_bytes=limit * 1024 * 1024),
        cost_estimate=pl.CostEstimate(flops=flops, bytes_accessed=nbytes, transcendentals=0),
        **kw,
    )(*ins)


def sds(shape, dtype):
    return jax.ShapeDtypeStruct(shape, dtype)


def loop(n, fn):
    lax.fori_loop(0, n, lambda i, c: (fn(i), c)[1], 0)


def cut(i, size):
    return pl.ds(pl.multiple_of(i * size, size), size)


def qkv_body(x_ref, gain_ref, shift_ref, wa_ref, bias_ref, h_ref, qkv_ref, wq_ref, wo_ref):
    parts, groups, sub, _ = wa_ref.shape
    width = x_ref.shape[1]
    local = width // groups
    for j in range(groups):
        w = wa_ref[:, j].reshape(parts * sub, 4 * local)
        for s in range(3):
            wq_ref[:, s * width + j * local : s * width + (j + 1) * local] = w[:, s * local : (s + 1) * local]
        wo_ref[:, j * local : (j + 1) * local] = w[:, 3 * local :]

    def norm(i):
        rows = cut(i, 128)
        normal, _ = norm_stats(x_ref[rows, :].astype(F32))
        h_ref[rows, :] = (normal * gain_ref[...] + shift_ref[...]).astype(BF)

    loop(ROWS // 128, norm)

    def project(n):
        cols = cut(n, 256)
        qkv_ref[:, cols] = (dot(h_ref[...], wq_ref[:, cols]) + bias_ref[:, cols]).astype(BF)

    loop(3 * width // 256, project)


def attend_body(slots, length, q_ref, k_ref, v_ref, o_ref, p_ref):
    low_half = lax.broadcasted_iota(jnp.int32, (SLOT_ROWS, 2 * HEAD_DIM), 1) < HEAD_DIM
    valid = lax.broadcasted_iota(jnp.int32, (SLOT_ROWS, SLOT_ROWS), 1) < length

    def image(i):
        rows = cut(i, SLOT_ROWS)
        q = q_ref[rows, :] * jnp.bfloat16(0.125)
        k = k_ref[rows, :]
        v = v_ref[rows, :]
        zero = jnp.zeros_like(q)
        mixed = []
        for h in range(2):
            s = dot(jnp.where(low_half if h == 0 else ~low_half, q, zero), k, NT)
            s = jnp.where(valid, s, -1e30)
            e = jnp.exp(s - jnp.max(s, axis=-1, keepdims=True))
            p = (e * (1.0 / jnp.sum(e, axis=-1, keepdims=True))).astype(BF)
            p_ref[h, i] = p
            mixed.append(dot(p, v))
        o_ref[rows, :] = jnp.where(low_half, mixed[0], mixed[1]).astype(BF)

    loop(slots, image)
    tail = slots * SLOT_ROWS
    o_ref[tail:, :] = jnp.zeros((ROWS - tail, 2 * HEAD_DIM), BF)


def mix_body(x_ref, o_ref, wo_ref, bias_ref, gain_ref, shift_ref, mid_ref, h_ref):
    mid_ref[...] = dot(o_ref[...], wo_ref[...], NT)

    def norm(i):
        rows = cut(i, 128)
        mid = x_ref[rows, :].astype(F32) + (mid_ref[rows, :] + bias_ref[...])
        mid_ref[rows, :] = mid
        normal, _ = norm_stats(mid)
        h_ref[rows, :] = (normal * gain_ref[...] + shift_ref[...]).astype(BF)

    loop(mid_ref.shape[0] // 128, norm)


def hidden_body(h_ref, w_ref, bias_ref, act_ref, slope_ref):
    parts, _, sub, cols = w_ref.shape
    w = w_ref[:, 0].reshape(parts * sub, cols)

    def chunk(i):
        rows = cut(i, 256)
        u = dot(h_ref[rows, :], w) + bias_ref[...]
        half = 0.5 * (1.0 + lax.erf(u * 0.7071067811865476))
        act_ref[rows, :] = (u * half).astype(BF)
        slope_ref[rows, :] = (half + u * jnp.exp(-0.5 * u * u) * 0.3989422804014327).astype(BF)

    loop(ROWS // 256, chunk)


def down_body(slots, length, live_ref, act_ref, wc_ref, mid_ref, bias_ref, out_ref, acc_ref):
    parts, groups, sub, cols = wc_ref.shape
    for j in range(groups):
        part = dot(act_ref[:, j * cols : (j + 1) * cols], wc_ref[:, j].reshape(parts * sub, cols), NT)
        if j == 0:
            acc_ref[...] = part
        else:
            acc_ref[...] += part
    for i in range(slots):
        rows = slice(i * SLOT_ROWS, (i + 1) * SLOT_ROWS)
        live = jnp.where(i < live_ref[0], 1.0, 0.0)
        value = (mid_ref[rows, :] + acc_ref[rows, :] + bias_ref[...]) * live
        out_ref[i] = value[:length].astype(BF)


def outer_body(left_ref, right_ref, g_ref, t_ref):
    @pl.when(pl.program_id(0) == 0)
    def _():
        t_ref[...] = left_ref[...].T

    parts, _, sub, cols = g_ref.shape
    g_ref[:, 0] = dot(t_ref[...], right_ref[...]).astype(BF).reshape(parts, sub, cols)


def dact_body(dy_ref, wc_ref, slope_ref, du_ref, sum_ref):
    parts, _, sub, cols = wc_ref.shape
    w = wc_ref[:, 0].reshape(parts * sub, cols)
    total = jnp.zeros((1, cols), F32)
    for i in range(ROWS // 256):
        rows = slice(i * 256, (i + 1) * 256)
        du = (dot(dy_ref[rows, :], w) * slope_ref[rows, :].astype(F32)).astype(BF)
        du_ref[rows, :] = du
        total = total + colsum(du.astype(F32))
    sum_ref[...] = jnp.broadcast_to(total, sum_ref.shape)


def mid_back_body(dy_ref, du_ref, wb_ref, mid_ref, gain_ref, dmid_ref, dlow_ref, sums_ref, acc_ref):
    parts, groups, sub, cols = wb_ref.shape
    for j in range(groups):
        part = dot(du_ref[:, j * cols : (j + 1) * cols], wb_ref[:, j].reshape(parts * sub, cols), NT)
        if j == 0:
            acc_ref[...] = part
        else:
            acc_ref[...] += part
    width = dy_ref.shape[1]

    def chunk(i, sums):
        rows = cut(i, 128)
        dh = acc_ref[rows, :]
        normal, scale_inv = norm_stats(mid_ref[rows, :])
        dy = dy_ref[rows, :].astype(F32)
        dmid = dy + norm_back(dh, normal, scale_inv, gain_ref[...])
        dmid_ref[rows, :] = dmid
        dlow_ref[rows, :] = dmid.astype(BF)
        new = (colsum(dh * normal), colsum(dh), colsum(dmid), colsum(dy))
        return tuple(a + b for a, b in zip(sums, new))

    zero = jnp.zeros((1, width), F32)
    sums = lax.fori_loop(0, ROWS // 128, chunk, (zero,) * 4)
    for n in range(4):
        sums_ref[n : n + 1, :] = sums[n]


def out_back_body(dlow_ref, o_ref, wo_ref, do_ref, g_ref):
    do_ref[...] = dot(dlow_ref[...], wo_ref[...]).astype(BF)
    parts, groups, sub, local = g_ref.shape
    g = dot(dlow_ref[...].T, o_ref[...]).astype(BF)
    for j in range(groups):
        g_ref[:, j] = g[:, j * local : (j + 1) * local].reshape(parts, sub, local)


def attend_back_body(slots, q_ref, k_ref, v_ref, p_ref, do_ref, dq_ref, dk_ref, dv_ref):
    low_half = lax.broadcasted_iota(jnp.int32, (SLOT_ROWS, 2 * HEAD_DIM), 1) < HEAD_DIM

    def image(i):
        rows = cut(i, SLOT_ROWS)
        q = q_ref[rows, :] * jnp.bfloat16(0.125)
        k = k_ref[rows, :] * jnp.bfloat16(0.125)
        v = v_ref[rows, :]
        do = do_ref[rows, :]
        zero = jnp.zeros_like(q)
        grads = []
        for h in range(2):
            mask = low_half if h == 0 else ~low_half
            p = p_ref[h, i]
            pf = p.astype(F32)
            dv = dot(p, do, TN)
            dp = dot(jnp.where(mask, do, zero), v, NT)
            ds = (pf * (dp - jnp.sum(pf * dp, axis=-1, keepdims=True))).astype(BF)
            grads.append((dot(ds, k), dot(ds, q, TN), dv))
        for ref, a, b in zip((dq_ref, dk_ref, dv_ref), *grads):
            ref[rows, :] = jnp.where(low_half, a, b).astype(BF)

    loop(slots, image)
    tail = slots * SLOT_ROWS
    for ref in (dq_ref, dk_ref, dv_ref):
        ref[tail:, :] = jnp.zeros((ROWS - tail, 2 * HEAD_DIM), BF)


def qkv_outer_body(h_ref, dq_ref, dk_ref, dv_ref, g_ref, sums_ref, t_ref):
    t_ref[...] = h_ref[...].T
    parts, groups, sub, cols = g_ref.shape
    local = cols // 3
    for s, ref in enumerate((dq_ref, dk_ref, dv_ref)):
        g = dot(t_ref[...], ref[...]).astype(BF)
        for j in range(groups):
            g_ref[:, j, :, s * local : (s + 1) * local] = g[:, j * local : (j + 1) * local].reshape(parts, sub, local)
        if s != 1:
            n = 0 if s == 0 else 1
            sums_ref[n : n + 1, :] = colsum(ref[...].astype(F32))


def input_back_body(slots, length, x_ref, dq_ref, dk_ref, dv_ref, wq_ref, dmid_ref, gain_ref, out_ref, sums_ref, acc_ref):
    width = x_ref.shape[1]
    for s, ref in enumerate((dq_ref, dk_ref, dv_ref)):
        part = dot(ref[...], wq_ref[:, s * width : (s + 1) * width], NT)
        if s == 0:
            acc_ref[...] = part
        else:
            acc_ref[...] += part

    sums = [jnp.zeros((1, width), F32)] * 2
    for i in range(slots):
        rows = slice(i * SLOT_ROWS, (i + 1) * SLOT_ROWS)
        dh = acc_ref[rows, :]
        normal, scale_inv = norm_stats(x_ref[rows, :].astype(F32))
        grad = dmid_ref[rows, :] + norm_back(dh, normal, scale_inv, gain_ref[...])
        out_ref[i] = grad[:length].astype(BF)
        sums[0] = sums[0] + colsum(dh * normal)
        sums[1] = sums[1] + colsum(dh)
    for n in range(2):
        sums_ref[n : n + 1, :] = sums[n]


def on_device(
    inputs,
    cotangent,
    counts,
    norm_gain,
    norm_shift,
    qkv_weight,
    query_bias,
    value_bias,
    out_weight,
    out_bias,
    mlp_gain,
    mlp_shift,
    hidden_weight,
    hidden_bias,
    down_weight,
    down_bias,
):
    batches, slots, length, width = inputs.shape
    sub = qkv_weight.shape[0]
    local = qkv_weight.shape[1] // 3
    units = hidden_weight.shape[1]
    parts, groups = width // sub, width // local
    ff = units * groups
    axes = ("dp", "mp")
    mine = lax.axis_index("mp")

    def padded(tokens):
        tokens = jnp.pad(tokens, ((0, 0), (0, SLOT_ROWS - length), (0, 0)))
        return jnp.pad(tokens.reshape(slots * SLOT_ROWS, width), ((0, ROWS - slots * SLOT_ROWS), (0, 0)))

    pick = lambda a: lax.dynamic_index_in_dim(a, mine, 0, keepdims=False)
    live = pick(counts)
    x = padded(pick(inputs))
    mask = (jnp.arange(slots, dtype=jnp.int32) < live[0]).astype(BF)
    dy = padded(pick(cotangent) * mask[:, None, None])
    row = lambda v: v.reshape(1, -1)

    shard = jnp.concatenate([qkv_weight, out_weight.T, hidden_weight, down_weight.T], axis=1)
    every = lax.all_gather(shard, axes, axis=0, tiled=False).reshape(parts, groups, sub, -1)
    piece = lambda n: lax.slice_in_dim(every, n * 4 * local, (n + 1) * 4 * local, axis=3)
    wa, wb, wc = piece(0), piece(1), piece(2)
    biases = lax.all_gather(jnp.concatenate([query_bias, value_bias, hidden_bias]), "mp", axis=0, tiled=False)
    qb, vb, hb = (biases[:, a:b].reshape(-1) for a, b in ((0, local), (local, 2 * local), (2 * local, None)))
    bias_row = row(jnp.concatenate([qb, jnp.zeros_like(qb), vb]))

    mm = 2 * ROWS * width * width
    t_bf = lambda n: sds((ROWS, n), BF)
    t_f = lambda n: sds((ROWS, n), F32)
    h1, qkv, wq, wo = call(
        qkv_body,
        [t_bf(width), t_bf(3 * width), sds((width, 3 * width), BF), sds((width, width), BF)],
        [x, row(norm_gain), row(norm_shift), wa, bias_row],
        flops=3 * mm,
    )
    pair = 2 * HEAD_DIM
    pairs = width // pair
    head = lambda s: pl.BlockSpec((ROWS, pair), lambda i: (0, s * pairs + i))
    p_spec = pl.BlockSpec((2, slots, SLOT_ROWS, SLOT_ROWS), lambda i: (i, 0, 0, 0))
    p_shape = sds((2 * pairs, slots, SLOT_ROWS, SLOT_ROWS), BF)
    mixed, probs = call(
        functools.partial(attend_body, slots, length),
        [t_bf(width), p_shape],
        [qkv, qkv, qkv],
        [head(0), head(1), head(2)],
        [head(0), p_spec],
        (pairs,),
        flops=mm,
    )
    rows256 = pl.BlockSpec((256, width), lambda i: (i, 0))
    middle, h2 = call(
        mix_body,
        [t_f(width), t_bf(width)],
        [x, mixed, wo, row(out_bias), row(mlp_gain), row(mlp_shift)],
        [rows256, rows256, None, None, None, None],
        [rows256, rows256],
        (ROWS // 256,),
        flops=mm,
    )
    step = 256
    per = units // step
    wcols = pl.BlockSpec((parts, 1, sub, step), lambda i: (0, i // per, 0, i % per))
    tcols = pl.BlockSpec((ROWS, step), lambda i: (0, i))
    vcols = lambda n: pl.BlockSpec((n, step), lambda i: (0, i))
    act, slope = call(
        hidden_body,
        [t_bf(ff), t_bf(ff)],
        [h2, wb, row(hb)],
        [None, wcols, vcols(1)],
        [tcols, tcols],
        (ff // step,),
        flops=4 * mm,
    )
    smem = pl.BlockSpec(memory_space=pltpu.SMEM)
    (block_out,) = call(
        functools.partial(down_body, slots, length),
        [sds((slots, length, width), BF)],
        [live, act, wc, middle, row(down_bias)],
        [smem, None, None, None, None],
        scratch=[pltpu.VMEM((ROWS, width), F32)],
        flops=4 * mm,
    )
    g_shape = lambda n: sds((parts, groups, sub, n), BF)

    def outer(left, right):
        (g,) = call(
            outer_body,
            [g_shape(units)],
            [left, right],
            [None, tcols],
            [wcols],
            (ff // step,),
            scratch=[pltpu.VMEM((width, ROWS), BF)],
            flops=4 * mm,
        )
        return g

    g_down = outer(dy, act)
    du, sum_hidden = call(
        dact_body,
        [t_bf(ff), sds((8, ff), F32)],
        [dy, wc, slope],
        [None, wcols, tcols],
        [tcols, vcols(8)],
        (ff // step,),
        flops=4 * mm,
    )
    g_hidden = outer(h2, du)
    dmid, dlow, sums_mid = call(
        mid_back_body,
        [t_f(width), t_bf(width), sds((8, width), F32)],
        [dy, du, wb, middle, row(mlp_gain)],
        scratch=[pltpu.VMEM((ROWS, width), F32)],
        flops=4 * mm,
    )
    do, g_out = call(
        out_back_body,
        [t_bf(width), g_shape(local)],
        [dlow, mixed, wo],
        flops=2 * mm,
    )
    dq, dk, dv = call(
        functools.partial(attend_back_body, slots),
        [t_bf(width)] * 3,
        [qkv, qkv, qkv, probs, do],
        [head(0), head(1), head(2), p_spec, head(0)],
        [head(0)] * 3,
        (pairs,),
        flops=2 * mm,
    )
    g_qkv, sums_qkv = call(
        qkv_outer_body,
        [g_shape(3 * local), sds((8, width), F32)],
        [h1, dq, dk, dv],
        scratch=[pltpu.VMEM((width, ROWS), BF)],
        flops=3 * mm,
    )
    input_grad, sums_in = call(
        functools.partial(input_back_body, slots, length),
        [sds((slots, length, width), BF), sds((8, width), F32)],
        [x, dq, dk, dv, wq, dmid, row(norm_gain)],
        scratch=[pltpu.VMEM((ROWS, width), F32)],
        flops=3 * mm,
    )

    gather = lambda a: lax.all_gather(a, "mp", axis=0, tiled=False)
    scatter = lambda g: lax.psum_scatter(
        g.reshape(parts * groups, sub, -1), axes, scatter_dimension=0, tiled=False
    ).astype(F32)
    s_down, s_hidden, s_out, s_qkv = scatter(g_down), scatter(g_hidden), scatter(g_out), scatter(g_qkv)
    sums = jnp.concatenate(
        [sums_in[:2].reshape(-1), sums_mid[:4].reshape(-1), sums_qkv[:2].reshape(-1), sum_hidden[0]]
    )
    sums = lax.psum(sums, axes)
    vec = [sums[n * width : (n + 1) * width] for n in range(8)]
    own = lambda v, n: lax.dynamic_slice_in_dim(v, mine * n, n, 0)
    return (
        gather(block_out),
        gather(input_grad),
        vec[0],
        vec[1],
        s_qkv,
        own(vec[6], local),
        own(vec[7], local),
        s_out.T,
        vec[4],
        vec[2],
        vec[3],
        s_hidden,
        own(sums[8 * width :], units),
        s_down.T,
        vec[5],
    )


def solution(mesh):
    token = P(None, "dp", None, None)
    weight, turned = P("dp", "mp"), P("mp", "dp")
    return jax.shard_map(
        on_device,
        mesh=mesh,
        in_specs=(token, token, P(None, "dp"), P(), P(), weight, P("mp"), P("mp"), turned)
        + (P(), P(), P(), weight, P("mp"), turned, P()),
        out_specs=(token, token, P(), P(), weight, P("mp"), P("mp"), turned)
        + (P(), P(), P(), weight, P("mp"), turned, P()),
        check_vma=False,
    )
```

```python
import functools
import jax
import jax.numpy as jnp
from jax import lax
from jax.experimental import pallas as pl
from jax.experimental.pallas import tpu as pltpu
from jax.sharding import PartitionSpec as P

HEAD_DIM = 64
NORM_EPS = 1e-06
SLOT_ROWS = 200
ROWS = 1024
BF = jnp.bfloat16
F32 = jnp.float32
NT = (((1,), (1,)), ((), ()))
NN = (((1,), (0,)), ((), ()))
TN = (((0,), (0,)), ((), ()))


def dot(a, b, dims=NN):
    return lax.dot_general(a, b, dims, preferred_element_type=F32)


def norm_stats(values):
    center = jnp.mean(values, axis=-1, keepdims=True)
    offset = values - center
    spread = jnp.mean(offset * offset, axis=-1, keepdims=True)
    scale_inv = lax.rsqrt(spread + NORM_EPS)
    return offset * scale_inv, scale_inv


def norm_back(upstream, normal, scale_inv, gain_vec):
    scaled = upstream * gain_vec
    return scale_inv * (
        scaled
        - jnp.mean(scaled, axis=-1, keepdims=True)
        - normal * jnp.mean(scaled * normal, axis=-1, keepdims=True)
    )


def colsum(values):
    return jnp.sum(values, axis=0, keepdims=True)


def call(body, outs, ins, in_specs=None, out_specs=None, grid=None, scratch=(), flops=0, nbytes=0, limit=60, name=None, **kw):
    full = lambda a: pl.BlockSpec(a.shape, (lambda *_: (0,) * len(a.shape)))
    if in_specs is None:
        in_specs = [None] * len(ins)
    if out_specs is None:
        out_specs = [None] * len(outs)
    in_specs = [full(a) if s is None else s for a, s in zip(ins, in_specs)]
    out_specs = [full(a) if s is None else s for a, s in zip(outs, out_specs)]
    nbytes = sum(a.size * a.dtype.itemsize for a in ins) + sum(a.size * a.dtype.itemsize for a in outs)
    return pl.pallas_call(
        body,
        out_shape=tuple(outs),
        grid=(1,) if grid is None else grid,
        in_specs=in_specs,
        out_specs=tuple(out_specs),
        scratch_shapes=list(scratch),
        compiler_params=pltpu.CompilerParams(vmem_limit_bytes=limit * 1024 * 1024),
        name=name,
        cost_estimate=pl.CostEstimate(flops=flops, bytes_accessed=nbytes, transcendentals=0),
        **kw,
    )(*ins)


def sds(shape, dtype):
    return jax.ShapeDtypeStruct(shape, dtype)


def loop(n, fn):
    lax.fori_loop(0, n, lambda i, c: (fn(i), c)[1], 0)


def cut(i, size):
    return pl.ds(pl.multiple_of(i * size, size), size)


def prep_body(slots, length, info_ref, x_ref, cot_ref, xo_ref, dy_ref):
    xo_ref[...] = jnp.zeros_like(xo_ref)
    dy_ref[...] = jnp.zeros_like(dy_ref)
    for i in range(slots):
        rows = slice(i * SLOT_ROWS, i * SLOT_ROWS + length)
        xo_ref[rows, :] = x_ref[0, i]

        @pl.when(i < info_ref[1])
        def _():
            dy_ref[rows, :] = cot_ref[0, i]


def place_chunks(info_ref, own_refs, other_refs, buf_ref):
    sub = own_refs[0].shape[1]
    for k, (own, other) in enumerate(zip(own_refs, other_refs)):
        rows = pl.ds(pl.multiple_of(info_ref[2 + k] * sub, sub), sub)
        buf_ref[0, rows, :] = own[0]
        buf_ref[2, rows, :] = own[1]
        buf_ref[1, rows, :] = other[0]
        buf_ref[3, rows, :] = other[1]


def qkv_ring_body(info_ref, x_ref, gain_ref, shift_ref, bias_ref, *refs):
    n = (len(refs) - 5) // 2
    own_refs, other_refs = refs[:n], refs[n : 2 * n]
    h_ref, qkv_ref, wq_ref, wo_ref, buf_ref = refs[2 * n :]
    place_chunks(info_ref, own_refs, other_refs, buf_ref)
    groups = buf_ref.shape[0]
    qkv_rest(lambda j: buf_ref[lax.bitwise_xor(info_ref[0], j)], groups, x_ref, gain_ref, shift_ref, bias_ref, h_ref, qkv_ref, wq_ref, wo_ref)


def qkv_gathered_body(x_ref, gain_ref, shift_ref, bias_ref, wa_ref, h_ref, qkv_ref, wq_ref, wo_ref):
    parts, groups, sub, cols = wa_ref.shape
    qkv_rest(lambda j: wa_ref[:, j].reshape(parts * sub, cols), groups, x_ref, gain_ref, shift_ref, bias_ref, h_ref, qkv_ref, wq_ref, wo_ref)


def qkv_rest(piece, groups, x_ref, gain_ref, shift_ref, bias_ref, h_ref, qkv_ref, wq_ref, wo_ref):
    width = x_ref.shape[1]
    local = width // groups
    for j in range(groups):
        w = piece(j)
        for s in range(3):
            wq_ref[:, s * width + j * local : s * width + (j + 1) * local] = w[:, s * local : (s + 1) * local]
        wo_ref[:, j * local : (j + 1) * local] = w[:, 3 * local :]

    def norm(i):
        rows = cut(i, 128)
        normal, _ = norm_stats(x_ref[rows, :].astype(F32))
        h_ref[rows, :] = (normal * gain_ref[...] + shift_ref[...]).astype(BF)

    loop(ROWS // 128, norm)

    def project(n):
        cols = cut(n, 256)
        qkv_ref[:, cols] = (dot(h_ref[...], wq_ref[:, cols]) + bias_ref[:, cols]).astype(BF)

    loop(3 * width // 256, project)


def attend_body(slots, length, q_ref, k_ref, v_ref, o_ref, p_ref):
    low_half = lax.broadcasted_iota(jnp.int32, (SLOT_ROWS, 2 * HEAD_DIM), 1) < HEAD_DIM
    valid = lax.broadcasted_iota(jnp.int32, (SLOT_ROWS, SLOT_ROWS), 1) < length

    def image(i):
        rows = cut(i, SLOT_ROWS)
        q = q_ref[rows, :] * jnp.bfloat16(0.125)
        k = k_ref[rows, :]
        v = v_ref[rows, :]
        zero = jnp.zeros_like(q)
        mixed = []
        for h in range(2):
            s = dot(jnp.where(low_half if h == 0 else ~low_half, q, zero), k, NT)
            s = jnp.where(valid, s, -1e30)
            e = jnp.exp(s - jnp.max(s, axis=-1, keepdims=True))
            p = (e * (1.0 / jnp.sum(e, axis=-1, keepdims=True))).astype(BF)
            p_ref[h, i] = p
            mixed.append(dot(p, v))
        o_ref[rows, :] = jnp.where(low_half, mixed[0], mixed[1]).astype(BF)

    loop(slots, image)
    tail = slots * SLOT_ROWS
    o_ref[tail:, :] = jnp.zeros((ROWS - tail, 2 * HEAD_DIM), BF)


def mix_body(x_ref, o_ref, wo_ref, bias_ref, gain_ref, shift_ref, mid_ref, h_ref):
    mid_ref[...] = dot(o_ref[...], wo_ref[...], NT)

    def norm(i):
        rows = cut(i, 128)
        mid = x_ref[rows, :].astype(F32) + (mid_ref[rows, :] + bias_ref[...])
        mid_ref[rows, :] = mid
        normal, _ = norm_stats(mid)
        h_ref[rows, :] = (normal * gain_ref[...] + shift_ref[...]).astype(BF)

    loop(mid_ref.shape[0] // 128, norm)


def hidden_body(h_ref, w_ref, bias_ref, act_ref, slope_ref):
    parts, _, sub, cols = w_ref.shape
    w = w_ref[:, 0].reshape(parts * sub, cols)

    def chunk(i):
        rows = cut(i, 256)
        u = dot(h_ref[rows, :], w) + bias_ref[...]
        half = 0.5 * (1.0 + lax.erf(u * 0.7071067811865476))
        act_ref[rows, :] = (u * half).astype(BF)
        slope_ref[rows, :] = (half + u * jnp.exp(-0.5 * u * u) * 0.3989422804014327).astype(BF)

    loop(ROWS // 256, chunk)


def down_body(slots, length, info_ref, act_ref, wc_ref, mid_ref, bias_ref, all_ref, out_ref, acc_ref):
    parts, groups, sub, cols = wc_ref.shape
    for j in range(groups):
        part = dot(act_ref[:, j * cols : (j + 1) * cols], wc_ref[:, j].reshape(parts * sub, cols), NT)
        if j == 0:
            acc_ref[...] = part
        else:
            acc_ref[...] += part
    for i in range(slots):
        rows = slice(i * SLOT_ROWS, (i + 1) * SLOT_ROWS)
        live = jnp.where(i < info_ref[1], 1.0, 0.0)
        value = ((mid_ref[rows, :] + acc_ref[rows, :] + bias_ref[...]) * live)[:length].astype(BF)
        out_ref[i] = value
        all_ref[0, i] = value


def outer_body(h_ref, dy_ref, du_ref, act_ref, g_ref, t_ref):
    step = pl.program_id(0)
    half = pl.num_programs(0) // 2
    parts, _, sub, cols = g_ref.shape

    @pl.when(step == 0)
    def _():
        t_ref[...] = dy_ref[...].T

    @pl.when(step == half)
    def _():
        t_ref[...] = h_ref[...].T

    @pl.when(step < half)
    def _():
        g_ref[:, 0] = dot(t_ref[...], act_ref[...]).astype(BF).reshape(parts, sub, cols)

    @pl.when(step >= half)
    def _():
        g_ref[:, 0] = dot(t_ref[...], du_ref[...]).astype(BF).reshape(parts, sub, cols)


def dact_body(dy_ref, wc_ref, slope_ref, du_ref, sum_ref):
    parts, _, sub, cols = wc_ref.shape
    w = wc_ref[:, 0].reshape(parts * sub, cols)
    total = jnp.zeros((1, cols), F32)
    for i in range(ROWS // 256):
        rows = slice(i * 256, (i + 1) * 256)
        du = (dot(dy_ref[rows, :], w) * slope_ref[rows, :].astype(F32)).astype(BF)
        du_ref[rows, :] = du
        total = total + colsum(du.astype(F32))
    sum_ref[...] = jnp.broadcast_to(total, sum_ref.shape)


def mid_back_body(dy_ref, du_ref, wb_ref, mid_ref, gain_ref, dmid_ref, dlow_ref, sums_ref, acc_ref):
    parts, groups, sub, cols = wb_ref.shape
    for j in range(groups):
        part = dot(du_ref[:, j * cols : (j + 1) * cols], wb_ref[:, j].reshape(parts * sub, cols), NT)
        if j == 0:
            acc_ref[...] = part
        else:
            acc_ref[...] += part
    width = dy_ref.shape[1]

    def chunk(i, sums):
        rows = cut(i, 128)
        dh = acc_ref[rows, :]
        normal, scale_inv = norm_stats(mid_ref[rows, :])
        dy = dy_ref[rows, :].astype(F32)
        dmid = dy + norm_back(dh, normal, scale_inv, gain_ref[...])
        dmid_ref[rows, :] = dmid
        dlow_ref[rows, :] = dmid.astype(BF)
        new = (colsum(dh * normal), colsum(dh), colsum(dmid), colsum(dy))
        return tuple(a + b for a, b in zip(sums, new))

    zero = jnp.zeros((1, width), F32)
    sums = lax.fori_loop(0, ROWS // 128, chunk, (zero,) * 4)
    for n in range(4):
        sums_ref[n : n + 1, :] = sums[n]


def out_back_body(dlow_ref, wo_ref, do_ref):
    do_ref[...] = dot(dlow_ref[...], wo_ref[...]).astype(BF)


def attend_back_body(slots, q_ref, k_ref, v_ref, p_ref, do_ref, dq_ref, dk_ref, dv_ref):
    low_half = lax.broadcasted_iota(jnp.int32, (SLOT_ROWS, 2 * HEAD_DIM), 1) < HEAD_DIM

    def image(i):
        rows = cut(i, SLOT_ROWS)
        q = q_ref[rows, :] * jnp.bfloat16(0.125)
        k = k_ref[rows, :] * jnp.bfloat16(0.125)
        v = v_ref[rows, :]
        do = do_ref[rows, :]
        zero = jnp.zeros_like(q)
        grads = []
        for h in range(2):
            mask = low_half if h == 0 else ~low_half
            p = p_ref[h, i]
            pf = p.astype(F32)
            dv = dot(p, do, TN)
            dp = dot(jnp.where(mask, do, zero), v, NT)
            ds = (pf * (dp - jnp.sum(pf * dp, axis=-1, keepdims=True))).astype(BF)
            grads.append((dot(ds, k), dot(ds, q, TN), dv))
        for ref, a, b in zip((dq_ref, dk_ref, dv_ref), *grads):
            ref[rows, :] = jnp.where(low_half, a, b).astype(BF)

    loop(slots, image)
    tail = slots * SLOT_ROWS
    for ref in (dq_ref, dk_ref, dv_ref):
        ref[tail:, :] = jnp.zeros((ROWS - tail, 2 * HEAD_DIM), BF)


def small_outer(h_ref, dq_ref, dk_ref, dv_ref, dlow_ref, o_ref, sums_ref, store):
    ht = h_ref[...].T
    for s, ref in enumerate((dq_ref, dk_ref, dv_ref)):
        store(s, dot(ht, ref[...]).astype(BF))
        if s != 1:
            n = 0 if s == 0 else 1
            sums_ref[n : n + 1, :] = colsum(ref[...].astype(F32))
    store(3, dot(dlow_ref[...].T, o_ref[...]).astype(BF))


def outer_ring_body(info_ref, h_ref, dq_ref, dk_ref, dv_ref, dlow_ref, o_ref, keep_ref, send_ref, sums_ref, buf_ref):
    groups = buf_ref.shape[0]
    local = h_ref.shape[1] // groups
    slots, _, sub, _ = keep_ref.shape

    def store(s, g):
        for j in range(groups):
            buf_ref[j, :, s * local : (s + 1) * local] = g[:, j * local : (j + 1) * local]

    small_outer(h_ref, dq_ref, dk_ref, dv_ref, dlow_ref, o_ref, sums_ref, store)
    for k in range(slots):
        rows = pl.ds(pl.multiple_of(info_ref[2 + k] * sub, sub), sub)
        for rel in range(4):
            ref = send_ref if rel % 2 else keep_ref
            ref[k, rel // 2] = buf_ref[lax.bitwise_xor(info_ref[0], rel), rows, :]


def outer_plain_body(h_ref, dq_ref, dk_ref, dv_ref, dlow_ref, o_ref, g_ref, sums_ref):
    parts, groups, sub, cols = g_ref.shape
    local = cols // 4

    def store(s, g):
        for j in range(groups):
            g_ref[:, j, :, s * local : (s + 1) * local] = g[:, j * local : (j + 1) * local].reshape(parts, sub, local)

    small_outer(h_ref, dq_ref, dk_ref, dv_ref, dlow_ref, o_ref, sums_ref, store)


def input_back_body(slots, length, info_ref, x_ref, dq_ref, dk_ref, dv_ref, wq_ref, dmid_ref, gain_ref, all_ref, out_ref, sums_ref, acc_ref):
    width = x_ref.shape[1]
    for s, ref in enumerate((dq_ref, dk_ref, dv_ref)):
        part = dot(ref[...], wq_ref[:, s * width : (s + 1) * width], NT)
        if s == 0:
            acc_ref[...] = part
        else:
            acc_ref[...] += part

    sums = [jnp.zeros((1, width), F32)] * 2
    for i in range(slots):
        rows = slice(i * SLOT_ROWS, (i + 1) * SLOT_ROWS)
        dh = acc_ref[rows, :]
        normal, scale_inv = norm_stats(x_ref[rows, :].astype(F32))
        grad = dmid_ref[rows, :] + norm_back(dh, normal, scale_inv, gain_ref[...])
        grad = grad[:length].astype(BF)
        out_ref[i] = grad
        all_ref[0, i] = grad
        sums[0] = sums[0] + colsum(dh * normal)
        sums[1] = sums[1] + colsum(dh)
    for n in range(2):
        sums_ref[n : n + 1, :] = sums[n]


def on_device(
    inputs,
    cotangent,
    counts,
    norm_gain,
    norm_shift,
    qkv_weight,
    query_bias,
    value_bias,
    out_weight,
    out_bias,
    mlp_gain,
    mlp_shift,
    hidden_weight,
    hidden_bias,
    down_weight,
    down_bias,
):
    batches, slots, length, width = inputs.shape
    sub = qkv_weight.shape[0]
    local = qkv_weight.shape[1] // 3
    units = hidden_weight.shape[1]
    parts, groups = width // sub, width // local
    ff = units * groups
    axes = ("dp", "mp")
    mine = lax.axis_index("mp")
    ring = sub % 32 == 0

    cycle = list(range(0, parts, 2)) + list(range(parts - 1, 0, -2))
    place = [cycle.index(d) for d in range(parts)]
    here = jnp.array(place, jnp.int32)[lax.axis_index("dp")]
    owner = jnp.array(cycle, jnp.int32)
    right = [(cycle[p], cycle[(p + 1) % parts]) for p in range(parts)]
    left = [(b, a) for a, b in right]
    far = parts // 2
    mp_swap = lambda a, bit: lax.ppermute(a, "mp", [(j, j ^ bit) for j in range(groups)])
    dp_swap = lambda a, bit: lax.ppermute(a, "dp", [(d, d ^ bit) for d in range(parts)])
    to_right = lambda a: lax.ppermute(a, "dp", right)
    to_left = lambda a: lax.ppermute(a, "dp", left)
    row = lambda v: v.reshape(1, -1)
    live = lax.dynamic_index_in_dim(counts, mine, 0, keepdims=False)[0]

    def info_of(offsets):
        return jnp.concatenate([jnp.stack([mine, live]), owner[(here + jnp.array(offsets, jnp.int32)) % parts]])

    smem = pl.BlockSpec(memory_space=pltpu.SMEM)
    info = jnp.stack([mine, live])

    shard_bc = jnp.concatenate([hidden_weight, down_weight.T], axis=1)
    bc = lax.all_gather(shard_bc, axes, axis=0, tiled=False).reshape(parts, groups, sub, 2 * units)
    shard_a = jnp.concatenate([qkv_weight, out_weight.T], axis=1)
    vectors = jnp.concatenate([query_bias, value_bias, hidden_bias])
    if ring:
        mate = mp_swap(shard_a, 2)
        start = jnp.stack([shard_a, mate])
        chunks = [start]
        offsets = [0]
        rights, lefts = start, start
        for k in range(1, far + 1):
            rights = to_right(rights)
            chunks.append(rights)
            offsets.append(-k)
            if k < far:
                lefts = to_left(lefts)
                chunks.append(lefts)
                offsets.append(k)
        others = [mp_swap(c, 1) for c in chunks]
        ring_info = info_of(offsets)
    else:
        wa = lax.all_gather(shard_a, axes, axis=0, tiled=False).reshape(parts, groups, sub, 4 * local)
    two = jnp.stack([vectors, mp_swap(vectors, 1)])
    four = jnp.concatenate([two, mp_swap(two, 2)])
    biases = four[jnp.arange(groups) ^ mine]
    qb, vb, hb = (biases[:, a:b].reshape(-1) for a, b in ((0, local), (local, 2 * local), (2 * local, None)))
    bias_row = row(jnp.concatenate([qb, jnp.zeros_like(qb), vb]))

    mm = 2 * ROWS * width * width
    t_bf = lambda n: sds((ROWS, n), BF)
    t_f = lambda n: sds((ROWS, n), F32)
    block = lambda shape: pl.BlockSpec(shape, lambda i, info: (0,) * len(shape))
    mine_block = pl.BlockSpec((1, slots, length, width), lambda i, info: (info[0], 0, 0, 0))
    x, dy = pl.pallas_call(
        functools.partial(prep_body, slots, length),
        out_shape=(t_bf(width), t_bf(width)),
        grid_spec=pltpu.PrefetchScalarGridSpec(
            num_scalar_prefetch=1,
            grid=(1,),
            in_specs=[mine_block, mine_block],
            out_specs=[block((ROWS, width)), block((ROWS, width))],
        ),
        compiler_params=pltpu.CompilerParams(vmem_limit_bytes=24 * 1024 * 1024),
        cost_estimate=pl.CostEstimate(flops=0, bytes_accessed=8 * ROWS * width, transcendentals=0),
        name="prep",
    )(info, inputs, cotangent)

    qkv_outs = [t_bf(width), t_bf(3 * width), sds((width, 3 * width), BF), sds((width, width), BF)]
    qkv_ins = [x, row(norm_gain), row(norm_shift), bias_row]
    if ring:
        h1, qkv, wq, wo = call(
            qkv_ring_body,
            qkv_outs,
            [ring_info] + qkv_ins + chunks + others,
            [smem] + [None] * (len(qkv_ins) + 2 * len(chunks)),
            scratch=[pltpu.VMEM((groups, width, 4 * local), BF)],
            flops=3 * mm,
            name="qkv",
        )
    else:
        h1, qkv, wq, wo = call(qkv_gathered_body, qkv_outs, qkv_ins + [wa], flops=3 * mm, name="qkv")
    pair = 2 * HEAD_DIM
    pairs = width // pair
    head = lambda s: pl.BlockSpec((ROWS, pair), lambda i: (0, s * pairs + i))
    p_spec = pl.BlockSpec((2, slots, SLOT_ROWS, SLOT_ROWS), lambda i: (i, 0, 0, 0))
    p_shape = sds((2 * pairs, slots, SLOT_ROWS, SLOT_ROWS), BF)
    mixed, probs = call(
        functools.partial(attend_body, slots, length),
        [t_bf(width), p_shape],
        [qkv, qkv, qkv],
        [head(0), head(1), head(2)],
        [head(0), p_spec],
        (pairs,),
        flops=mm,
        name="attend",
    )
    rows256 = pl.BlockSpec((256, width), lambda i: (i, 0))
    middle, h2 = call(
        mix_body,
        [t_f(width), t_bf(width)],
        [x, mixed, wo, row(out_bias), row(mlp_gain), row(mlp_shift)],
        [rows256, rows256, None, None, None, None],
        [rows256, rows256],
        (ROWS // 256,),
        flops=mm,
        name="mix",
    )
    step = 256
    per = units // step
    steps = ff // step
    wcols = lambda n: pl.BlockSpec((parts, 1, sub, step), lambda i: (0, i // per, 0, n * per + i % per))
    piece = lambda n: pl.BlockSpec((parts, groups, sub, units), lambda i: (0, 0, 0, n))
    tcols = pl.BlockSpec((ROWS, step), lambda i: (0, i))
    vcols = lambda n: pl.BlockSpec((n, step), lambda i: (0, i))
    act, slope = call(
        hidden_body,
        [t_bf(ff), t_bf(ff)],
        [h2, bc, row(hb)],
        [None, wcols(0), vcols(1)],
        [tcols, tcols],
        (steps,),
        flops=4 * mm,
        name="hidden",
    )
    du, sum_hidden = call(
        dact_body,
        [t_bf(ff), sds((8, ff), F32)],
        [dy, bc, slope],
        [None, wcols(1), tcols],
        [tcols, vcols(8)],
        (steps,),
        flops=4 * mm,
        name="dact",
    )
    (g_bc,) = call(
        outer_body,
        [sds((parts, groups, sub, 2 * units), BF)],
        [h2, dy, du, act],
        [
            None,
            None,
            pl.BlockSpec((ROWS, step), lambda i: (0, jnp.maximum(i - steps, 0))),
            pl.BlockSpec((ROWS, step), lambda i: (0, jnp.minimum(i, steps - 1))),
        ],
        [
            pl.BlockSpec(
                (parts, 1, sub, step),
                lambda i: (0, (i % steps) // per, 0, jnp.where(i < steps, per, 0) + i % per),
            )
        ],
        (2 * steps,),
        scratch=[pltpu.VMEM((width, ROWS), BF)],
        flops=8 * mm,
        name="outer_bc",
    )
    s_bc = lax.psum_scatter(
        g_bc.reshape(parts * groups, sub, 2 * units), axes, scatter_dimension=0, tiled=False
    ).astype(F32)

    out_shape = sds((batches, slots, length, width), BF)
    own_shape = sds((slots, length, width), BF)

    def with_slot(body, outs, ins, flops, name):
        fixed = lambda a: pl.BlockSpec(a.shape, lambda i, info: (0,) * len(a.shape))
        return pl.pallas_call(
            body,
            out_shape=tuple(outs),
            grid_spec=pltpu.PrefetchScalarGridSpec(
                num_scalar_prefetch=1,
                grid=(1,),
                in_specs=[fixed(a) if s is None else s for a, s in ins],
                out_specs=[mine_block] + [fixed(a) for a in outs[1:]],
                scratch_shapes=[pltpu.VMEM((ROWS, width), F32)],
            ),
            compiler_params=pltpu.CompilerParams(vmem_limit_bytes=60 * 1024 * 1024),
            cost_estimate=pl.CostEstimate(
                flops=flops, bytes_accessed=sum(a.size * a.dtype.itemsize for a, _ in ins), transcendentals=0
            ),
            name=name,
        )(info, *[a for a, _ in ins])

    def spread(all_out, own):
        crossed = mp_swap(own, 2)
        for rel, value in ((1, mp_swap(own, 1)), (2, crossed), (3, mp_swap(crossed, 1))):
            all_out = lax.dynamic_update_index_in_dim(all_out, value, mine ^ rel, 0)
        return all_out

    piece_c = pl.BlockSpec((parts, groups, sub, units), lambda i, info: (0, 0, 0, 1))
    all_out, own_out = with_slot(
        functools.partial(down_body, slots, length),
        [out_shape, own_shape],
        [(act, None), (bc, piece_c), (middle, None), (row(down_bias), None)],
        4 * mm,
        "down",
    )
    all_out = spread(all_out, own_out)

    dmid, dlow, sums_mid = call(
        mid_back_body,
        [t_f(width), t_bf(width), sds((8, width), F32)],
        [dy, du, bc, middle, row(mlp_gain)],
        [None, None, piece(0), None, None],
        scratch=[pltpu.VMEM((ROWS, width), F32)],
        flops=4 * mm,
        name="mid_back",
    )
    (do,) = call(out_back_body, [t_bf(width)], [dlow, wo], flops=mm, name="out_back")
    dq, dk, dv = call(
        functools.partial(attend_back_body, slots),
        [t_bf(width)] * 3,
        [qkv, qkv, qkv, probs, do],
        [head(0), head(1), head(2), p_spec, head(0)],
        [head(0)] * 3,
        (pairs,),
        flops=2 * mm,
        name="attend_back",
    )
    outer_ins = [h1, dq, dk, dv, dlow, mixed]
    sum_shape = sds((8, width), F32)
    if ring:
        send_order = []
        for k in range(far, 0, -1):
            send_order.append(k)
            if k > 1:
                send_order.append(1 - k)
        send_order.append(0)
        half_shape = sds((parts, 2, sub, 4 * local), BF)
        keep, send, sums_qkv = call(
            outer_ring_body,
            [half_shape, half_shape, sum_shape],
            [info_of(send_order)] + outer_ins,
            [smem] + [None] * len(outer_ins),
            scratch=[pltpu.VMEM((groups, width, 4 * local), BF)],
            flops=4 * mm,
            name="outer_a",
        )
        cuts = [0, 2, 4, parts]
        got = [mp_swap(send[a:b], 1) for a, b in zip(cuts, cuts[1:])]
        got = [(a, g) for a, g in zip(cuts, got)]

        def term(offset):
            n = send_order.index(offset)
            a, g = [(a, g) for a, g in got if a <= n][-1]
            return keep[n].astype(F32) + g[n - a].astype(F32)

        rights = to_right(term(far).astype(BF))
        lefts = to_left(term(1 - far).astype(BF))
        for k in range(far - 1, 0, -1):
            rights = to_right((term(k) + rights.astype(F32)).astype(BF))
            if k > 1:
                lefts = to_left((term(1 - k) + lefts.astype(F32)).astype(BF))
        total = term(0) + rights.astype(F32) + lefts.astype(F32)
        s_a = total[0] + mp_swap(total[1].astype(BF), 2).astype(F32)
    else:
        g_a, sums_qkv = call(
            outer_plain_body,
            [sds((parts, groups, sub, 4 * local), BF), sum_shape],
            outer_ins,
            flops=4 * mm,
            name="outer_a",
        )
        s_a = lax.psum_scatter(
            g_a.reshape(parts * groups, sub, 4 * local), axes, scatter_dimension=0, tiled=False
        ).astype(F32)
    all_grad, own_grad, sums_in = with_slot(
        functools.partial(input_back_body, slots, length),
        [out_shape, own_shape, sum_shape],
        [(x, None), (dq, None), (dk, None), (dv, None), (wq, None), (dmid, None), (row(norm_gain), None)],
        3 * mm,
        "input_back",
    )
    all_grad = spread(all_grad, own_grad)

    sums = jnp.concatenate(
        [sums_in[:2].reshape(-1), sums_mid[:4].reshape(-1), sums_qkv[:2].reshape(-1), sum_hidden[0]]
    )
    for bit in (1, 2):
        sums = sums + mp_swap(sums, bit)
    bit = 1
    while bit < parts:
        sums = sums + dp_swap(sums, bit)
        bit *= 2
    vec = [sums[n * width : (n + 1) * width] for n in range(8)]
    own = lambda v, n: lax.dynamic_slice_in_dim(v, mine * n, n, 0)
    return (
        all_out,
        all_grad,
        vec[0],
        vec[1],
        s_a[:, : 3 * local],
        own(vec[6], local),
        own(vec[7], local),
        s_a[:, 3 * local :].T,
        vec[4],
        vec[2],
        vec[3],
        s_bc[:, :units],
        own(sums[8 * width :], units),
        s_bc[:, units:].T,
        vec[5],
    )


def solution(mesh):
    token = P(None, "dp", None, None)
    weight, turned = P("dp", "mp"), P("mp", "dp")
    return jax.shard_map(
        on_device,
        mesh=mesh,
        in_specs=(token, token, P(None, "dp"), P(), P(), weight, P("mp"), P("mp"), turned)
        + (P(), P(), P(), weight, P("mp"), turned, P()),
        out_specs=(token, token, P(), P(), weight, P("mp"), P("mp"), turned)
        + (P(), P(), P(), weight, P("mp"), turned, P()),
        check_vma=False,
    )
```

```python
import functools
import jax
import jax.numpy as jnp
from jax import lax
from jax.experimental import pallas as pl
from jax.experimental.pallas import tpu as pltpu
from jax.sharding import PartitionSpec as P

HEAD_DIM = 64
NORM_EPS = 1e-06
SLOT_ROWS = 200
ROWS = 1024
UNROLL = 5
BF = jnp.bfloat16
F32 = jnp.float32
NT = (((1,), (1,)), ((), ()))
NN = (((1,), (0,)), ((), ()))
TN = (((0,), (0,)), ((), ()))


def dot(a, b, dims=NN):
    return lax.dot_general(a, b, dims, preferred_element_type=F32)


def norm_stats(values):
    center = jnp.mean(values, axis=-1, keepdims=True)
    offset = values - center
    spread = jnp.mean(offset * offset, axis=-1, keepdims=True)
    scale_inv = lax.rsqrt(spread + NORM_EPS)
    return offset * scale_inv, scale_inv


def norm_back(upstream, normal, scale_inv, gain_vec):
    scaled = upstream * gain_vec
    return scale_inv * (
        scaled
        - jnp.mean(scaled, axis=-1, keepdims=True)
        - normal * jnp.mean(scaled * normal, axis=-1, keepdims=True)
    )


def colsum(values):
    return jnp.sum(values, axis=0, keepdims=True)


def call(body, outs, ins, in_specs=None, out_specs=None, grid=None, scratch=(), flops=0, nbytes=0, limit=60, name=None, **kw):
    full = lambda a: pl.BlockSpec(a.shape, (lambda *_: (0,) * len(a.shape)))
    if in_specs is None:
        in_specs = [None] * len(ins)
    if out_specs is None:
        out_specs = [None] * len(outs)
    in_specs = [full(a) if s is None else s for a, s in zip(ins, in_specs)]
    out_specs = [full(a) if s is None else s for a, s in zip(outs, out_specs)]
    nbytes = sum(a.size * a.dtype.itemsize for a in ins) + sum(a.size * a.dtype.itemsize for a in outs)
    return pl.pallas_call(
        body,
        out_shape=tuple(outs),
        grid=(1,) if grid is None else grid,
        in_specs=in_specs,
        out_specs=tuple(out_specs),
        scratch_shapes=list(scratch),
        compiler_params=pltpu.CompilerParams(vmem_limit_bytes=limit * 1024 * 1024),
        name=name,
        cost_estimate=pl.CostEstimate(flops=flops, bytes_accessed=nbytes, transcendentals=0),
        **kw,
    )(*ins)


def sds(shape, dtype):
    return jax.ShapeDtypeStruct(shape, dtype)


def loop(n, fn, unroll=1):
    lax.fori_loop(0, n, lambda i, c: (fn(i), c)[1], 0, unroll=unroll)


def cut(i, size):
    return pl.ds(pl.multiple_of(i * size, size), size)


def prep_body(slots, length, info_ref, x_ref, cot_ref, xo_ref, dy_ref):
    xo_ref[...] = jnp.zeros_like(xo_ref)
    dy_ref[...] = jnp.zeros_like(dy_ref)
    for i in range(slots):
        rows = slice(i * SLOT_ROWS, i * SLOT_ROWS + length)
        xo_ref[rows, :] = x_ref[0, i]

        @pl.when(i < info_ref[1])
        def _():
            dy_ref[rows, :] = cot_ref[0, i]


def place_chunks(info_ref, refs, buf_ref):
    sub = refs[0].shape[1]

    def put(n, ref):
        rows = pl.ds(pl.multiple_of(info_ref[2 + n] * sub, sub), sub)
        for j in range(ref.shape[0]):
            buf_ref[j, rows, :] = ref[j]

    for n, ref in enumerate(refs[:-2]):
        put(n, ref)
    even = info_ref[0] % 2 == 0
    pl.when(even)(lambda: put(len(refs) - 2, refs[-2]))
    pl.when(~even)(lambda: put(len(refs) - 2, refs[-1]))


def qkv_ring_body(info_ref, x_ref, gain_ref, shift_ref, bias_ref, *refs):
    h_ref, qkv_ref, wq_ref, wo_ref, buf_ref = refs[-5:]
    place_chunks(info_ref, refs[:-5], buf_ref)
    qkv_rest(lambda j: buf_ref[j], buf_ref.shape[0], x_ref, gain_ref, shift_ref, bias_ref, h_ref, qkv_ref, wq_ref, wo_ref)


def qkv_gathered_body(x_ref, gain_ref, shift_ref, bias_ref, wa_ref, h_ref, qkv_ref, wq_ref, wo_ref):
    parts, groups, sub, cols = wa_ref.shape
    qkv_rest(lambda j: wa_ref[:, j].reshape(parts * sub, cols), groups, x_ref, gain_ref, shift_ref, bias_ref, h_ref, qkv_ref, wq_ref, wo_ref)


def qkv_rest(piece, groups, x_ref, gain_ref, shift_ref, bias_ref, h_ref, qkv_ref, wq_ref, wo_ref):
    width = x_ref.shape[1]
    local = width // groups
    for j in range(groups):
        w = piece(j)
        for s in range(3):
            wq_ref[:, s * width + j * local : s * width + (j + 1) * local] = w[:, s * local : (s + 1) * local]
        wo_ref[:, j * local : (j + 1) * local] = w[:, 3 * local :]

    def norm(i):
        rows = cut(i, 128)
        normal, _ = norm_stats(x_ref[rows, :].astype(F32))
        h_ref[rows, :] = (normal * gain_ref[...] + shift_ref[...]).astype(BF)

    loop(ROWS // 128, norm)

    def project(n):
        cols = cut(n, 256)
        qkv_ref[:, cols] = (dot(h_ref[...], wq_ref[:, cols]) + bias_ref[:, cols]).astype(BF)

    loop(3 * width // 256, project)


def attend_body(slots, length, q_ref, k_ref, v_ref, o_ref, p_ref):
    low_half = lax.broadcasted_iota(jnp.int32, (SLOT_ROWS, 2 * HEAD_DIM), 1) < HEAD_DIM
    valid = lax.broadcasted_iota(jnp.int32, (SLOT_ROWS, SLOT_ROWS), 0) < length

    def image(i):
        rows = cut(i, SLOT_ROWS)
        q = q_ref[rows, :] * jnp.bfloat16(0.125)
        k = k_ref[rows, :]
        v_t = v_ref[rows, :].T
        zero = jnp.zeros_like(k)
        mixed = []
        for h in range(2):
            s = dot(jnp.where(low_half if h == 0 else ~low_half, k, zero), q, NT)
            s = jnp.where(valid, s, -1e30)
            e = jnp.exp(s - jnp.max(s, axis=0, keepdims=True))
            p = (e * (1.0 / jnp.sum(e, axis=0, keepdims=True))).astype(BF)
            p_ref[h, i] = p
            mixed.append(dot(v_t[h * HEAD_DIM : (h + 1) * HEAD_DIM], p))
        o_ref[rows, :] = jnp.concatenate(mixed, axis=0).T.astype(BF)

    loop(slots, image, UNROLL)
    tail = slots * SLOT_ROWS
    o_ref[tail:, :] = jnp.zeros((ROWS - tail, 2 * HEAD_DIM), BF)


def mix_body(x_ref, o_ref, wo_ref, bias_ref, gain_ref, shift_ref, mid_ref, h_ref):
    mid_ref[...] = dot(o_ref[...], wo_ref[...], NT)

    def norm(i):
        rows = cut(i, 128)
        mid = x_ref[rows, :].astype(F32) + (mid_ref[rows, :] + bias_ref[...])
        mid_ref[rows, :] = mid
        normal, _ = norm_stats(mid)
        h_ref[rows, :] = (normal * gain_ref[...] + shift_ref[...]).astype(BF)

    loop(mid_ref.shape[0] // 128, norm)


def hidden_body(h_ref, w_ref, bias_ref, act_ref, slope_ref):
    parts, _, sub, cols = w_ref.shape
    w = w_ref[:, 0].reshape(parts * sub, cols)

    def chunk(i):
        rows = cut(i, 256)
        u = dot(h_ref[rows, :], w) + bias_ref[...]
        half = 0.5 * (1.0 + lax.erf(u * 0.7071067811865476))
        act_ref[rows, :] = (u * half).astype(BF)
        slope_ref[rows, :] = (half + u * jnp.exp(-0.5 * u * u) * 0.3989422804014327).astype(BF)

    loop(ROWS // 256, chunk)


def down_body(slots, info_ref, act_ref, wc_ref, mid_ref, bias_ref, out_ref, acc_ref):
    parts, groups, sub, cols = wc_ref.shape
    for j in range(groups):
        part = dot(act_ref[:, j * cols : (j + 1) * cols], wc_ref[:, j].reshape(parts * sub, cols), NT)
        if j == 0:
            acc_ref[...] = part
        else:
            acc_ref[...] += part
    for i in range(slots):
        rows = slice(i * SLOT_ROWS, (i + 1) * SLOT_ROWS)
        live = jnp.where(i < info_ref[1], 1.0, 0.0)
        out_ref[rows, :] = ((mid_ref[rows, :] + acc_ref[rows, :] + bias_ref[...]) * live).astype(BF)


def weave_body(length, info_ref, a_ref, b_ref, c_ref, d_ref, o_ref):
    def part(start, n, keep):
        x = jnp.concatenate([r[start : start + n, :] for r in (a_ref, b_ref, c_ref, d_ref)], axis=0)
        row = lax.broadcasted_iota(jnp.int32, (4 * n, 4 * n), 0)
        col = lax.broadcasted_iota(jnp.int32, (4 * n, 4 * n), 1)
        take = jnp.where(lax.bitwise_xor(row % 4, info_ref[0]) * n + row // 4 == col, 1.0, 0.0).astype(BF)
        y = dot(take, x).astype(BF).reshape(n, 4, x.shape[1])
        o_ref[0, start : start + keep] = y[:keep]

    full = length // 64 * 64
    for start in range(0, full, 64):
        part(start, 64, 64)
    part(full, 8, length - full)


def outer_body(h_ref, dy_ref, du_ref, act_ref, g_ref, t_ref):
    step = pl.program_id(0)
    half = pl.num_programs(0) // 2
    parts, _, sub, cols = g_ref.shape

    @pl.when(step == 0)
    def _():
        t_ref[...] = dy_ref[...].T

    @pl.when(step == half)
    def _():
        t_ref[...] = h_ref[...].T

    @pl.when(step < half)
    def _():
        g_ref[:, 0] = dot(t_ref[...], act_ref[...]).astype(BF).reshape(parts, sub, cols)

    @pl.when(step >= half)
    def _():
        g_ref[:, 0] = dot(t_ref[...], du_ref[...]).astype(BF).reshape(parts, sub, cols)


def dact_body(dy_ref, wc_ref, slope_ref, du_ref, sum_ref):
    parts, _, sub, cols = wc_ref.shape
    w = wc_ref[:, 0].reshape(parts * sub, cols)
    total = jnp.zeros((1, cols), F32)
    for i in range(ROWS // 256):
        rows = slice(i * 256, (i + 1) * 256)
        du = (dot(dy_ref[rows, :], w) * slope_ref[rows, :].astype(F32)).astype(BF)
        du_ref[rows, :] = du
        total = total + colsum(du.astype(F32))
    sum_ref[...] = jnp.broadcast_to(total, sum_ref.shape)


def mid_back_body(dy_ref, du_ref, wb_ref, mid_ref, gain_ref, dmid_ref, dlow_ref, sums_ref, acc_ref):
    parts, groups, sub, cols = wb_ref.shape
    for j in range(groups):
        part = dot(du_ref[:, j * cols : (j + 1) * cols], wb_ref[:, j].reshape(parts * sub, cols), NT)
        if j == 0:
            acc_ref[...] = part
        else:
            acc_ref[...] += part
    width = dy_ref.shape[1]

    def chunk(i, sums):
        rows = cut(i, 128)
        dh = acc_ref[rows, :]
        normal, scale_inv = norm_stats(mid_ref[rows, :])
        dy = dy_ref[rows, :].astype(F32)
        dmid = dy + norm_back(dh, normal, scale_inv, gain_ref[...])
        dmid_ref[rows, :] = dmid
        dlow_ref[rows, :] = dmid.astype(BF)
        new = (colsum(dh * normal), colsum(dh), colsum(dmid), colsum(dy))
        return tuple(a + b for a, b in zip(sums, new))

    zero = jnp.zeros((1, width), F32)
    sums = lax.fori_loop(0, ROWS // 128, chunk, (zero,) * 4)
    for n in range(4):
        sums_ref[n : n + 1, :] = sums[n]


def out_back_body(dlow_ref, wo_ref, do_ref):
    do_ref[...] = dot(dlow_ref[...], wo_ref[...]).astype(BF)


def attend_back_body(slots, q_ref, k_ref, v_ref, p_ref, do_ref, dq_ref, dk_ref, dv_ref):
    low_half = lax.broadcasted_iota(jnp.int32, (SLOT_ROWS, 2 * HEAD_DIM), 1) < HEAD_DIM

    def image(i):
        rows = cut(i, SLOT_ROWS)
        q = q_ref[rows, :] * jnp.bfloat16(0.125)
        k_t = (k_ref[rows, :] * jnp.bfloat16(0.125)).T
        v = v_ref[rows, :]
        do = do_ref[rows, :]
        zero = jnp.zeros_like(v)
        grads = []
        for h in range(2):
            p = p_ref[h, i]
            pf = p.astype(F32)
            dp = dot(jnp.where(low_half if h == 0 else ~low_half, v, zero), do, NT)
            ds = (pf * (dp - jnp.sum(pf * dp, axis=0, keepdims=True))).astype(BF)
            grads.append((dot(k_t[h * HEAD_DIM : (h + 1) * HEAD_DIM], ds), dot(ds, q), dot(p, do)))
        (dq0, dk0, dv0), (dq1, dk1, dv1) = grads
        dq_ref[rows, :] = jnp.concatenate([dq0, dq1], axis=0).T.astype(BF)
        dk_ref[rows, :] = jnp.where(low_half, dk0, dk1).astype(BF)
        dv_ref[rows, :] = jnp.where(low_half, dv0, dv1).astype(BF)

    loop(slots, image, UNROLL)
    tail = slots * SLOT_ROWS
    for ref in (dq_ref, dk_ref, dv_ref):
        ref[tail:, :] = jnp.zeros((ROWS - tail, 2 * HEAD_DIM), BF)


def small_outer(h_ref, dq_ref, dk_ref, dv_ref, dlow_ref, o_ref, sums_ref, store):
    ht = h_ref[...].T
    for s, ref in enumerate((dq_ref, dk_ref, dv_ref)):
        store(s, dot(ht, ref[...]).astype(BF))
        if s != 1:
            n = 0 if s == 0 else 1
            sums_ref[n : n + 1, :] = colsum(ref[...].astype(F32))
    store(3, dot(dlow_ref[...].T, o_ref[...]).astype(BF))


def outer_ring_body(info_ref, h_ref, dq_ref, dk_ref, dv_ref, dlow_ref, o_ref, keep_ref, send_ref, sums_ref, buf_ref):
    groups = buf_ref.shape[0]
    local = h_ref.shape[1] // groups
    slots, _, sub, _ = keep_ref.shape

    def store(s, g):
        for j in range(groups):
            buf_ref[j, :, s * local : (s + 1) * local] = g[:, j * local : (j + 1) * local]

    small_outer(h_ref, dq_ref, dk_ref, dv_ref, dlow_ref, o_ref, sums_ref, store)
    for n in range(2 * slots):
        rows = pl.ds(pl.multiple_of(info_ref[2 + n] * sub, sub), sub)
        ref = keep_ref if n < slots else send_ref
        for j in range(groups):
            ref[n % slots, j] = buf_ref[j, rows, :]


def outer_plain_body(h_ref, dq_ref, dk_ref, dv_ref, dlow_ref, o_ref, g_ref, sums_ref):
    parts, groups, sub, cols = g_ref.shape
    local = cols // 4

    def store(s, g):
        for j in range(groups):
            g_ref[:, j, :, s * local : (s + 1) * local] = g[:, j * local : (j + 1) * local].reshape(parts, sub, local)

    small_outer(h_ref, dq_ref, dk_ref, dv_ref, dlow_ref, o_ref, sums_ref, store)


def input_back_body(slots, x_ref, dq_ref, dk_ref, dv_ref, wq_ref, dmid_ref, gain_ref, out_ref, sums_ref, acc_ref):
    width = x_ref.shape[1]
    for s, ref in enumerate((dq_ref, dk_ref, dv_ref)):
        part = dot(ref[...], wq_ref[:, s * width : (s + 1) * width], NT)
        if s == 0:
            acc_ref[...] = part
        else:
            acc_ref[...] += part

    sums = [jnp.zeros((1, width), F32)] * 2
    for i in range(slots):
        rows = slice(i * SLOT_ROWS, (i + 1) * SLOT_ROWS)
        dh = acc_ref[rows, :]
        normal, scale_inv = norm_stats(x_ref[rows, :].astype(F32))
        grad = dmid_ref[rows, :] + norm_back(dh, normal, scale_inv, gain_ref[...])
        out_ref[rows, :] = grad.astype(BF)
        sums[0] = sums[0] + colsum(dh * normal)
        sums[1] = sums[1] + colsum(dh)
    for n in range(2):
        sums_ref[n : n + 1, :] = sums[n]


def on_device(
    inputs,
    cotangent,
    counts,
    norm_gain,
    norm_shift,
    qkv_weight,
    query_bias,
    value_bias,
    out_weight,
    out_bias,
    mlp_gain,
    mlp_shift,
    hidden_weight,
    hidden_bias,
    down_weight,
    down_bias,
):
    batches, slots, length, width = inputs.shape
    sub = qkv_weight.shape[0]
    local = qkv_weight.shape[1] // 3
    units = hidden_weight.shape[1]
    parts, groups = width // sub, width // local
    ff = units * groups
    axes = ("dp", "mp")
    mine = lax.axis_index("mp")
    ring = sub % 32 == 0

    cycle = list(range(0, parts, 2)) + list(range(parts - 1, 0, -2))
    place = [cycle.index(d) for d in range(parts)]
    here = jnp.array(place, jnp.int32)[lax.axis_index("dp")]
    owner = jnp.array(cycle, jnp.int32)
    far = parts // 2
    mp_swap = lambda a, bit: lax.ppermute(a, "mp", [(j, j ^ bit) for j in range(groups)])
    dp_swap = lambda a, bit: lax.ppermute(a, "dp", [(d, d ^ bit) for d in range(parts)])

    def hop(a, odd=True):
        pairs = []
        for p in range(parts):
            for j in range(groups):
                if j % 2 == 0:
                    pairs.append((cycle[p] * groups + j, cycle[(p + 1) % parts] * groups + j))
                elif odd:
                    pairs.append((cycle[p] * groups + j, cycle[(p - 1) % parts] * groups + j))
        return lax.ppermute(a, axes, pairs)

    even = mine % 2 == 0
    side = jnp.where(even, 1, -1)
    row = lambda v: v.reshape(1, -1)
    live = lax.dynamic_index_in_dim(counts, mine, 0, keepdims=False)[0]

    def info_of(offsets):
        return jnp.concatenate([jnp.stack([mine, live]), owner[(here + jnp.stack(offsets)) % parts]])

    smem = pl.BlockSpec(memory_space=pltpu.SMEM)
    info = jnp.stack([mine, live])

    mm = 2 * ROWS * width * width
    t_bf = lambda n: sds((ROWS, n), BF)
    t_f = lambda n: sds((ROWS, n), F32)
    block = lambda shape: pl.BlockSpec(shape, lambda i, info: (0,) * len(shape))
    mine_block = pl.BlockSpec((1, slots, length, width), lambda i, info: (info[0], 0, 0, 0))
    x, dy = pl.pallas_call(
        functools.partial(prep_body, slots, length),
        out_shape=(t_bf(width), t_bf(width)),
        grid_spec=pltpu.PrefetchScalarGridSpec(
            num_scalar_prefetch=1,
            grid=(1,),
            in_specs=[mine_block, mine_block],
            out_specs=[block((ROWS, width)), block((ROWS, width))],
        ),
        compiler_params=pltpu.CompilerParams(vmem_limit_bytes=24 * 1024 * 1024),
        cost_estimate=pl.CostEstimate(flops=0, bytes_accessed=8 * ROWS * width, transcendentals=0),
        name="prep",
    )(info, inputs, cotangent)

    shard_bc = jnp.concatenate([hidden_weight, down_weight.T], axis=1)
    bc = lax.all_gather(shard_bc, axes, axis=0, tiled=False).reshape(parts, groups, sub, 2 * units)
    shard_a = jnp.concatenate([qkv_weight, out_weight.T], axis=1)
    vectors = jnp.concatenate([query_bias, value_bias, hidden_bias])
    if ring:
        two = jnp.stack([shard_a, mp_swap(shard_a, 2)])
        near = mp_swap(two, 1)
        rel = [two[0], near[0], two[1], near[1]]
        rel = [jnp.where(even, rel[j], rel[j ^ 1]) for j in range(groups)]
        start = jnp.stack([jnp.where(mine < 2, rel[j], rel[j ^ 2]) for j in range(groups)])
        chunks, offsets = [start], [jnp.int32(0)]
        held = start
        for k in range(1, far):
            held = hop(held)
            if k == 1:
                held, x, dy = lax.optimization_barrier((held, x, dy))
            chunks += [held, mp_swap(held, 1)]
            offsets += [-k * side, k * side]
        held = hop(held, False)
        chunks += [held, mp_swap(held, 1)]
        offsets += [jnp.int32(far)]
        ring_info = info_of(offsets)
    else:
        wa = lax.all_gather(shard_a, axes, axis=0, tiled=False).reshape(parts, groups, sub, 4 * local)
    two = jnp.stack([vectors, mp_swap(vectors, 1)])
    four = jnp.concatenate([two, mp_swap(two, 2)])
    biases = four[jnp.arange(groups) ^ mine]
    qb, vb, hb = (biases[:, a:b].reshape(-1) for a, b in ((0, local), (local, 2 * local), (2 * local, None)))
    bias_row = row(jnp.concatenate([qb, jnp.zeros_like(qb), vb]))

    qkv_outs = [t_bf(width), t_bf(3 * width), sds((width, 3 * width), BF), sds((width, width), BF)]
    qkv_ins = [x, row(norm_gain), row(norm_shift), bias_row]
    if ring:
        h1, qkv, wq, wo = call(
            qkv_ring_body,
            qkv_outs,
            [ring_info] + qkv_ins + chunks,
            [smem] + [None] * (len(qkv_ins) + len(chunks)),
            scratch=[pltpu.VMEM((groups, width, 4 * local), BF)],
            flops=3 * mm,
            name="qkv",
        )
    else:
        h1, qkv, wq, wo = call(qkv_gathered_body, qkv_outs, qkv_ins + [wa], flops=3 * mm, name="qkv")
    pair = 2 * HEAD_DIM
    pairs = width // pair
    head = lambda s: pl.BlockSpec((ROWS, pair), lambda i: (0, s * pairs + i))
    p_spec = pl.BlockSpec((2, slots, SLOT_ROWS, SLOT_ROWS), lambda i: (i, 0, 0, 0))
    p_shape = sds((2 * pairs, slots, SLOT_ROWS, SLOT_ROWS), BF)
    mixed, probs = call(
        functools.partial(attend_body, slots, length),
        [t_bf(width), p_shape],
        [qkv, qkv, qkv],
        [head(0), head(1), head(2)],
        [head(0), p_spec],
        (pairs,),
        flops=mm,
        name="attend",
    )
    rows256 = pl.BlockSpec((256, width), lambda i: (i, 0))
    middle, h2 = call(
        mix_body,
        [t_f(width), t_bf(width)],
        [x, mixed, wo, row(out_bias), row(mlp_gain), row(mlp_shift)],
        [rows256, rows256, None, None, None, None],
        [rows256, rows256],
        (ROWS // 256,),
        flops=mm,
        name="mix",
    )
    wcols = lambda n: pl.BlockSpec((parts, 1, sub, units), lambda i: (0, i, 0, n))
    piece = lambda n: pl.BlockSpec((parts, groups, sub, units), lambda i: (0, 0, 0, n))
    tcols = pl.BlockSpec((ROWS, units), lambda i: (0, i))
    vcols = lambda n: pl.BlockSpec((n, units), lambda i: (0, i))
    act, slope = call(
        hidden_body,
        [t_bf(ff), t_bf(ff)],
        [h2, bc, row(hb)],
        [None, wcols(0), vcols(1)],
        [tcols, tcols],
        (groups,),
        flops=4 * mm,
        name="hidden",
    )
    du, sum_hidden = call(
        dact_body,
        [t_bf(ff), sds((8, ff), F32)],
        [dy, bc, slope],
        [None, wcols(1), tcols],
        [tcols, vcols(8)],
        (groups,),
        flops=4 * mm,
        name="dact",
    )
    (g_bc,) = call(
        outer_body,
        [sds((parts, groups, sub, 2 * units), BF)],
        [h2, dy, du, act],
        [
            None,
            None,
            pl.BlockSpec((ROWS, units), lambda i: (0, jnp.maximum(i - groups, 0))),
            pl.BlockSpec((ROWS, units), lambda i: (0, jnp.minimum(i, groups - 1))),
        ],
        [
            pl.BlockSpec(
                (parts, 1, sub, units), lambda i: (0, i % groups, 0, jnp.where(i < groups, 1, 0))
            )
        ],
        (2 * groups,),
        scratch=[pltpu.VMEM((width, ROWS), BF)],
        flops=8 * mm,
        name="outer_bc",
    )
    s_bc = lax.psum_scatter(
        g_bc.reshape(parts * groups, sub, 2 * units), axes, scatter_dimension=0, tiled=False
    ).astype(F32)

    own_shape = sds((slots * SLOT_ROWS, width), BF)

    def spread(own):
        crossed = mp_swap(own, 2)
        image = pl.BlockSpec((SLOT_ROWS, width), lambda i: (i, 0))
        (woven,) = call(
            functools.partial(weave_body, length),
            [sds((slots, length, groups, width), BF)],
            [info, own, mp_swap(own, 1), crossed, mp_swap(crossed, 1)],
            [smem] + [image] * 4,
            [pl.BlockSpec((1, length, groups, width), lambda i: (i, 0, 0, 0))],
            (slots,),
            flops=mm,
            limit=16,
            name="weave",
        )
        return woven.transpose(2, 0, 1, 3)

    act_late, g_bc_tie = lax.optimization_barrier((act, g_bc))
    (own_out,) = call(
        functools.partial(down_body, slots),
        [own_shape],
        [info, act_late, bc, middle, row(down_bias)],
        [smem, None, piece(1), None, None],
        scratch=[pltpu.VMEM((ROWS, width), F32)],
        flops=4 * mm,
        name="down",
    )
    all_out = spread(own_out)
    du, _ = lax.optimization_barrier((du, own_out))

    dmid, dlow, sums_mid = call(
        mid_back_body,
        [t_f(width), t_bf(width), sds((8, width), F32)],
        [dy, du, bc, middle, row(mlp_gain)],
        [None, None, piece(0), None, None],
        scratch=[pltpu.VMEM((ROWS, width), F32)],
        flops=4 * mm,
        name="mid_back",
    )
    (do,) = call(out_back_body, [t_bf(width)], [dlow, wo], flops=mm, name="out_back")
    dq, dk, dv = call(
        functools.partial(attend_back_body, slots),
        [t_bf(width)] * 3,
        [qkv, qkv, qkv, probs, do],
        [head(0), head(1), head(2), p_spec, head(0)],
        [head(0)] * 3,
        (pairs,),
        flops=2 * mm,
        name="attend_back",
    )
    def scatter_ring(keep, send):
        first, rest = mp_swap(send[:1], 1), mp_swap(send[1:], 1)
        total = keep[0].astype(F32) + first[0].astype(F32)
        for k in range(1, far):
            moved = hop(total.astype(BF))
            total = keep[k].astype(F32) + rest[k - 1].astype(F32) + moved.astype(F32)
        total = total.astype(BF)
        total = jnp.where(even, hop(total, False), total).reshape(2, 2, sub, -1)
        split = lambda a, b, first: (jnp.where(first, a, b), jnp.where(first, b, a))
        mine_half, other_half = split(total[:, 0], total[:, 1], even)
        total = mine_half.astype(F32) + mp_swap(other_half, 1).astype(F32)
        mine_half, other_half = split(total[0], total[1], mine < 2)
        return mine_half + mp_swap(other_half.astype(BF), 2).astype(F32)

    outer_ins = [h1, dq, dk, dv, dlow, mixed]
    sum_shape = sds((8, width), F32)
    if ring:
        leave = [jnp.where(even, far - k, k + 1 - far) for k in range(far)]
        stay = [jnp.where(even, k + 1 - far, far - k) for k in range(far)]
        half_shape = sds((far, groups, sub, 4 * local), BF)
        keep, send, sums_qkv = call(
            outer_ring_body,
            [half_shape, half_shape, sum_shape],
            [info_of(leave + stay)] + outer_ins,
            [smem] + [None] * len(outer_ins),
            scratch=[pltpu.VMEM((groups, width, 4 * local), BF)],
            flops=4 * mm,
            name="outer_a",
        )
        s_a = scatter_ring(keep, send)
    else:
        g_a, sums_qkv = call(
            outer_plain_body,
            [sds((parts, groups, sub, 4 * local), BF), sum_shape],
            outer_ins,
            flops=4 * mm,
            name="outer_a",
        )
        s_a = lax.psum_scatter(
            g_a.reshape(parts * groups, sub, 4 * local), axes, scatter_dimension=0, tiled=False
        ).astype(F32)
    own_grad, sums_in = call(
        functools.partial(input_back_body, slots),
        [own_shape, sum_shape],
        [x, dq, dk, dv, wq, dmid, row(norm_gain)],
        scratch=[pltpu.VMEM((ROWS, width), F32)],
        flops=3 * mm,
        name="input_back",
    )
    all_grad = spread(own_grad)

    sums = jnp.concatenate(
        [sums_in[:2].reshape(-1), sums_mid[:4].reshape(-1), sums_qkv[:2].reshape(-1), sum_hidden[0]]
    )
    for bit in (1, 2):
        sums = sums + mp_swap(sums, bit)
    bit = 1
    while bit < parts:
        sums = sums + dp_swap(sums, bit)
        bit *= 2
    vec = [sums[n * width : (n + 1) * width] for n in range(8)]
    own = lambda v, n: lax.dynamic_slice_in_dim(v, mine * n, n, 0)
    return (
        all_out,
        all_grad,
        vec[0],
        vec[1],
        s_a[:, : 3 * local],
        own(vec[6], local),
        own(vec[7], local),
        s_a[:, 3 * local :].T,
        vec[4],
        vec[2],
        vec[3],
        s_bc[:, :units],
        own(sums[8 * width :], units),
        s_bc[:, units:].T,
        vec[5],
    )


def solution(mesh):
    token = P(None, "dp", None, None)
    weight, turned = P("dp", "mp"), P("mp", "dp")
    return jax.shard_map(
        on_device,
        mesh=mesh,
        in_specs=(token, token, P(None, "dp"), P(), P(), weight, P("mp"), P("mp"), turned)
        + (P(), P(), P(), weight, P("mp"), turned, P()),
        out_specs=(token, token, P(), P(), weight, P("mp"), P("mp"), turned)
        + (P(), P(), P(), weight, P("mp"), turned, P()),
        check_vma=False,
    )
```

```python
import functools
import jax
import jax.numpy as jnp
from jax import lax
from jax.experimental import pallas as pl
from jax.experimental.pallas import tpu as pltpu
from jax.sharding import PartitionSpec as P


HEAD_DIM = 64
NORM_EPS = 1e-06
SLOT_ROWS = 200
ROWS = 1024
UNROLL = 5
BF = jnp.bfloat16
F32 = jnp.float32
NT = (((1,), (1,)), ((), ()))
NN = (((1,), (0,)), ((), ()))


def dot(a, b, dims=NN):
    return lax.dot_general(a, b, dims, preferred_element_type=F32)


def norm_stats(values):
    center = jnp.mean(values, axis=-1, keepdims=True)
    offset = values - center
    spread = jnp.mean(offset * offset, axis=-1, keepdims=True)
    scale_inv = lax.rsqrt(spread + NORM_EPS)
    return offset * scale_inv, scale_inv


def norm_back(upstream, normal, scale_inv, gain_vec):
    scaled = upstream * gain_vec
    return scale_inv * (
        scaled
        - jnp.mean(scaled, axis=-1, keepdims=True)
        - normal * jnp.mean(scaled * normal, axis=-1, keepdims=True)
    )


def colsum(values):
    return jnp.sum(values, axis=0, keepdims=True)


def call(body, outs, ins, in_specs=None, out_specs=None, grid=None, scratch=(), flops=0, nbytes=0, limit=60, **kw):
    full = lambda a: pl.BlockSpec(a.shape, (lambda *_: (0,) * len(a.shape)))
    if in_specs is None:
        in_specs = [None] * len(ins)
    if out_specs is None:
        out_specs = [None] * len(outs)
    in_specs = [full(a) if s is None else s for a, s in zip(ins, in_specs)]
    out_specs = [full(a) if s is None else s for a, s in zip(outs, out_specs)]
    nbytes = sum(a.size * a.dtype.itemsize for a in ins) + sum(a.size * a.dtype.itemsize for a in outs)
    return pl.pallas_call(
        body,
        out_shape=tuple(outs),
        grid=(1,) if grid is None else grid,
        in_specs=in_specs,
        out_specs=tuple(out_specs),
        scratch_shapes=list(scratch),
        compiler_params=pltpu.CompilerParams(vmem_limit_bytes=limit * 1024 * 1024),
        cost_estimate=pl.CostEstimate(flops=flops, bytes_accessed=nbytes, transcendentals=0),
        **kw,
    )(*ins)


def sds(shape, dtype):
    return jax.ShapeDtypeStruct(shape, dtype)


def loop(n, fn, unroll=1):
    lax.fori_loop(0, n, lambda i, c: (fn(i), c)[1], 0, unroll=unroll)


def cut(i, size):
    return pl.ds(pl.multiple_of(i * size, size), size)


def prep_body(slots, length, info_ref, x_ref, cot_ref, xo_ref, dy_ref):
    xo_ref[...] = jnp.zeros_like(xo_ref)
    dy_ref[...] = jnp.zeros_like(dy_ref)
    for i in range(slots):
        rows = slice(i * SLOT_ROWS, i * SLOT_ROWS + length)
        xo_ref[rows, :] = x_ref[0, i]

        @pl.when(i < info_ref[1])
        def _():
            dy_ref[rows, :] = cot_ref[0, i]


def place(info_ref, refs, buf_ref, group=0):
    for n, ref in enumerate(refs):
        sub = ref.shape[1]
        rows = pl.ds(pl.multiple_of(info_ref[2 + n] * sub, sub), sub)
        buf_ref[rows, :] = ref[group]


def weights(info_ref, refs, buf_ref):
    if len(refs) == 1:
        parts, groups, sub, cols = refs[0].shape
        return [refs[0][:, j].reshape(parts * sub, cols) for j in range(groups)]
    groups = refs[0].shape[0]
    for j in range(groups):
        place(info_ref, refs, buf_ref.at[j], j)
    return [buf_ref[j] for j in range(groups)]


def qkv_ring_body(info_ref, x_ref, gain_ref, shift_ref, bias_ref, *refs):
    h_ref, qkv_ref, wq_ref, wo_ref, buf_ref = refs[-5:]
    groups = buf_ref.shape[0]
    for j in range(groups):
        place(info_ref, refs[:-5], buf_ref.at[j], j)
    qkv_rest(lambda j: buf_ref[j], groups, x_ref, gain_ref, shift_ref, bias_ref, h_ref, qkv_ref, wq_ref, wo_ref)


def qkv_gathered_body(x_ref, gain_ref, shift_ref, bias_ref, wa_ref, h_ref, qkv_ref, wq_ref, wo_ref):
    parts, groups, sub, cols = wa_ref.shape
    qkv_rest(lambda j: wa_ref[:, j].reshape(parts * sub, cols), groups, x_ref, gain_ref, shift_ref, bias_ref, h_ref, qkv_ref, wq_ref, wo_ref)


def qkv_rest(piece, groups, x_ref, gain_ref, shift_ref, bias_ref, h_ref, qkv_ref, wq_ref, wo_ref):
    width = x_ref.shape[1]
    local = width // groups
    for j in range(groups):
        w = piece(j)
        for s in range(3):
            wq_ref[:, s * width + j * local : s * width + (j + 1) * local] = w[:, s * local : (s + 1) * local]
        wo_ref[:, j * local : (j + 1) * local] = w[:, 3 * local :]

    def norm(i):
        rows = cut(i, 128)
        normal, _ = norm_stats(x_ref[rows, :].astype(F32))
        h_ref[rows, :] = (normal * gain_ref[...] + shift_ref[...]).astype(BF)

    loop(ROWS // 128, norm)

    def project(n):
        cols = cut(n, 256)
        qkv_ref[:, cols] = (dot(h_ref[...], wq_ref[:, cols]) + bias_ref[:, cols]).astype(BF)

    loop(3 * width // 256, project)


def attend_body(slots, length, q_ref, k_ref, v_ref, o_ref, p_ref):
    low_half = lax.broadcasted_iota(jnp.int32, (SLOT_ROWS, 2 * HEAD_DIM), 1) < HEAD_DIM
    valid = lax.broadcasted_iota(jnp.int32, (SLOT_ROWS, SLOT_ROWS), 0) < length

    def image(i):
        rows = cut(i, SLOT_ROWS)
        q = q_ref[rows, :] * jnp.bfloat16(0.125)
        k = k_ref[rows, :]
        v_t = v_ref[rows, :].T
        zero = jnp.zeros_like(k)
        mixed = []
        for h in range(2):
            s = dot(jnp.where(low_half if h == 0 else ~low_half, k, zero), q, NT)
            s = jnp.where(valid, s, -1e30)
            e = jnp.exp(s - jnp.max(s, axis=0, keepdims=True))
            p = (e * (1.0 / jnp.sum(e, axis=0, keepdims=True))).astype(BF)
            p_ref[h, i] = p
            mixed.append(dot(v_t[h * HEAD_DIM : (h + 1) * HEAD_DIM], p))
        o_ref[rows, :] = jnp.concatenate(mixed, axis=0).T.astype(BF)

    loop(slots, image, UNROLL)
    tail = slots * SLOT_ROWS
    o_ref[tail:, :] = jnp.zeros((ROWS - tail, 2 * HEAD_DIM), BF)


def mix_body(x_ref, o_ref, wo_ref, bias_ref, gain_ref, shift_ref, mid_ref, h_ref):
    mid_ref[...] = dot(o_ref[...], wo_ref[...], NT)

    def norm(i):
        rows = cut(i, 128)
        mid = x_ref[rows, :].astype(F32) + (mid_ref[rows, :] + bias_ref[...])
        mid_ref[rows, :] = mid
        normal, _ = norm_stats(mid)
        h_ref[rows, :] = (normal * gain_ref[...] + shift_ref[...]).astype(BF)

    loop(mid_ref.shape[0] // 128, norm)


def hidden_body(info_ref, h_ref, bias_ref, *refs):
    act_ref, slope_ref, buf_ref = refs[-3:]
    (w,) = weights(info_ref, refs[:-3], buf_ref)

    def chunk(i):
        rows = cut(i, 256)
        u = dot(h_ref[rows, :], w) + bias_ref[...]
        half = 0.5 * (1.0 + lax.erf(u * 0.7071067811865476))
        act_ref[rows, :] = (u * half).astype(BF)
        slope_ref[rows, :] = (half + u * jnp.exp(-0.5 * u * u) * 0.3989422804014327).astype(BF)

    loop(ROWS // 256, chunk)


def wide_dot(left_ref, ws, acc_ref):
    for j, w in enumerate(ws):
        cols = w.shape[1]
        part = dot(left_ref[:, j * cols : (j + 1) * cols], w, NT)
        if j == 0:
            acc_ref[...] = part
        else:
            acc_ref[...] += part


def down_body(slots, info_ref, act_ref, mid_ref, bias_ref, *refs):
    out_ref, acc_ref, buf_ref = refs[-3:]
    wide_dot(act_ref, weights(info_ref, refs[:-3], buf_ref), acc_ref)
    for i in range(slots):
        rows = slice(i * SLOT_ROWS, (i + 1) * SLOT_ROWS)
        live = jnp.where(i < info_ref[1], 1.0, 0.0)
        out_ref[rows, :] = ((mid_ref[rows, :] + acc_ref[rows, :] + bias_ref[...]) * live).astype(BF)


def weave_body(length, info_ref, a_ref, b_ref, c_ref, d_ref, o_ref):
    def part(start, n, keep):
        x = jnp.concatenate([r[start : start + n, :] for r in (a_ref, b_ref, c_ref, d_ref)], axis=0)
        row = lax.broadcasted_iota(jnp.int32, (4 * n, 4 * n), 0)
        col = lax.broadcasted_iota(jnp.int32, (4 * n, 4 * n), 1)
        take = jnp.where(lax.bitwise_xor(row % 4, info_ref[0]) * n + row // 4 == col, 1.0, 0.0).astype(BF)
        y = dot(take, x).astype(BF).reshape(n, 4, x.shape[1])
        o_ref[0, start : start + keep] = y[:keep]

    full = length // 64 * 64
    for start in range(0, full, 64):
        part(start, 64, 64)
    part(full, 8, length - full)


def outer_steps(h_ref, dy_ref, du_ref, act_ref, t_ref, store):
    step = pl.program_id(0)
    half = pl.num_programs(0) // 2

    @pl.when(step == 0)
    def _():
        t_ref[...] = dy_ref[...].T

    @pl.when(step == half)
    def _():
        t_ref[...] = h_ref[...].T

    pl.when(step < half)(lambda: store(dot(t_ref[...], act_ref[...]).astype(BF)))
    pl.when(step >= half)(lambda: store(dot(t_ref[...], du_ref[...]).astype(BF)))


def outer_body(h_ref, dy_ref, du_ref, act_ref, g_ref, t_ref):
    parts, _, sub, cols = g_ref.shape

    def store(g):
        g_ref[:, 0] = g.reshape(parts, sub, cols)

    outer_steps(h_ref, dy_ref, du_ref, act_ref, t_ref, store)


def outer_halves_body(info_ref, h_ref, dy_ref, du_ref, act_ref, *refs):
    halves, t_ref, buf_ref = refs[:-2], refs[-2], refs[-1]

    def store(g):
        buf_ref[...] = g
        for n, ref in enumerate(halves):
            sub = ref.shape[1]
            ref[0] = buf_ref[pl.ds(pl.multiple_of(info_ref[2 + n] * sub, sub), sub), :]

    outer_steps(h_ref, dy_ref, du_ref, act_ref, t_ref, store)


def dact_body(info_ref, dy_ref, slope_ref, *refs):
    du_ref, sum_ref, buf_ref = refs[-3:]
    (w,) = weights(info_ref, refs[:-3], buf_ref)
    cols = w.shape[1]
    total = jnp.zeros((1, cols), F32)
    for i in range(ROWS // 256):
        rows = slice(i * 256, (i + 1) * 256)
        du = (dot(dy_ref[rows, :], w) * slope_ref[rows, :].astype(F32)).astype(BF)
        du_ref[rows, :] = du
        total = total + colsum(du.astype(F32))
    sum_ref[...] = jnp.broadcast_to(total, sum_ref.shape)


def mid_back_body(info_ref, dy_ref, du_ref, mid_ref, gain_ref, *refs):
    dmid_ref, dlow_ref, sums_ref, acc_ref, buf_ref = refs[-5:]
    wide_dot(du_ref, weights(info_ref, refs[:-5], buf_ref), acc_ref)
    width = dy_ref.shape[1]

    def chunk(i, sums):
        rows = cut(i, 128)
        dh = acc_ref[rows, :]
        normal, scale_inv = norm_stats(mid_ref[rows, :])
        dy = dy_ref[rows, :].astype(F32)
        dmid = dy + norm_back(dh, normal, scale_inv, gain_ref[...])
        dmid_ref[rows, :] = dmid
        dlow_ref[rows, :] = dmid.astype(BF)
        new = (colsum(dh * normal), colsum(dh), colsum(dmid), colsum(dy))
        return tuple(a + b for a, b in zip(sums, new))

    zero = jnp.zeros((1, width), F32)
    sums = lax.fori_loop(0, ROWS // 128, chunk, (zero,) * 4)
    for n in range(4):
        sums_ref[n : n + 1, :] = sums[n]


def out_back_body(dlow_ref, wo_ref, do_ref):
    do_ref[...] = dot(dlow_ref[...], wo_ref[...]).astype(BF)


def attend_back_body(slots, q_ref, k_ref, v_ref, p_ref, do_ref, *refs):
    dq_ref, dk_ref, dv_ref = refs[-3:]
    low_half = lax.broadcasted_iota(jnp.int32, (SLOT_ROWS, 2 * HEAD_DIM), 1) < HEAD_DIM

    def image(i):
        rows = cut(i, SLOT_ROWS)
        q = q_ref[rows, :] * jnp.bfloat16(0.125)
        k_t = (k_ref[rows, :] * jnp.bfloat16(0.125)).T
        v = v_ref[rows, :]
        do = do_ref[rows, :]
        zero = jnp.zeros_like(v)
        grads = []
        for h in range(2):
            p = p_ref[h, i]
            pf = p.astype(F32)
            dp = dot(jnp.where(low_half if h == 0 else ~low_half, v, zero), do, NT)
            ds = (pf * (dp - jnp.sum(pf * dp, axis=0, keepdims=True))).astype(BF)
            grads.append((dot(k_t[h * HEAD_DIM : (h + 1) * HEAD_DIM], ds), dot(ds, q), dot(p, do)))
        (dq0, dk0, dv0), (dq1, dk1, dv1) = grads
        dq_ref[rows, :] = jnp.concatenate([dq0, dq1], axis=0).T.astype(BF)
        dk_ref[rows, :] = jnp.where(low_half, dk0, dk1).astype(BF)
        dv_ref[rows, :] = jnp.where(low_half, dv0, dv1).astype(BF)

    loop(slots, image, UNROLL)
    tail = slots * SLOT_ROWS
    for ref in (dq_ref, dk_ref, dv_ref):
        ref[tail:, :] = jnp.zeros((ROWS - tail, 2 * HEAD_DIM), BF)


def small_outer(h_ref, dq_ref, dk_ref, dv_ref, dlow_ref, o_ref, sums_ref, store):
    ht = h_ref[...].T
    for s, ref in enumerate((dq_ref, dk_ref, dv_ref)):
        store(s, dot(ht, ref[...]).astype(BF))
        if s != 1:
            n = 0 if s == 0 else 1
            sums_ref[n : n + 1, :] = colsum(ref[...].astype(F32))
    store(3, dot(dlow_ref[...].T, o_ref[...]).astype(BF))


def outer_ring_body(info_ref, h_ref, dq_ref, dk_ref, dv_ref, dlow_ref, o_ref, *refs):
    halves, sums_ref, buf_ref = refs[:-2], refs[-2], refs[-1]
    groups = buf_ref.shape[0]
    local = h_ref.shape[1] // groups

    def store(s, g):
        for j in range(groups):
            buf_ref[j, :, s * local : (s + 1) * local] = g[:, j * local : (j + 1) * local]

    small_outer(h_ref, dq_ref, dk_ref, dv_ref, dlow_ref, o_ref, sums_ref, store)
    for n, ref in enumerate(halves):
        sub = ref.shape[1]
        rows = pl.ds(pl.multiple_of(info_ref[2 + n] * sub, sub), sub)
        for j in range(groups):
            ref[j] = buf_ref[j, rows, :]


def outer_plain_body(h_ref, dq_ref, dk_ref, dv_ref, dlow_ref, o_ref, g_ref, sums_ref):
    parts, groups, sub, cols = g_ref.shape
    local = cols // 4

    def store(s, g):
        for j in range(groups):
            g_ref[:, j, :, s * local : (s + 1) * local] = g[:, j * local : (j + 1) * local].reshape(parts, sub, local)

    small_outer(h_ref, dq_ref, dk_ref, dv_ref, dlow_ref, o_ref, sums_ref, store)


def input_back_body(slots, x_ref, dq_ref, dk_ref, dv_ref, wq_ref, dmid_ref, gain_ref, out_ref, sums_ref, acc_ref):
    width = x_ref.shape[1]
    for s, ref in enumerate((dq_ref, dk_ref, dv_ref)):
        part = dot(ref[...], wq_ref[:, s * width : (s + 1) * width], NT)
        if s == 0:
            acc_ref[...] = part
        else:
            acc_ref[...] += part

    sums = [jnp.zeros((1, width), F32)] * 2
    for i in range(slots):
        rows = slice(i * SLOT_ROWS, (i + 1) * SLOT_ROWS)
        dh = acc_ref[rows, :]
        normal, scale_inv = norm_stats(x_ref[rows, :].astype(F32))
        grad = dmid_ref[rows, :] + norm_back(dh, normal, scale_inv, gain_ref[...])
        out_ref[rows, :] = grad.astype(BF)
        sums[0] = sums[0] + colsum(dh * normal)
        sums[1] = sums[1] + colsum(dh)
    for n in range(2):
        sums_ref[n : n + 1, :] = sums[n]


def block_step(
    inputs, cotangent, counts, norm_gain, norm_shift, qkv_weight, query_bias, value_bias,
    out_weight, out_bias, mlp_gain, mlp_shift, hidden_weight, hidden_bias, down_weight, down_bias,
):
    _, slots, length, width = inputs.shape
    sub = qkv_weight.shape[0]
    local = qkv_weight.shape[1] // 3
    units = hidden_weight.shape[1]
    parts, groups = width // sub, width // local
    ff = units * groups
    axes = ("dp", "mp")
    mine = lax.axis_index("mp")
    ring = sub % 32 == 0

    cycle = list(range(0, parts, 2)) + list(range(parts - 1, 0, -2))
    place = [cycle.index(d) for d in range(parts)]
    here = jnp.array(place, jnp.int32)[lax.axis_index("dp")]
    owner = jnp.array(cycle, jnp.int32)
    far = parts // 2
    mp_swap = lambda a, bit: lax.ppermute(a, "mp", [(j, j ^ bit) for j in range(groups)])
    dp_swap = lambda a, bit: lax.ppermute(a, "dp", [(d, d ^ bit) for d in range(parts)])

    def hop(a, odd=True):
        pairs = []
        for p in range(parts):
            for j in range(groups):
                if j % 2 == 0:
                    pairs.append((cycle[p] * groups + j, cycle[(p + 1) % parts] * groups + j))
                elif odd:
                    pairs.append((cycle[p] * groups + j, cycle[(p - 1) % parts] * groups + j))
        return lax.ppermute(a, axes, pairs)

    even = mine % 2 == 0
    row = lambda v: v.reshape(1, -1)
    live = lax.dynamic_index_in_dim(counts, mine, 0, keepdims=False)[0]

    def info_of(offsets):
        return jnp.concatenate([jnp.stack([mine, live]), owner[(here + jnp.stack(offsets)) % parts]])

    smem = pl.BlockSpec(memory_space=pltpu.SMEM)
    info = jnp.stack([mine, live])

    mm = 2 * ROWS * width * width
    t_bf = lambda n: sds((ROWS, n), BF)
    t_f = lambda n: sds((ROWS, n), F32)
    block = lambda shape: pl.BlockSpec(shape, lambda i, info: (0,) * len(shape))
    mine_block = pl.BlockSpec((1, slots, length, width), lambda i, info: (info[0], 0, 0, 0))
    x, dy = pl.pallas_call(
        functools.partial(prep_body, slots, length),
        out_shape=(t_bf(width), t_bf(width)),
        grid_spec=pltpu.PrefetchScalarGridSpec(
            num_scalar_prefetch=1,
            grid=(1,),
            in_specs=[mine_block, mine_block],
            out_specs=[block((ROWS, width)), block((ROWS, width))],
        ),
        compiler_params=pltpu.CompilerParams(vmem_limit_bytes=24 * 1024 * 1024),
        cost_estimate=pl.CostEstimate(flops=0, bytes_accessed=8 * ROWS * width, transcendentals=0),
        name="prep",
    )(info, inputs, cotangent)

    def scatter_ring(halves):
        got = [mp_swap(send, 1) for send in halves[far:]]

        def term(n):
            return halves[n].astype(F32) + got[n].astype(F32)

        total = term(0)
        for k in range(1, far):
            moved = hop(total.astype(BF))
            total = term(k) + moved.astype(F32)
        total = total.astype(BF)
        last = hop(total, False)
        total = jnp.where(even, last, total).reshape(2, 2, sub, -1)
        split = lambda a, b, first: (jnp.where(first, a, b), jnp.where(first, b, a))
        mine_half, other_half = split(total[:, 0], total[:, 1], even)
        total = mine_half.astype(F32) + mp_swap(other_half, 1).astype(F32)
        mine_half, other_half = split(total[0], total[1], mine < 2)
        return mine_half + mp_swap(other_half.astype(BF), 2).astype(F32)

    leave = [jnp.where(even, far - k, k + 1 - far) for k in range(far)]
    stay = [jnp.where(even, k + 1 - far, far - k) for k in range(far)]
    halves = lambda n: [sds((groups, sub, n), BF)] * (2 * far)

    shard_bc = jnp.concatenate([hidden_weight, down_weight.T], axis=1)
    shard_a = jnp.concatenate([qkv_weight, out_weight.T], axis=1)
    vectors = jnp.concatenate([query_bias, value_bias, hidden_bias])

    def chip_chunk(shard):
        two = jnp.stack([shard, mp_swap(shard, 2)])
        near = mp_swap(two, 1)
        rel = [two[0], near[0], two[1], near[1]]
        rel = [jnp.where(even, rel[j], rel[j ^ 1]) for j in range(groups)]
        return jnp.stack([jnp.where(mine < 2, rel[j], rel[j ^ 2]) for j in range(groups)])

    def gather_ring(start, between):
        chunks, held = [start], start
        for k in range(1, far):
            held = hop(held)
            held = between(k, held)
            chunks += [held, mp_swap(held, 1)]
        half = hop(jnp.where(even, held[: groups // 2], held[groups // 2 :]))
        other = mp_swap(half, 1)
        first, second = jnp.where(even, half, other), jnp.where(even, other, half)
        return chunks + [jnp.concatenate([first, second])], half

    if ring:
        side = jnp.where(even, 1, -1)
        offsets = [jnp.int32(0)]
        for k in range(1, far):
            offsets += [-k * side, k * side]
        ring_info = info_of(offsets + [jnp.int32(far)])
        start_bc = chip_chunk(shard_bc)
        prepared = (x, dy)

        def between(k, held):
            nonlocal prepared
            if k == 1:
                held, prepared = lax.optimization_barrier((held, prepared))
            return held

        chunks, last = gather_ring(chip_chunk(shard_a), between)
        x, dy = prepared
        start_bc, last = lax.optimization_barrier((start_bc, last))
        bc, _ = gather_ring(start_bc, lambda k, held: held)
        piece = lambda n: [pl.BlockSpec((groups, sub, units), lambda i: (0, 0, n))] * len(bc)
        wcols = lambda n: [pl.BlockSpec((1, sub, units), lambda i: (i, 0, n))] * len(bc)
    else:
        ring_info = info
        wa = lax.all_gather(shard_a, axes, axis=0, tiled=False).reshape(parts, groups, sub, 4 * local)
        bc = [lax.all_gather(shard_bc, axes, axis=0, tiled=False).reshape(parts, groups, sub, 2 * units)]
        piece = lambda n: [pl.BlockSpec((parts, groups, sub, units), lambda i: (0, 0, 0, n))]
        wcols = lambda n: [pl.BlockSpec((parts, 1, sub, units), lambda i: (0, i, 0, n))]
    two = jnp.stack([vectors, mp_swap(vectors, 1)])
    four = jnp.concatenate([two, mp_swap(two, 2)])
    biases = four[jnp.arange(groups) ^ mine]
    qb, vb, hb = (biases[:, a:b].reshape(-1) for a, b in ((0, local), (local, 2 * local), (2 * local, None)))
    bias_row = row(jnp.concatenate([qb, jnp.zeros_like(qb), vb]))

    qkv_outs = [t_bf(width), t_bf(3 * width), sds((width, 3 * width), BF), sds((width, width), BF)]
    qkv_ins = [x, row(norm_gain), row(norm_shift), bias_row]
    if ring:
        h1, qkv, wq, wo = call(
            qkv_ring_body,
            qkv_outs,
            [ring_info] + qkv_ins + chunks,
            [smem] + [None] * (len(qkv_ins) + len(chunks)),
            scratch=[pltpu.VMEM((groups, width, 4 * local), BF)],
            flops=3 * mm,
        )
    else:
        h1, qkv, wq, wo = call(qkv_gathered_body, qkv_outs, qkv_ins + [wa], flops=3 * mm)
    pair = 2 * HEAD_DIM
    pairs = width // pair
    head = lambda s: pl.BlockSpec((ROWS, pair), lambda i: (0, s * pairs + i))
    p_spec = pl.BlockSpec((2, slots, SLOT_ROWS, SLOT_ROWS), lambda i: (i, 0, 0, 0))
    p_shape = sds((2 * pairs, slots, SLOT_ROWS, SLOT_ROWS), BF)
    mixed, probs = call(
        functools.partial(attend_body, slots, length),
        [t_bf(width), p_shape],
        [qkv, qkv, qkv],
        [head(0), head(1), head(2)],
        [head(0), p_spec],
        (pairs,),
        flops=mm,
    )
    rows256 = pl.BlockSpec((256, width), lambda i: (i, 0))
    middle, h2 = call(
        mix_body,
        [t_f(width), t_bf(width)],
        [x, mixed, wo, row(out_bias), row(mlp_gain), row(mlp_shift)],
        [rows256, rows256, None, None, None, None],
        [rows256, rows256],
        (ROWS // 256,),
        flops=mm,
    )
    tcols = pl.BlockSpec((ROWS, units), lambda i: (0, i))
    vcols = lambda n: pl.BlockSpec((n, units), lambda i: (0, i))
    group_buf = lambda n: pltpu.VMEM((n, width, units), BF)
    act, slope = call(
        hidden_body,
        [t_bf(ff), t_bf(ff)],
        [ring_info, h2, row(hb)] + bc,
        [smem, None, vcols(1)] + wcols(0),
        [tcols, tcols],
        (groups,),
        scratch=[group_buf(1)],
        flops=4 * mm,
    )
    du, sum_hidden = call(
        dact_body,
        [t_bf(ff), sds((8, ff), F32)],
        [ring_info, dy, slope] + bc,
        [smem, None, tcols] + wcols(1),
        [tcols, vcols(8)],
        (groups,),
        scratch=[group_buf(1)],
        flops=4 * mm,
    )
    outer_in_specs = [
        None,
        None,
        pl.BlockSpec((ROWS, units), lambda i: (0, jnp.maximum(i - groups, 0))),
        pl.BlockSpec((ROWS, units), lambda i: (0, jnp.minimum(i, groups - 1))),
    ]
    outer_map = lambda i: (0, i % groups, 0, jnp.where(i < groups, 1, 0))
    transposed = pltpu.VMEM((width, ROWS), BF)
    if ring:
        halves_bc = call(
            outer_halves_body,
            halves(2 * units),
            [info_of(leave + stay), h2, dy, du, act],
            [smem] + outer_in_specs,
            [pl.BlockSpec((1, sub, units), lambda i: outer_map(i)[1:])] * (2 * far),
            (2 * groups,),
            scratch=[transposed, pltpu.VMEM((width, units), BF)],
            flops=8 * mm,
        )
        s_bc = scatter_ring(halves_bc)
        g_bc = halves_bc[0]
    else:
        (g_bc,) = call(
            outer_body,
            [sds((parts, groups, sub, 2 * units), BF)],
            [h2, dy, du, act],
            outer_in_specs,
            [pl.BlockSpec((parts, 1, sub, units), outer_map)],
            (2 * groups,),
            scratch=[transposed],
            flops=8 * mm,
        )
        s_bc = lax.psum_scatter(
            g_bc.reshape(parts * groups, sub, 2 * units), axes, scatter_dimension=0, tiled=False
        ).astype(F32)

    own_shape = sds((slots * SLOT_ROWS, width), BF)

    def spread(own):
        crossed = mp_swap(own, 2)
        image = pl.BlockSpec((SLOT_ROWS, width), lambda i: (i, 0))
        (woven,) = call(
            functools.partial(weave_body, length),
            [sds((slots, length, groups, width), BF)],
            [info, own, mp_swap(own, 1), crossed, mp_swap(crossed, 1)],
            [smem] + [image] * 4,
            [pl.BlockSpec((1, length, groups, width), lambda i: (i, 0, 0, 0))],
            (slots,),
            flops=mm,
            limit=16,
        )
        return woven.transpose(2, 0, 1, 3)

    down_info = jnp.concatenate([info, ring_info[2:]])
    act_late, _ = lax.optimization_barrier((act, g_bc))
    (own_out,) = call(
        functools.partial(down_body, slots),
        [own_shape],
        [down_info, act_late, middle, row(down_bias)] + bc,
        [smem, None, None, None] + piece(1),
        scratch=[pltpu.VMEM((ROWS, width), F32), group_buf(groups)],
        flops=4 * mm,
    )
    all_out = spread(own_out)
    du, _ = lax.optimization_barrier((du, own_out))

    dmid, dlow, sums_mid = call(
        mid_back_body,
        [t_f(width), t_bf(width), sds((8, width), F32)],
        [ring_info, dy, du, middle, row(mlp_gain)] + bc,
        [smem, None, None, None, None] + piece(0),
        scratch=[pltpu.VMEM((ROWS, width), F32), group_buf(groups)],
        flops=4 * mm,
    )
    (do,) = call(out_back_body, [t_bf(width)], [dlow, wo], flops=mm)
    grads = []
    hbm = pl.BlockSpec(memory_space=pl.ANY)
    calls = 3 if pairs % 3 == 0 else 1
    for n in range(calls):
        first = n * pairs // calls
        at = lambda s, first=first: pl.BlockSpec((ROWS, pair), lambda i: (0, s * pairs + first + i))
        grads = call(
            functools.partial(attend_back_body, slots),
            [t_bf(width)] * 3,
            [qkv, qkv, qkv, probs, do] + list(grads),
            [at(0), at(1), at(2), pl.BlockSpec((2, slots, SLOT_ROWS, SLOT_ROWS), lambda i, first=first: (first + i, 0, 0, 0)), at(0)]
            + [hbm] * len(grads),
            [at(0)] * 3,
            (pairs // calls,),
            flops=2 * mm // calls,
            limit=24,
            input_output_aliases={5 + m: m for m in range(len(grads))},
        )
    dq, dk, dv = grads
    outer_ins = [h1, dq, dk, dv, dlow, mixed]
    sum_shape = sds((8, width), F32)
    if ring:
        *halves_a, sums_qkv = call(
            outer_ring_body,
            halves(4 * local) + [sum_shape],
            [info_of(leave + stay)] + outer_ins,
            [smem] + [None] * len(outer_ins),
            scratch=[pltpu.VMEM((groups, width, 4 * local), BF)],
            flops=4 * mm,
        )
        s_a = scatter_ring(halves_a)
    else:
        g_a, sums_qkv = call(
            outer_plain_body, [sds((parts, groups, sub, 4 * local), BF), sum_shape], outer_ins, flops=4 * mm
        )
        s_a = lax.psum_scatter(
            g_a.reshape(parts * groups, sub, 4 * local), axes, scatter_dimension=0, tiled=False
        ).astype(F32)
    own_grad, sums_in = call(
        functools.partial(input_back_body, slots),
        [own_shape, sum_shape],
        [x, dq, dk, dv, wq, dmid, row(norm_gain)],
        scratch=[pltpu.VMEM((ROWS, width), F32)],
        flops=3 * mm,
    )
    sums = jnp.concatenate(
        [sums_in[:2].reshape(-1), sums_mid[:4].reshape(-1), sums_qkv[:2].reshape(-1), sum_hidden[0]]
    )
    all_grad = spread(own_grad)
    sums = sums + mp_swap(sums, 1)
    bit = 1
    while bit < parts:
        sums = sums + dp_swap(sums, bit)
        bit *= 2
    sums = sums + mp_swap(sums, 2)
    vec = [sums[n * width : (n + 1) * width] for n in range(8)]
    own = lambda v, n: lax.dynamic_slice_in_dim(v, mine * n, n, 0)
    return (
        all_out,
        all_grad,
        vec[0],
        vec[1],
        s_a[:, : 3 * local],
        own(vec[6], local),
        own(vec[7], local),
        s_a[:, 3 * local :].T,
        vec[4],
        vec[2],
        vec[3],
        s_bc[:, :units],
        own(sums[8 * width :], units),
        s_bc[:, units:].T,
        vec[5],
    )


def solution(mesh):
    token = P(None, "dp", None, None)
    weight, turned = P("dp", "mp"), P("mp", "dp")
    return jax.shard_map(
        block_step,
        mesh=mesh,
        in_specs=(token, token, P(None, "dp"), P(), P(), weight, P("mp"), P("mp"), turned)
        + (P(), P(), P(), weight, P("mp"), turned, P()),
        out_specs=(token, token, P(), P(), weight, P("mp"), P("mp"), turned)
        + (P(), P(), P(), weight, P("mp"), turned, P()),
        check_vma=False,
    )
```

```python
import functools
import jax
import jax.numpy as jnp
from jax import lax
from jax.experimental import pallas as pl
from jax.experimental.pallas import tpu as pltpu
from jax.sharding import PartitionSpec as P


HEAD_DIM = 64
NORM_EPS = 1e-06
SLOT_ROWS = 200
ROWS = 1024
BF = jnp.bfloat16
F32 = jnp.float32
NT = (((1,), (1,)), ((), ()))
NN = (((1,), (0,)), ((), ()))


def dot(a, b, dims=NN):
    return lax.dot_general(a, b, dims, preferred_element_type=F32)


def norm_stats(values):
    center = jnp.mean(values, axis=-1, keepdims=True)
    offset = values - center
    spread = jnp.mean(offset * offset, axis=-1, keepdims=True)
    scale_inv = lax.rsqrt(spread + NORM_EPS)
    return offset * scale_inv, scale_inv


def norm_back(upstream, normal, scale_inv, gain_vec):
    scaled = upstream * gain_vec
    return scale_inv * (
        scaled
        - jnp.mean(scaled, axis=-1, keepdims=True)
        - normal * jnp.mean(scaled * normal, axis=-1, keepdims=True)
    )


def colsum(values):
    return jnp.sum(values, axis=0, keepdims=True)


def call(body, outs, ins, in_specs=None, out_specs=None, grid=None, scratch=(), flops=0, nbytes=0, limit=60, **kw):
    full = lambda a: pl.BlockSpec(a.shape, (lambda *_: (0,) * len(a.shape)))
    if in_specs is None:
        in_specs = [None] * len(ins)
    if out_specs is None:
        out_specs = [None] * len(outs)
    in_specs = [full(a) if s is None else s for a, s in zip(ins, in_specs)]
    out_specs = [full(a) if s is None else s for a, s in zip(outs, out_specs)]
    nbytes = sum(a.size * a.dtype.itemsize for a in ins) + sum(a.size * a.dtype.itemsize for a in outs)
    return pl.pallas_call(
        body,
        out_shape=tuple(outs),
        grid=(1,) if grid is None else grid,
        in_specs=in_specs,
        out_specs=tuple(out_specs),
        scratch_shapes=list(scratch),
        compiler_params=pltpu.CompilerParams(vmem_limit_bytes=limit * 1024 * 1024),
        cost_estimate=pl.CostEstimate(flops=flops, bytes_accessed=nbytes, transcendentals=0),
        **kw,
    )(*ins)


def sds(shape, dtype):
    return jax.ShapeDtypeStruct(shape, dtype)


def loop(n, fn, unroll=1):
    lax.fori_loop(0, n, lambda i, c: (fn(i), c)[1], 0, unroll=unroll)


def cut(i, size):
    return pl.ds(pl.multiple_of(i * size, size), size)


def prep_body(info_ref, in_ref, out_ref):
    out_ref[...] = jnp.zeros_like(out_ref)
    _, slots, length, _ = in_ref.shape
    for i in range(slots):

        @pl.when(i < info_ref[1])
        def _():
            out_ref[i * SLOT_ROWS : i * SLOT_ROWS + length, :] = in_ref[0, i]


def place(info_ref, refs, dst_ref, group=0, cols=slice(None), into=slice(None)):
    if len(refs) == 1:
        parts, _, sub, _ = refs[0].shape
        dst_ref[:, into] = refs[0][:, group, :, cols].reshape(parts * sub, -1)
        return
    for n, ref in enumerate(refs):
        sub = ref.shape[1]
        rows = pl.ds(pl.multiple_of(info_ref[2 + n] * sub, sub), sub)
        dst_ref[rows, into] = ref[group, :, cols]


def qkv_body(info_ref, x_ref, gain_ref, shift_ref, bias_ref, *refs):
    h_ref, qkv_ref, wq_ref, wo_ref = refs[-4:]
    chunks = refs[:-4]
    width = x_ref.shape[1]
    groups = chunks[0].shape[0 if len(chunks) > 1 else 1]
    local = width // groups

    def columns(s, dst_ref):
        for j in range(groups):
            place(info_ref, chunks, dst_ref, j, slice(s * local, (s + 1) * local), slice(j * local, (j + 1) * local))

    step = pl.program_id(0)

    @pl.when(step == 0)
    def _():
        def norm(i):
            rows = cut(i, 128)
            normal, _ = norm_stats(x_ref[rows, :].astype(F32))
            h_ref[rows, :] = (normal * gain_ref[...] + shift_ref[...]).astype(BF)

        loop(ROWS // 128, norm, 2)
        columns(3, wo_ref)

    for s in range(3):
        pl.when(step == s)(functools.partial(columns, s, wq_ref))
    qkv_ref[...] = (dot(h_ref[...], wq_ref[...]) + bias_ref[...]).astype(BF)


def half_masks():
    low_half = lax.broadcasted_iota(jnp.int32, (SLOT_ROWS, 2 * HEAD_DIM), 1) < HEAD_DIM
    return low_half, ~low_half


def attend_body(slots, length, q_ref, k_ref, v_ref, o_ref, p_ref, s_ref):
    masks = half_masks()
    tile = length // 8 * 8
    valid = lax.broadcasted_iota(jnp.int32, (SLOT_ROWS - tile, SLOT_ROWS), 0) < length - tile
    rows = [slice(i * SLOT_ROWS, (i + 1) * SLOT_ROWS) for i in range(slots)]

    def scores(i):
        q = q_ref[rows[i], :] * jnp.bfloat16(0.125)
        k = k_ref[rows[i], :]
        for h in range(2):
            s_ref[h, i] = dot(jnp.where(masks[h], k, jnp.zeros_like(k)), q, NT)

    def softmax(i):
        for h in range(2):
            s_ref[h, i, tile:] = jnp.where(valid, s_ref[h, i, tile:], -1e30)
            s = s_ref[h, i]
            e = jnp.exp(s - jnp.max(s, axis=0, keepdims=True))
            p_ref[h, i] = (e * (1.0 / jnp.sum(e, axis=0, keepdims=True))).astype(BF)

    def mix(i):
        v_t = v_ref[rows[i], :].T
        mixed = [dot(v_t[h * HEAD_DIM : (h + 1) * HEAD_DIM], p_ref[h, i]) for h in range(2)]
        o_ref[rows[i], :] = jnp.concatenate(mixed, axis=0).T.astype(BF)

    for i in range(slots):
        scores(i)
    for i in range(slots):
        softmax(i)
    for i in range(slots):
        mix(i)
    tail = slots * SLOT_ROWS
    o_ref[tail:, :] = jnp.zeros((ROWS - tail, 2 * HEAD_DIM), BF)


def mix_body(x_ref, o_ref, wo_ref, bias_ref, gain_ref, shift_ref, mid_ref, h_ref):
    mid_ref[...] = dot(o_ref[...], wo_ref[...], NT)

    def norm(i):
        rows = cut(i, 128)
        mid = x_ref[rows, :].astype(F32) + (mid_ref[rows, :] + bias_ref[...])
        mid_ref[rows, :] = mid
        normal, _ = norm_stats(mid)
        h_ref[rows, :] = (normal * gain_ref[...] + shift_ref[...]).astype(BF)

    loop(mid_ref.shape[0] // 128, norm)


def hidden_body(info_ref, h_ref, bias_ref, *refs):
    act_ref, slope_ref, buf_ref = refs[-3:]
    place(info_ref, refs[:-3], buf_ref)
    w = buf_ref[...]

    def chunk(i):
        rows = cut(i, 256)
        u = dot(h_ref[rows, :], w) + bias_ref[...]
        half = 0.5 * (1.0 + lax.erf(u * 0.7071067811865476))
        act_ref[rows, :] = (u * half).astype(BF)
        slope_ref[rows, :] = (half + u * jnp.exp(-0.5 * u * u) * 0.3989422804014327).astype(BF)

    loop(ROWS // 256, chunk, 4)


def wide_dot(info_ref, left_ref, refs, buf_ref):
    groups, _, cols = buf_ref.shape

    @pl.when(pl.program_id(0) == 0)
    def _():
        for j in range(groups):
            place(info_ref, refs, buf_ref.at[j], j)

    return sum(dot(left_ref[:, j * cols : (j + 1) * cols], buf_ref[j], NT) for j in range(groups))


def down_body(info_ref, act_ref, mid_ref, bias_ref, *refs):
    out_ref, buf_ref = refs[-2:]
    value = mid_ref[...] + wide_dot(info_ref, act_ref, refs[:-2], buf_ref) + bias_ref[...]
    rows = out_ref.shape[0]
    row = pl.program_id(0) * rows + lax.broadcasted_iota(jnp.int32, (rows, 1), 0)
    out_ref[...] = jnp.where(row < info_ref[1] * SLOT_ROWS, value, 0.0).astype(BF)


def weave_body(length, info_ref, a_ref, b_ref, c_ref, d_ref, o_ref):
    def part(start, n, keep):
        x = jnp.concatenate([r[start : start + n, :] for r in (a_ref, b_ref, c_ref, d_ref)], axis=0)
        row = lax.broadcasted_iota(jnp.int32, (4 * n, 4 * n), 0)
        col = lax.broadcasted_iota(jnp.int32, (4 * n, 4 * n), 1)
        take = jnp.where(lax.bitwise_xor(row % 4, info_ref[0]) * n + row // 4 == col, 1.0, 0.0).astype(BF)
        y = dot(take, x).astype(BF).reshape(n, 4, x.shape[1])
        o_ref[0, start : start + keep] = y[:keep]

    full = length // 64 * 64
    for start in range(0, full, 64):
        part(start, 64, 64)
    part(full, 8, length - full)


def outer_steps(h_ref, dy_ref, du_ref, act_ref, t_ref, store):
    step = pl.program_id(0)
    half = pl.num_programs(0) // 2

    @pl.when(step == 0)
    def _():
        t_ref[...] = dy_ref[...].T

    @pl.when(step == half)
    def _():
        t_ref[...] = h_ref[...].T

    pl.when(step < half)(lambda: store(dot(t_ref[...], act_ref[...]).astype(BF)))
    pl.when(step >= half)(lambda: store(dot(t_ref[...], du_ref[...]).astype(BF)))


def outer_body(h_ref, dy_ref, du_ref, act_ref, g_ref, t_ref):
    parts, _, sub, cols = g_ref.shape

    def store(g):
        g_ref[:, 0] = g.reshape(parts, sub, cols)

    outer_steps(h_ref, dy_ref, du_ref, act_ref, t_ref, store)


def outer_halves_body(info_ref, h_ref, dy_ref, du_ref, act_ref, *refs):
    halves, t_ref, buf_ref = refs[:-2], refs[-2], refs[-1]

    def store(g):
        buf_ref[...] = g
        for n, ref in enumerate(halves):
            sub = ref.shape[1]
            ref[0] = buf_ref[pl.ds(pl.multiple_of(info_ref[2 + n] * sub, sub), sub), :]

    outer_steps(h_ref, dy_ref, du_ref, act_ref, t_ref, store)


def dact_body(info_ref, dy_ref, slope_ref, *refs):
    du_ref, sum_ref, buf_ref = refs[-3:]
    place(info_ref, refs[:-3], buf_ref)
    w = buf_ref[...]
    cols = w.shape[1]
    total = jnp.zeros((1, cols), F32)
    for i in range(ROWS // 256):
        rows = slice(i * 256, (i + 1) * 256)
        du = (dot(dy_ref[rows, :], w) * slope_ref[rows, :].astype(F32)).astype(BF)
        du_ref[rows, :] = du
        total = total + colsum(du.astype(F32))
    sum_ref[...] = jnp.broadcast_to(total, sum_ref.shape)


def add_rows(sums_ref, rows):
    @pl.when(pl.program_id(0) == 0)
    def _():
        sums_ref[...] = jnp.zeros_like(sums_ref)

    for n, value in enumerate(rows):
        sums_ref[n : n + 1, :] += colsum(value)


def mid_back_body(info_ref, dy_ref, du_ref, mid_ref, gain_ref, *refs):
    dmid_ref, dlow_ref, sums_ref, buf_ref = refs[-4:]
    dh = wide_dot(info_ref, du_ref, refs[:-4], buf_ref)
    normal, scale_inv = norm_stats(mid_ref[...])
    dy = dy_ref[...].astype(F32)
    dmid = dy + norm_back(dh, normal, scale_inv, gain_ref[...])
    dmid_ref[...] = dmid
    dlow_ref[...] = dmid.astype(BF)
    add_rows(sums_ref, (dh * normal, dh, dmid, dy))


def out_back_body(dlow_ref, wo_ref, do_ref):
    do_ref[...] = dot(dlow_ref[...], wo_ref[...]).astype(BF)


def attend_back_body(slots, q_ref, k_ref, v_ref, p_ref, do_ref, *refs):
    dq_ref, dk_ref, dv_ref, dp_ref, ds_ref = refs[-5:]
    masks = half_masks()
    rows = [slice(i * SLOT_ROWS, (i + 1) * SLOT_ROWS) for i in range(slots)]

    def upstream(i):
        v = v_ref[rows[i], :]
        do = do_ref[rows[i], :]
        for h in range(2):
            dp_ref[h, i] = dot(jnp.where(masks[h], v, jnp.zeros_like(v)), do, NT)
        dv = [dot(p_ref[h, i], do) for h in range(2)]
        dv_ref[rows[i], :] = jnp.where(masks[0], *dv).astype(BF)

    def softmax_back(i):
        for h in range(2):
            p = p_ref[h, i].astype(F32)
            dp = dp_ref[h, i]
            ds_ref[h, i] = (p * (dp - jnp.sum(p * dp, axis=0, keepdims=True))).astype(BF)

    def downstream(i):
        q = q_ref[rows[i], :] * jnp.bfloat16(0.125)
        k_t = (k_ref[rows[i], :] * jnp.bfloat16(0.125)).T
        dk = [dot(ds_ref[h, i], q) for h in range(2)]
        dk_ref[rows[i], :] = jnp.where(masks[0], *dk).astype(BF)
        dq = [dot(k_t[h * HEAD_DIM : (h + 1) * HEAD_DIM], ds_ref[h, i]) for h in range(2)]
        dq_ref[rows[i], :] = jnp.concatenate(dq, axis=0).T.astype(BF)

    for i in range(slots):
        upstream(i)
    for i in range(slots):
        softmax_back(i)
    for i in range(slots):
        downstream(i)
    tail = slots * SLOT_ROWS
    for ref in (dq_ref, dk_ref, dv_ref):
        ref[tail:, :] = jnp.zeros((ROWS - tail, 2 * HEAD_DIM), BF)


def small_outer(h_ref, dq_ref, dk_ref, dv_ref, dlow_ref, o_ref, sums_ref, store):
    ht = h_ref[...].T
    for s, ref in enumerate((dq_ref, dk_ref, dv_ref)):
        store(s, dot(ht, ref[...]).astype(BF))
        if s != 1:
            n = 0 if s == 0 else 1
            sums_ref[n : n + 1, :] = colsum(ref[...].astype(F32))
    store(3, dot(dlow_ref[...].T, o_ref[...]).astype(BF))


def outer_ring_body(info_ref, h_ref, dq_ref, dk_ref, dv_ref, dlow_ref, o_ref, *refs):
    halves, sums_ref, buf_ref = refs[:-2], refs[-2], refs[-1]
    groups = buf_ref.shape[0]
    local = h_ref.shape[1] // groups

    def store(s, g):
        for j in range(groups):
            buf_ref[j, :, s * local : (s + 1) * local] = g[:, j * local : (j + 1) * local]

    small_outer(h_ref, dq_ref, dk_ref, dv_ref, dlow_ref, o_ref, sums_ref, store)
    for n, ref in enumerate(halves):
        sub = ref.shape[1]
        rows = pl.ds(pl.multiple_of(info_ref[2 + n] * sub, sub), sub)
        for j in range(groups):
            ref[j] = buf_ref[j, rows, :]


def outer_plain_body(h_ref, dq_ref, dk_ref, dv_ref, dlow_ref, o_ref, g_ref, sums_ref):
    parts, groups, sub, cols = g_ref.shape
    local = cols // 4

    def store(s, g):
        for j in range(groups):
            g_ref[:, j, :, s * local : (s + 1) * local] = g[:, j * local : (j + 1) * local].reshape(parts, sub, local)

    small_outer(h_ref, dq_ref, dk_ref, dv_ref, dlow_ref, o_ref, sums_ref, store)


def input_back_body(x_ref, dq_ref, dk_ref, dv_ref, wq_ref, dmid_ref, gain_ref, out_ref, sums_ref):
    width = x_ref.shape[1]
    dh = sum(
        dot(ref[...], wq_ref[:, s * width : (s + 1) * width], NT) for s, ref in enumerate((dq_ref, dk_ref, dv_ref))
    )
    normal, scale_inv = norm_stats(x_ref[...].astype(F32))
    out_ref[...] = (dmid_ref[...] + norm_back(dh, normal, scale_inv, gain_ref[...])).astype(BF)
    add_rows(sums_ref, (dh * normal, dh))


def block_step(
    inputs, cotangent, counts, norm_gain, norm_shift, qkv_weight, query_bias, value_bias,
    out_weight, out_bias, mlp_gain, mlp_shift, hidden_weight, hidden_bias, down_weight, down_bias,
):
    _, slots, length, width = inputs.shape
    sub = qkv_weight.shape[0]
    local = qkv_weight.shape[1] // 3
    units = hidden_weight.shape[1]
    parts, groups = width // sub, width // local
    ff = units * groups
    axes = ("dp", "mp")
    mine = lax.axis_index("mp")
    ring = sub % 32 == 0

    cycle = list(range(0, parts, 2)) + list(range(parts - 1, 0, -2))
    place = [cycle.index(d) for d in range(parts)]
    here = jnp.array(place, jnp.int32)[lax.axis_index("dp")]
    owner = jnp.array(cycle, jnp.int32)
    far = parts // 2
    mp_swap = lambda a, bit: lax.ppermute(a, "mp", [(j, j ^ bit) for j in range(groups)])
    dp_swap = lambda a, bit: lax.ppermute(a, "dp", [(d, d ^ bit) for d in range(parts)])

    def hop(a, odd=True):
        pairs = []
        for p in range(parts):
            for j in range(groups):
                if j % 2 == 0:
                    pairs.append((cycle[p] * groups + j, cycle[(p + 1) % parts] * groups + j))
                elif odd:
                    pairs.append((cycle[p] * groups + j, cycle[(p - 1) % parts] * groups + j))
        return lax.ppermute(a, axes, pairs)

    even = mine % 2 == 0
    row = lambda v: v.reshape(1, -1)
    live = lax.dynamic_index_in_dim(counts, mine, 0, keepdims=False)[0]

    def info_of(offsets):
        return jnp.concatenate([jnp.stack([mine, live]), owner[(here + jnp.stack(offsets)) % parts]])

    smem = pl.BlockSpec(memory_space=pltpu.SMEM)
    info = jnp.stack([mine, live])

    mm = 2 * ROWS * width * width
    t_bf = lambda n: sds((ROWS, n), BF)
    t_f = lambda n: sds((ROWS, n), F32)
    block = lambda shape: pl.BlockSpec(shape, lambda i, info: (0,) * len(shape))
    mine_block = pl.BlockSpec((1, slots, length, width), lambda i, info: (info[0], 0, 0, 0))

    def prep(array, count):
        return pl.pallas_call(
            prep_body,
            out_shape=t_bf(width),
            grid_spec=pltpu.PrefetchScalarGridSpec(
                num_scalar_prefetch=1, grid=(1,), in_specs=[mine_block], out_specs=block((ROWS, width))
            ),
            compiler_params=pltpu.CompilerParams(vmem_limit_bytes=24 * 1024 * 1024),
            cost_estimate=pl.CostEstimate(flops=0, bytes_accessed=4 * ROWS * width, transcendentals=0),
        )(jnp.stack([mine, count]), array)

    x = prep(inputs, jnp.int32(slots))
    dy = prep(cotangent, live)

    def scatter_ring(halves):
        got = [mp_swap(halves[far], 1)]
        got += [mp_swap(send, 1) for send in halves[far + 1 :]]

        def term(n):
            return halves[n].astype(F32) + got[n].astype(F32)

        total = term(0)
        for k in range(1, far):
            moved = hop(total.astype(BF))
            total = term(k) + moved.astype(F32)
        total = total.astype(BF)
        last = hop(total, False)
        total = jnp.where(even, last, total).reshape(2, 2, sub, -1)
        split = lambda a, b, first: (jnp.where(first, a, b), jnp.where(first, b, a))
        mine_half, other_half = split(total[:, 0], total[:, 1], even)
        other_half = mp_swap(other_half, 1)
        total = mine_half.astype(F32) + other_half.astype(F32)
        mine_half, other_half = split(total[0], total[1], mine < 2)
        other_half = mp_swap(other_half.astype(BF), 2)
        return lax.optimization_barrier(mine_half + other_half.astype(F32))

    leave = [jnp.where(even, far - k, k + 1 - far) for k in range(far)]
    stay = [jnp.where(even, k + 1 - far, far - k) for k in range(far)]
    halves = lambda n: [sds((groups, sub, n), BF)] * (2 * far)

    shard_bc = jnp.concatenate([hidden_weight, down_weight.T], axis=1)
    shard_a = jnp.concatenate([qkv_weight, out_weight.T], axis=1)
    vectors = jnp.concatenate([query_bias, value_bias, hidden_bias])

    def chip_chunk(shard):
        two = jnp.stack([shard, mp_swap(shard, 2)])
        near = mp_swap(two, 1)
        rel = [two[0], near[0], two[1], near[1]]
        rel = [jnp.where(even, rel[j], rel[j ^ 1]) for j in range(groups)]
        return jnp.stack([jnp.where(mine < 2, rel[j], rel[j ^ 2]) for j in range(groups)])

    def gather_ring(start, between):
        chunks, held = [start], start
        for k in range(1, far):
            held = hop(held)
            held = between(k, held)
            chunks += [held, mp_swap(held, 1)]
        half = hop(jnp.where(even, held[: groups // 2], held[groups // 2 :]))
        other = mp_swap(half, 1)
        first, second = jnp.where(even, half, other), jnp.where(even, other, half)
        return chunks + [jnp.concatenate([first, second])], half

    if ring:
        side = jnp.where(even, 1, -1)
        offsets = [jnp.int32(0)]
        for k in range(1, far):
            offsets += [-k * side, k * side]
        ring_info = info_of(offsets + [jnp.int32(far)])
        start_bc = chip_chunk(shard_bc)
        prepared = [x]

        def between(k, held):
            if k == 1:
                held, prepared[0] = lax.optimization_barrier((held, prepared[0]))
            return held

        chunks, last = gather_ring(chip_chunk(shard_a), between)
        (x,) = prepared
        start_bc, last = lax.optimization_barrier((start_bc, last))
        bc, _ = gather_ring(start_bc, lambda k, held: held)
        piece = lambda n: [pl.BlockSpec((groups, sub, units), lambda i: (0, 0, n))] * len(bc)
        wcols = lambda n: [pl.BlockSpec((1, sub, units), lambda i: (i, 0, n))] * len(bc)
    else:
        ring_info = info
        wa = lax.all_gather(shard_a, axes, axis=0, tiled=False).reshape(parts, groups, sub, 4 * local)
        bc = [lax.all_gather(shard_bc, axes, axis=0, tiled=False).reshape(parts, groups, sub, 2 * units)]
        piece = lambda n: [pl.BlockSpec((parts, groups, sub, units), lambda i: (0, 0, 0, n))]
        wcols = lambda n: [pl.BlockSpec((parts, 1, sub, units), lambda i: (0, i, 0, n))]
    two = jnp.stack([vectors, mp_swap(vectors, 1)])
    four = jnp.concatenate([two, mp_swap(two, 2)])
    biases = four[jnp.arange(groups) ^ mine]
    qb, vb, hb = (biases[:, a:b].reshape(-1) for a, b in ((0, local), (local, 2 * local), (2 * local, None)))
    bias_row = row(jnp.concatenate([qb, jnp.zeros_like(qb), vb]))

    third = lambda n: pl.BlockSpec((n, width), lambda i: (0, i))
    chunks = chunks if ring else [wa]
    h1, qkv, wq, wo = call(
        qkv_body,
        [t_bf(width), t_bf(3 * width), sds((width, 3 * width), BF), sds((width, width), BF)],
        [ring_info, x, row(norm_gain), row(norm_shift), bias_row] + chunks,
        [smem, None, None, None, third(1)] + [None] * len(chunks),
        [None, third(ROWS), third(width), None],
        (3,),
        flops=3 * mm,
    )
    pair = 2 * HEAD_DIM
    pairs = width // pair
    head = lambda s: pl.BlockSpec((ROWS, pair), lambda i: (0, s * pairs + i))
    p_spec = pl.BlockSpec((2, slots, SLOT_ROWS, SLOT_ROWS), lambda i: (i, 0, 0, 0))
    p_shape = sds((2 * pairs, slots, SLOT_ROWS, SLOT_ROWS), BF)
    mixed, probs = call(
        functools.partial(attend_body, slots, length),
        [t_bf(width), p_shape],
        [qkv, qkv, qkv],
        [head(0), head(1), head(2)],
        [head(0), p_spec],
        (pairs,),
        scratch=[pltpu.VMEM((2, slots, SLOT_ROWS, SLOT_ROWS), F32)],
        flops=mm,
    )
    rows256 = pl.BlockSpec((256, width), lambda i: (i, 0))
    middle, h2 = call(
        mix_body,
        [t_f(width), t_bf(width)],
        [x, mixed, wo, row(out_bias), row(mlp_gain), row(mlp_shift)],
        [rows256, rows256, None, None, None, None],
        [rows256, rows256],
        (ROWS // 256,),
        flops=mm,
    )
    tcols = pl.BlockSpec((ROWS, units), lambda i: (0, i))
    vcols = lambda n: pl.BlockSpec((n, units), lambda i: (0, i))
    group_buf = lambda n: pltpu.VMEM((n, width, units), BF)
    act, slope = call(
        hidden_body,
        [t_bf(ff), t_bf(ff)],
        [ring_info, h2, row(hb)] + bc,
        [smem, None, vcols(1)] + wcols(0),
        [tcols, tcols],
        (groups,),
        scratch=[pltpu.VMEM((width, units), BF)],
        flops=4 * mm,
    )
    du, sum_hidden = call(
        dact_body,
        [t_bf(ff), sds((8, ff), F32)],
        [ring_info, dy, slope] + bc,
        [smem, None, tcols] + wcols(1),
        [tcols, vcols(8)],
        (groups,),
        scratch=[pltpu.VMEM((width, units), BF)],
        flops=4 * mm,
    )
    outer_in_specs = [
        None,
        None,
        pl.BlockSpec((ROWS, units), lambda i: (0, jnp.maximum(i - groups, 0))),
        pl.BlockSpec((ROWS, units), lambda i: (0, jnp.minimum(i, groups - 1))),
    ]
    outer_map = lambda i: (0, i % groups, 0, jnp.where(i < groups, 1, 0))
    transposed = pltpu.VMEM((width, ROWS), BF)
    if ring:
        halves_bc = call(
            outer_halves_body,
            halves(2 * units),
            [info_of(leave + stay), h2, dy, du, act],
            [smem] + outer_in_specs,
            [pl.BlockSpec((1, sub, units), lambda i: outer_map(i)[1:])] * (2 * far),
            (2 * groups,),
            scratch=[transposed, pltpu.VMEM((width, units), BF)],
            flops=8 * mm,
        )
        s_bc = scatter_ring(halves_bc)
        g_bc = halves_bc[0]
    else:
        (g_bc,) = call(
            outer_body,
            [sds((parts, groups, sub, 2 * units), BF)],
            [h2, dy, du, act],
            outer_in_specs,
            [pl.BlockSpec((parts, 1, sub, units), outer_map)],
            (2 * groups,),
            scratch=[transposed],
            flops=8 * mm,
        )
        s_bc = lax.psum_scatter(
            g_bc.reshape(parts * groups, sub, 2 * units), axes, scatter_dimension=0, tiled=False
        ).astype(F32)

    own_shape = sds((slots * SLOT_ROWS, width), BF)

    def spread(own):
        crossed = mp_swap(own, 2)
        near = mp_swap(own, 1)
        far_core = mp_swap(crossed, 1)
        image = pl.BlockSpec((SLOT_ROWS, width), lambda i: (i, 0))
        (woven,) = call(
            functools.partial(weave_body, length),
            [sds((slots, length, groups, width), BF)],
            [info, own, near, crossed, far_core],
            [smem] + [image] * 4,
            [pl.BlockSpec((1, length, groups, width), lambda i: (i, 0, 0, 0))],
            (slots,),
            flops=mm,
            limit=24,
        )
        return woven.transpose(2, 0, 1, 3)

    down_info = jnp.concatenate([info, ring_info[2:]])
    act_late, _ = lax.optimization_barrier((act, g_bc))
    wide256 = pl.BlockSpec((256, ff), lambda i: (i, 0))
    (own_out,) = call(
        down_body,
        [own_shape],
        [down_info, act_late, middle, row(down_bias)] + bc,
        [smem, wide256, rows256, None] + piece(1),
        [rows256],
        (ROWS // 256,),
        scratch=[group_buf(groups)],
        flops=4 * mm,
    )
    all_out = spread(own_out)
    du, _ = lax.optimization_barrier((du, own_out))

    dmid, dlow, sums_mid = call(
        mid_back_body,
        [t_f(width), t_bf(width), sds((8, width), F32)],
        [ring_info, dy, du, middle, row(mlp_gain)] + bc,
        [smem, rows256, wide256, rows256, None] + piece(0),
        [rows256, rows256, None],
        (ROWS // 256,),
        scratch=[group_buf(groups)],
        flops=4 * mm,
    )
    (do,) = call(out_back_body, [t_bf(width)], [dlow, wo], flops=mm)
    dq, dk, dv = call(
        functools.partial(attend_back_body, slots),
        [t_bf(width)] * 3,
        [qkv, qkv, qkv, probs, do],
        [head(0), head(1), head(2), p_spec, head(0)],
        [head(0)] * 3,
        (pairs,),
        scratch=[pltpu.VMEM((2, slots, SLOT_ROWS, SLOT_ROWS), dtype) for dtype in (F32, BF)],
        flops=2 * mm,
    )
    outer_ins = [h1, dq, dk, dv, dlow, mixed]
    sum_shape = sds((8, width), F32)
    if ring:
        *halves_a, sums_qkv = call(
            outer_ring_body,
            halves(4 * local) + [sum_shape],
            [info_of(leave + stay)] + outer_ins,
            [smem] + [None] * len(outer_ins),
            scratch=[pltpu.VMEM((groups, width, 4 * local), BF)],
            flops=4 * mm,
        )
        s_a = scatter_ring(halves_a)
    else:
        g_a, sums_qkv = call(
            outer_plain_body, [sds((parts, groups, sub, 4 * local), BF), sum_shape], outer_ins, flops=4 * mm
        )
        s_a = lax.psum_scatter(
            g_a.reshape(parts * groups, sub, 4 * local), axes, scatter_dimension=0, tiled=False
        ).astype(F32)
    own_grad, sums_in = call(
        input_back_body,
        [own_shape, sum_shape],
        [x, dq, dk, dv, wq, dmid, row(norm_gain)],
        [rows256] * 4 + [None, rows256, None],
        [rows256, None],
        (ROWS // 256,),
        flops=3 * mm,
    )

    sums = jnp.concatenate(
        [sums_in[:2].reshape(-1), sums_mid[:4].reshape(-1), sums_qkv[:2].reshape(-1), sum_hidden[0]]
    )
    all_grad = spread(own_grad)
    steps = [(mp_swap, 1)] + [(dp_swap, 1 << n) for n in range(parts.bit_length() - 1)] + [(mp_swap, 2)]
    for swap, bit in steps:
        other = swap(sums, bit)
        sums = sums + other
    vec = [sums[n * width : (n + 1) * width] for n in range(8)]
    own = lambda v, n: lax.dynamic_slice_in_dim(v, mine * n, n, 0)
    return (
        all_out,
        all_grad,
        vec[0],
        vec[1],
        s_a[:, : 3 * local],
        own(vec[6], local),
        own(vec[7], local),
        s_a[:, 3 * local :].T,
        vec[4],
        vec[2],
        vec[3],
        s_bc[:, :units],
        own(sums[8 * width :], units),
        s_bc[:, units:].T,
        vec[5],
    )


def solution(mesh):
    token = P(None, "dp", None, None)
    weight, turned = P("dp", "mp"), P("mp", "dp")
    return jax.shard_map(
        block_step,
        mesh=mesh,
        in_specs=(token, token, P(None, "dp"), P(), P(), weight, P("mp"), P("mp"), turned)
        + (P(), P(), P(), weight, P("mp"), turned, P()),
        out_specs=(token, token, P(), P(), weight, P("mp"), P("mp"), turned)
        + (P(), P(), P(), weight, P("mp"), turned, P()),
        check_vma=False,
    )
```

```python
import functools
import jax
import jax.numpy as jnp
from jax import lax
from jax.experimental import pallas as pl
from jax.experimental.pallas import tpu as pltpu
from jax.sharding import PartitionSpec as P


HEAD_DIM = 64
NORM_EPS = 1e-06
SLOT_ROWS = 200
ROWS = 1024
BF = jnp.bfloat16
F32 = jnp.float32
NT = (((1,), (1,)), ((), ()))
NN = (((1,), (0,)), ((), ()))


def dot(a, b, dims=NN):
    return lax.dot_general(a, b, dims, preferred_element_type=F32)


def norm_stats(values):
    center = jnp.mean(values, axis=-1, keepdims=True)
    offset = values - center
    spread = jnp.mean(offset * offset, axis=-1, keepdims=True)
    scale_inv = lax.rsqrt(spread + NORM_EPS)
    return offset * scale_inv, scale_inv


def norm_back(upstream, normal, scale_inv, gain_vec):
    scaled = upstream * gain_vec
    return scale_inv * (
        scaled
        - jnp.mean(scaled, axis=-1, keepdims=True)
        - normal * jnp.mean(scaled * normal, axis=-1, keepdims=True)
    )


def colsum(values):
    return jnp.sum(values, axis=0, keepdims=True)


def call(body, outs, ins, in_specs=None, out_specs=None, grid=None, scratch=(), flops=0, nbytes=0, limit=60, **kw):
    full = lambda a: pl.BlockSpec(a.shape, (lambda *_: (0,) * len(a.shape)))
    if in_specs is None:
        in_specs = [None] * len(ins)
    if out_specs is None:
        out_specs = [None] * len(outs)
    in_specs = [full(a) if s is None else s for a, s in zip(ins, in_specs)]
    out_specs = [full(a) if s is None else s for a, s in zip(outs, out_specs)]
    nbytes = sum(a.size * a.dtype.itemsize for a in ins) + sum(a.size * a.dtype.itemsize for a in outs)
    return pl.pallas_call(
        body,
        out_shape=tuple(outs),
        grid=(1,) if grid is None else grid,
        in_specs=in_specs,
        out_specs=tuple(out_specs),
        scratch_shapes=list(scratch),
        compiler_params=pltpu.CompilerParams(vmem_limit_bytes=limit * 1024 * 1024),
        cost_estimate=pl.CostEstimate(flops=flops, bytes_accessed=nbytes, transcendentals=0),
        **kw,
    )(*ins)


def sds(shape, dtype):
    return jax.ShapeDtypeStruct(shape, dtype)


def loop(n, fn, unroll=1):
    lax.fori_loop(0, n, lambda i, c: (fn(i), c)[1], 0, unroll=unroll)


def cut(i, size):
    return pl.ds(pl.multiple_of(i * size, size), size)


def prep_body(info_ref, in_ref, out_ref):
    out_ref[...] = jnp.zeros_like(out_ref)
    _, slots, length, _ = in_ref.shape
    for i in range(slots):

        @pl.when(i < info_ref[1])
        def _():
            out_ref[i * SLOT_ROWS : i * SLOT_ROWS + length, :] = in_ref[0, i]


def place(info_ref, refs, dst_ref, group=0, cols=slice(None), into=slice(None)):
    if len(refs) == 1:
        parts, _, sub, _ = refs[0].shape
        dst_ref[:, into] = refs[0][:, group, :, cols].reshape(parts * sub, -1)
        return
    for n, ref in enumerate(refs):
        sub = ref.shape[1]
        rows = pl.ds(pl.multiple_of(info_ref[2 + n] * sub, sub), sub)
        dst_ref[rows, into] = ref[group, :, cols]


def qkv_body(info_ref, x_ref, gain_ref, shift_ref, bias_ref, *refs):
    h_ref, qkv_ref, wq_ref, wo_ref = refs[-4:]
    chunks = refs[:-4]
    width = x_ref.shape[1]
    groups = chunks[0].shape[0 if len(chunks) > 1 else 1]
    local = width // groups

    def columns(s, dst_ref):
        for j in range(groups):
            place(info_ref, chunks, dst_ref, j, slice(s * local, (s + 1) * local), slice(j * local, (j + 1) * local))

    step = pl.program_id(0)

    @pl.when(step == 0)
    def _():
        def norm(i):
            rows = cut(i, 128)
            normal, _ = norm_stats(x_ref[rows, :].astype(F32))
            h_ref[rows, :] = (normal * gain_ref[...] + shift_ref[...]).astype(BF)

        loop(ROWS // 128, norm, 2)
        columns(3, wo_ref)

    for s in range(3):
        pl.when(step == s)(functools.partial(columns, s, wq_ref))
    qkv_ref[...] = (dot(h_ref[...], wq_ref[...]) + bias_ref[...]).astype(BF)


def half_masks():
    low_half = lax.broadcasted_iota(jnp.int32, (SLOT_ROWS, 2 * HEAD_DIM), 1) < HEAD_DIM
    return low_half, ~low_half


def attend_body(slots, length, q_ref, k_ref, v_ref, o_ref, p_ref, s_ref):
    masks = half_masks()
    tile = length // 8 * 8
    valid = lax.broadcasted_iota(jnp.int32, (SLOT_ROWS - tile, SLOT_ROWS), 0) < length - tile
    rows = [slice(i * SLOT_ROWS, (i + 1) * SLOT_ROWS) for i in range(slots)]

    def scores(i):
        q = q_ref[rows[i], :] * jnp.bfloat16(0.125)
        k = k_ref[rows[i], :]
        for h in range(2):
            s_ref[h, i] = dot(jnp.where(masks[h], k, jnp.zeros_like(k)), q, NT)

    def softmax(i):
        for h in range(2):
            s_ref[h, i, tile:] = jnp.where(valid, s_ref[h, i, tile:], -1e30)
            s = s_ref[h, i]
            e = jnp.exp(s - jnp.max(s, axis=0, keepdims=True))
            p_ref[h, i] = (e * (1.0 / jnp.sum(e, axis=0, keepdims=True))).astype(BF)

    def mix(i):
        v_t = v_ref[rows[i], :].T
        mixed = [dot(v_t[h * HEAD_DIM : (h + 1) * HEAD_DIM], p_ref[h, i]) for h in range(2)]
        o_ref[rows[i], :] = jnp.concatenate(mixed, axis=0).T.astype(BF)

    for i in range(slots):
        scores(i)
    for i in range(slots):
        softmax(i)
    for i in range(slots):
        mix(i)
    tail = slots * SLOT_ROWS
    o_ref[tail:, :] = jnp.zeros((ROWS - tail, 2 * HEAD_DIM), BF)


def mix_body(x_ref, o_ref, wo_ref, bias_ref, gain_ref, shift_ref, mid_ref, h_ref):
    mid_ref[...] = dot(o_ref[...], wo_ref[...], NT)

    def norm(i):
        rows = cut(i, 128)
        mid = x_ref[rows, :].astype(F32) + (mid_ref[rows, :] + bias_ref[...])
        mid_ref[rows, :] = mid
        normal, _ = norm_stats(mid)
        h_ref[rows, :] = (normal * gain_ref[...] + shift_ref[...]).astype(BF)

    loop(mid_ref.shape[0] // 128, norm)


def hidden_body(n_chunks, info_ref, halves_ref, h_ref, bias_ref, dy_ref, *refs):
    chunks, outs = refs[:n_chunks], refs[n_chunks:-6]
    act_ref, du_ref, sum_ref, *grads = outs
    wb_ref, wc_ref, ht_ref, dyt_ref, gb_ref, gc_ref = refs[-6:]
    cols = wb_ref.shape[1]

    @pl.when(pl.program_id(0) == 0)
    def _():
        ht_ref[...] = h_ref[...].T
        dyt_ref[...] = dy_ref[...].T

    place(info_ref, chunks, wb_ref, 0, slice(0, cols))
    place(info_ref, chunks, wc_ref, 0, slice(cols, 2 * cols))
    total = jnp.zeros((1, cols), F32)
    for i in range(ROWS // 256):
        rows = slice(i * 256, (i + 1) * 256)
        u = dot(h_ref[rows, :], wb_ref[...]) + bias_ref[...]
        half = 0.5 * (1.0 + lax.erf(u * 0.7071067811865476))
        act_ref[rows, :] = (u * half).astype(BF)
        slope = half + u * jnp.exp(-0.5 * u * u) * 0.3989422804014327
        du = dot(dy_ref[rows, :], wc_ref[...]) * slope
        du_ref[rows, :] = du.astype(BF)
        total = total + colsum(du)
    sum_ref[...] = jnp.broadcast_to(total, sum_ref.shape)
    gc_ref[...] = dot(dyt_ref[...], act_ref[...]).astype(BF)
    gb_ref[...] = dot(ht_ref[...], du_ref[...]).astype(BF)
    for piece, g_ref in enumerate((gb_ref, gc_ref)):
        lanes = slice(piece * cols, (piece + 1) * cols)
        if len(grads) == 1:
            parts, _, sub, _ = grads[0].shape
            grads[0][:, 0, :, lanes] = g_ref[...].reshape(parts, sub, cols)
            continue
        for n, ref in enumerate(grads):
            sub = ref.shape[1]
            ref[0, :, lanes] = g_ref[pl.ds(pl.multiple_of(halves_ref[2 + n] * sub, sub), sub), :]


def wide_dot(info_ref, left_ref, refs, buf_ref):
    groups, _, cols = buf_ref.shape

    @pl.when(pl.program_id(0) == 0)
    def _():
        for j in range(groups):
            place(info_ref, refs, buf_ref.at[j], j)

    return sum(dot(left_ref[:, j * cols : (j + 1) * cols], buf_ref[j], NT) for j in range(groups))


def down_body(info_ref, act_ref, mid_ref, bias_ref, *refs):
    out_ref, buf_ref = refs[-2:]
    value = mid_ref[...] + wide_dot(info_ref, act_ref, refs[:-2], buf_ref) + bias_ref[...]
    rows = out_ref.shape[0]
    row = pl.program_id(0) * rows + lax.broadcasted_iota(jnp.int32, (rows, 1), 0)
    out_ref[...] = jnp.where(row < info_ref[1] * SLOT_ROWS, value, 0.0).astype(BF)


def weave_body(length, info_ref, a_ref, b_ref, c_ref, d_ref, *refs):
    o_ref = refs[-1]

    def part(start, n, keep):
        x = jnp.concatenate([r[start : start + n, :] for r in (a_ref, b_ref, c_ref, d_ref)], axis=0)
        row = lax.broadcasted_iota(jnp.int32, (4 * n, 4 * n), 0)
        col = lax.broadcasted_iota(jnp.int32, (4 * n, 4 * n), 1)
        take = jnp.where(lax.bitwise_xor(row % 4, info_ref[0]) * n + row // 4 == col, 1.0, 0.0).astype(BF)
        y = dot(take, x).astype(BF).reshape(n, 4, x.shape[1])
        o_ref[0, start : start + keep] = y[:keep]

    full = length // 64 * 64
    for start in range(0, full, 64):
        part(start, 64, 64)
    part(full, 8, length - full)


def add_rows(sums_ref, rows):
    @pl.when(pl.program_id(0) == 0)
    def _():
        sums_ref[...] = jnp.zeros_like(sums_ref)

    for n, value in enumerate(rows):
        sums_ref[n : n + 1, :] += colsum(value)


def mid_back_body(info_ref, dy_ref, du_ref, mid_ref, gain_ref, *refs):
    dmid_ref, dlow_ref, sums_ref, buf_ref = refs[-4:]
    dh = wide_dot(info_ref, du_ref, refs[:-4], buf_ref)
    normal, scale_inv = norm_stats(mid_ref[...])
    dy = dy_ref[...].astype(F32)
    dmid = dy + norm_back(dh, normal, scale_inv, gain_ref[...])
    dmid_ref[...] = dmid
    dlow_ref[...] = dmid.astype(BF)
    add_rows(sums_ref, (dh * normal, dh, dmid, dy))


def out_back_body(dlow_ref, wo_ref, do_ref):
    do_ref[...] = dot(dlow_ref[...], wo_ref[...]).astype(BF)


def attend_back_body(slots, q_ref, k_ref, v_ref, p_ref, do_ref, *refs):
    dq_ref, dk_ref, dv_ref, dp_ref, ds_ref = refs
    masks = half_masks()
    rows = [slice(i * SLOT_ROWS, (i + 1) * SLOT_ROWS) for i in range(slots)]

    def upstream(i):
        v = v_ref[rows[i], :]
        do = do_ref[rows[i], :]
        for h in range(2):
            dp_ref[h, i] = dot(jnp.where(masks[h], v, jnp.zeros_like(v)), do, NT)
        dv = [dot(p_ref[h, i], do) for h in range(2)]
        dv_ref[rows[i], :] = jnp.where(masks[0], *dv).astype(BF)

    def softmax_back(i):
        for h in range(2):
            p = p_ref[h, i].astype(F32)
            dp = dp_ref[h, i]
            ds_ref[h, i] = (p * (dp - jnp.sum(p * dp, axis=0, keepdims=True))).astype(BF)

    def downstream(i):
        q = q_ref[rows[i], :] * jnp.bfloat16(0.125)
        k_t = (k_ref[rows[i], :] * jnp.bfloat16(0.125)).T
        dk = [dot(ds_ref[h, i], q) for h in range(2)]
        dk_ref[rows[i], :] = jnp.where(masks[0], *dk).astype(BF)
        dq = [dot(k_t[h * HEAD_DIM : (h + 1) * HEAD_DIM], ds_ref[h, i]) for h in range(2)]
        dq_ref[rows[i], :] = jnp.concatenate(dq, axis=0).T.astype(BF)

    for i in range(slots):
        upstream(i)
    for i in range(slots):
        softmax_back(i)
    for i in range(slots):
        downstream(i)
    tail = slots * SLOT_ROWS
    for ref in (dq_ref, dk_ref, dv_ref):
        ref[tail:, :] = jnp.zeros((ROWS - tail, 2 * HEAD_DIM), BF)


def small_outer(h_ref, dq_ref, dk_ref, dv_ref, dlow_ref, o_ref, sums_ref, store):
    ht = h_ref[...].T
    for s, ref in enumerate((dq_ref, dk_ref, dv_ref)):
        store(s, dot(ht, ref[...]).astype(BF))
        if s != 1:
            n = 0 if s == 0 else 1
            sums_ref[n : n + 1, :] = colsum(ref[...].astype(F32))
    store(3, dot(dlow_ref[...].T, o_ref[...]).astype(BF))


def outer_ring_body(info_ref, h_ref, dq_ref, dk_ref, dv_ref, dlow_ref, o_ref, *refs):
    halves, sums_ref, buf_ref = refs[:-2], refs[-2], refs[-1]
    groups = buf_ref.shape[0]
    local = h_ref.shape[1] // groups

    def store(s, g):
        for j in range(groups):
            buf_ref[j, :, s * local : (s + 1) * local] = g[:, j * local : (j + 1) * local]

    small_outer(h_ref, dq_ref, dk_ref, dv_ref, dlow_ref, o_ref, sums_ref, store)
    for n, ref in enumerate(halves):
        sub = ref.shape[1]
        rows = pl.ds(pl.multiple_of(info_ref[2 + n] * sub, sub), sub)
        for j in range(groups):
            ref[j] = buf_ref[j, rows, :]


def outer_plain_body(h_ref, dq_ref, dk_ref, dv_ref, dlow_ref, o_ref, g_ref, sums_ref):
    parts, groups, sub, cols = g_ref.shape
    local = cols // 4

    def store(s, g):
        for j in range(groups):
            g_ref[:, j, :, s * local : (s + 1) * local] = g[:, j * local : (j + 1) * local].reshape(parts, sub, local)

    small_outer(h_ref, dq_ref, dk_ref, dv_ref, dlow_ref, o_ref, sums_ref, store)


def input_back_body(x_ref, dq_ref, dk_ref, dv_ref, wq_ref, dmid_ref, gain_ref, out_ref, sums_ref):
    width = x_ref.shape[1]
    dh = sum(
        dot(ref[...], wq_ref[:, s * width : (s + 1) * width], NT) for s, ref in enumerate((dq_ref, dk_ref, dv_ref))
    )
    normal, scale_inv = norm_stats(x_ref[...].astype(F32))
    out_ref[...] = (dmid_ref[...] + norm_back(dh, normal, scale_inv, gain_ref[...])).astype(BF)
    add_rows(sums_ref, (dh * normal, dh))


def block_step(
    inputs, cotangent, counts, norm_gain, norm_shift, qkv_weight, query_bias, value_bias,
    out_weight, out_bias, mlp_gain, mlp_shift, hidden_weight, hidden_bias, down_weight, down_bias,
):
    _, slots, length, width = inputs.shape
    sub = qkv_weight.shape[0]
    local = qkv_weight.shape[1] // 3
    units = hidden_weight.shape[1]
    parts, groups = width // sub, width // local
    ff = units * groups
    axes = ("dp", "mp")
    mine = lax.axis_index("mp")
    ring = sub % 32 == 0

    cycle = list(range(0, parts, 2)) + list(range(parts - 1, 0, -2))
    at = lax.axis_index("dp")
    here = jnp.where(at % 2 == 0, at // 2, parts - 1 - at // 2)
    far = parts // 2
    mp_swap = lambda a, bit: lax.ppermute(a, "mp", [(j, j ^ bit) for j in range(groups)])
    dp_swap = lambda a, bit: lax.ppermute(a, "dp", [(d, d ^ bit) for d in range(parts)])

    def hop(a, odd=True):
        pairs = []
        for p in range(parts):
            for j in range(groups):
                if j % 2 == 0:
                    pairs.append((cycle[p] * groups + j, cycle[(p + 1) % parts] * groups + j))
                elif odd:
                    pairs.append((cycle[p] * groups + j, cycle[(p - 1) % parts] * groups + j))
        return lax.ppermute(a, axes, pairs)

    even = mine % 2 == 0
    row = lambda v: v.reshape(1, -1)
    live = lax.dynamic_index_in_dim(counts, mine, 0, keepdims=False)[0]

    def info_of(offsets):
        spots = here + offsets + 2 * parts
        spots = spots - parts * (spots // parts)
        return jnp.concatenate([info, jnp.where(spots < far, 2 * spots, 2 * (parts - spots) - 1)])

    smem = pl.BlockSpec(memory_space=pltpu.SMEM)
    info = jnp.stack([mine, live])

    mm = 2 * ROWS * width * width
    t_bf = lambda n: sds((ROWS, n), BF)
    t_f = lambda n: sds((ROWS, n), F32)
    block = lambda shape: pl.BlockSpec(shape, lambda i, info: (0,) * len(shape))
    mine_block = pl.BlockSpec((1, slots, length, width), lambda i, info: (info[0], 0, 0, 0))

    def prep(array, count):
        return pl.pallas_call(
            prep_body,
            out_shape=t_bf(width),
            grid_spec=pltpu.PrefetchScalarGridSpec(
                num_scalar_prefetch=1, grid=(1,), in_specs=[mine_block], out_specs=block((ROWS, width))
            ),
            compiler_params=pltpu.CompilerParams(vmem_limit_bytes=24 * 1024 * 1024),
            cost_estimate=pl.CostEstimate(flops=0, bytes_accessed=4 * ROWS * width, transcendentals=0),
        )(jnp.stack([mine, count]), array)

    x = prep(inputs, jnp.int32(slots))
    dy = prep(cotangent, live)

    def scatter_ring(halves):
        got = [mp_swap(halves[far], 1)]
        got += [mp_swap(send, 1) for send in halves[far + 1 :]]

        def term(n):
            return halves[n].astype(F32) + got[n].astype(F32)

        total = term(0)
        for k in range(1, far):
            moved = hop(total.astype(BF))
            total = term(k) + moved.astype(F32)
        total = total.astype(BF)
        last = hop(total, False)
        total = jnp.where(even, last, total).reshape(2, 2, sub, -1)
        split = lambda a, b, first: (jnp.where(first, a, b), jnp.where(first, b, a))
        mine_half, other_half = split(total[:, 0], total[:, 1], even)
        other_half = mp_swap(other_half, 1)
        total = mine_half.astype(F32) + other_half.astype(F32)
        mine_half, other_half = split(total[0], total[1], mine < 2)
        other_half = mp_swap(other_half.astype(BF), 2)
        return lax.optimization_barrier(mine_half + other_half.astype(F32))

    to_right = jnp.arange(far, 0, -1, dtype=jnp.int32)
    to_left = jnp.arange(1 - far, 1, dtype=jnp.int32)
    halves_info = info_of(
        jnp.concatenate([jnp.where(even, to_right, to_left), jnp.where(even, to_left, to_right)])
    )
    halves = lambda n: [sds((groups, sub, n), BF)] * (2 * far)

    shard_bc = jnp.concatenate([hidden_weight, down_weight.T], axis=1)
    shard_a = jnp.concatenate([qkv_weight, out_weight.T], axis=1)
    vectors = jnp.concatenate([query_bias, value_bias, hidden_bias])

    def chip_chunk(shard):
        two = jnp.stack([shard, mp_swap(shard, 2)])
        near = mp_swap(two, 1)
        rel = [two[0], near[0], two[1], near[1]]
        rel = [jnp.where(even, rel[j], rel[j ^ 1]) for j in range(groups)]
        return jnp.stack([jnp.where(mine < 2, rel[j], rel[j ^ 2]) for j in range(groups)])

    def gather_ring(start, between):
        chunks, held = [start], start
        for k in range(1, far):
            held = hop(held)
            held = between(k, held)
            chunks += [held, mp_swap(held, 1)]
        half = hop(jnp.where(even, held[: groups // 2], held[groups // 2 :]))
        other = mp_swap(half, 1)
        first, second = jnp.where(even, half, other), jnp.where(even, other, half)
        return chunks + [jnp.concatenate([first, second])], half

    biases = chip_chunk(row(vectors))[:, 0]
    qb, vb, hb = (biases[:, a:b].reshape(-1) for a, b in ((0, local), (local, 2 * local), (2 * local, None)))
    bias_row = row(jnp.concatenate([qb, jnp.zeros_like(qb), vb]))

    if ring:
        offsets = [0]
        for k in range(1, far):
            offsets += [-k, k]
        ring_info = info_of(jnp.array(offsets + [far], jnp.int32) * jnp.where(even, 1, -1))
        start_bc = chip_chunk(shard_bc)
        prepared = [x, (start_bc, bias_row)]

        def between(k, held):
            if k <= 2:
                held, prepared[k - 1] = lax.optimization_barrier((held, prepared[k - 1]))
            return held

        chunks, _ = gather_ring(chip_chunk(shard_a), between)
        x, (start_bc, bias_row) = prepared
        bc, _ = gather_ring(start_bc, lambda k, held: held)
        piece = lambda n: [pl.BlockSpec((groups, sub, units), lambda i: (0, 0, n))] * len(bc)
    else:
        ring_info = info
        wa = lax.all_gather(shard_a, axes, axis=0, tiled=False).reshape(parts, groups, sub, 4 * local)
        bc = [lax.all_gather(shard_bc, axes, axis=0, tiled=False).reshape(parts, groups, sub, 2 * units)]
        piece = lambda n: [pl.BlockSpec((parts, groups, sub, units), lambda i: (0, 0, 0, n))]
    third = lambda n: pl.BlockSpec((n, width), lambda i: (0, i))
    chunks = chunks if ring else [wa]
    h1, qkv, wq, wo = call(
        qkv_body,
        [t_bf(width), t_bf(3 * width), sds((width, 3 * width), BF), sds((width, width), BF)],
        [ring_info, x, row(norm_gain), row(norm_shift), bias_row] + chunks,
        [smem, None, None, None, third(1)] + [None] * len(chunks),
        [None, third(ROWS), third(width), None],
        (3,),
        flops=3 * mm,
    )
    pair = 2 * HEAD_DIM
    pairs = width // pair
    head = lambda s: pl.BlockSpec((ROWS, pair), lambda i: (0, s * pairs + i))
    p_spec = pl.BlockSpec((2, slots, SLOT_ROWS, SLOT_ROWS), lambda i: (i, 0, 0, 0))
    p_shape = sds((2 * pairs, slots, SLOT_ROWS, SLOT_ROWS), BF)
    mixed, probs = call(
        functools.partial(attend_body, slots, length),
        [t_bf(width), p_shape],
        [qkv, qkv, qkv],
        [head(0), head(1), head(2)],
        [head(0), p_spec],
        (pairs,),
        scratch=[pltpu.VMEM((2, slots, SLOT_ROWS, SLOT_ROWS), F32)],
        flops=mm,
    )
    rows256 = pl.BlockSpec((256, width), lambda i: (i, 0))
    middle, h2 = call(
        mix_body,
        [t_f(width), t_bf(width)],
        [x, mixed, wo, row(out_bias), row(mlp_gain), row(mlp_shift)],
        [rows256, rows256, None, None, None, None],
        [rows256, rows256],
        (ROWS // 256,),
        flops=mm,
    )
    tcols = pl.BlockSpec((ROWS, units), lambda i: (0, i))
    vcols = lambda n: pl.BlockSpec((n, units), lambda i: (0, i))
    group_buf = lambda n: pltpu.VMEM((n, width, units), BF)
    both = [
        pl.BlockSpec((1, sub, 2 * units), lambda i: (i, 0, 0))
        if ring
        else pl.BlockSpec((parts, 1, sub, 2 * units), lambda i: (0, i, 0, 0))
    ]
    grad_shapes = halves(2 * units) if ring else [sds((parts, groups, sub, 2 * units), BF)]
    act, du, sum_hidden, *halves_bc = call(
        functools.partial(hidden_body, len(bc)),
        [t_bf(ff), t_bf(ff), sds((8, ff), F32)] + grad_shapes,
        [ring_info, halves_info if ring else info, h2, row(hb), dy] + bc,
        [smem, smem, None, vcols(1), None] + both * len(bc),
        [tcols, tcols, vcols(8)] + both * len(grad_shapes),
        (groups,),
        scratch=[pltpu.VMEM((width, units), BF)] * 2
        + [pltpu.VMEM((width, ROWS), BF)] * 2
        + [pltpu.VMEM((width, units), BF)] * 2,
        flops=16 * mm,
    )
    g_bc = halves_bc[0]
    if ring:
        s_bc = scatter_ring(halves_bc)
    else:
        s_bc = lax.psum_scatter(
            g_bc.reshape(parts * groups, sub, 2 * units), axes, scatter_dimension=0, tiled=False
        ).astype(F32)

    own_shape = sds((slots * SLOT_ROWS, width), BF)

    def cross(own):
        crossed = mp_swap(own, 2)
        near = mp_swap(own, 1)
        return [own, near, crossed, mp_swap(crossed, 1)]

    def weave(parts_of, first, woven=()):
        image = pl.BlockSpec((SLOT_ROWS, width), lambda i: (i, 0))
        (woven,) = call(
            functools.partial(weave_body, length),
            [sds((slots, length, groups, width), BF)],
            [info, *parts_of, *woven],
            [smem] + [image] * 4 + [pl.BlockSpec(memory_space=pl.ANY)] * len(woven),
            [pl.BlockSpec((1, length, groups, width), lambda i: (first + i, 0, 0, 0))],
            (parts_of[0].shape[0] // SLOT_ROWS,),
            flops=mm,
            limit=24,
            input_output_aliases={5: 0} if woven else {},
        )
        return woven

    down_info = jnp.concatenate([info, ring_info[2:]])
    act_late, _ = lax.optimization_barrier((act, g_bc))
    wide256 = pl.BlockSpec((256, ff), lambda i: (i, 0))
    (own_out,) = call(
        down_body,
        [own_shape],
        [down_info, act_late, middle, row(down_bias)] + bc,
        [smem, wide256, rows256, None] + piece(1),
        [rows256],
        (ROWS // 256,),
        scratch=[group_buf(groups)],
        flops=4 * mm,
    )
    all_out = weave(cross(own_out), 0).transpose(2, 0, 1, 3)
    du, _ = lax.optimization_barrier((du, own_out))

    dmid, dlow, sums_mid = call(
        mid_back_body,
        [t_f(width), t_bf(width), sds((8, width), F32)],
        [ring_info, dy, du, middle, row(mlp_gain)] + bc,
        [smem, rows256, wide256, rows256, None] + piece(0),
        [rows256, rows256, None],
        (ROWS // 256,),
        scratch=[group_buf(groups)],
        flops=4 * mm,
    )
    (do,) = call(out_back_body, [t_bf(width)], [dlow, wo], flops=mm)
    dq, dk, dv = call(
        functools.partial(attend_back_body, slots),
        [t_bf(width)] * 3,
        [qkv, qkv, qkv, probs, do],
        [head(0), head(1), head(2), p_spec, head(0)],
        [head(0)] * 3,
        (pairs,),
        scratch=[pltpu.VMEM((2, slots, SLOT_ROWS, SLOT_ROWS), dtype) for dtype in (F32, BF)],
        flops=2 * mm,
    )
    outer_ins = [h1, dq, dk, dv, dlow, mixed]
    sum_shape = sds((8, width), F32)
    if ring:
        *halves_a, sums_qkv = call(
            outer_ring_body,
            halves(4 * local) + [sum_shape],
            [halves_info] + outer_ins,
            [smem] + [None] * len(outer_ins),
            scratch=[pltpu.VMEM((groups, width, 4 * local), BF)],
            flops=4 * mm,
        )
        s_a = scatter_ring(halves_a)
    else:
        g_a, sums_qkv = call(
            outer_plain_body, [sds((parts, groups, sub, 4 * local), BF), sum_shape], outer_ins, flops=4 * mm
        )
        s_a = lax.psum_scatter(
            g_a.reshape(parts * groups, sub, 4 * local), axes, scatter_dimension=0, tiled=False
        ).astype(F32)
    grad_parts, sums_in = [], 0.0
    for first, count in ((0, slots - slots // 2), (slots - slots // 2, slots // 2)):
        rows = count * SLOT_ROWS
        image = pl.BlockSpec(
            (pl.Element(rows), pl.Element(width)), lambda i, first=first: (first * SLOT_ROWS, 0)
        )
        own_grad, sums_part = call(
            input_back_body,
            [sds((rows, width), BF), sum_shape],
            [x, dq, dk, dv, wq, dmid, row(norm_gain)],
            [image] * 4 + [None, image, None],
            [None, None],
            (1,),
            flops=3 * mm * count // slots,
        )
        grad_parts.append((cross(own_grad), first))
        sums_in = sums_in + sums_part[:2]

    sums = jnp.concatenate(
        [sums_in.reshape(-1), sums_mid[:4].reshape(-1), sums_qkv[:2].reshape(-1), sum_hidden[0]]
    )
    woven = ()
    for parts_of, first in grad_parts:
        woven = (weave(parts_of, first, woven),)
    all_grad = woven[0].transpose(2, 0, 1, 3)
    steps = [(mp_swap, 1)] + [(dp_swap, 1 << n) for n in range(parts.bit_length() - 1)] + [(mp_swap, 2)]
    for swap, bit in steps:
        other = swap(sums, bit)
        sums = sums + other
    vec = [sums[n * width : (n + 1) * width] for n in range(8)]
    own = lambda v, n: lax.dynamic_slice_in_dim(v, mine * n, n, 0)
    return (
        all_out,
        all_grad,
        vec[0],
        vec[1],
        s_a[:, : 3 * local],
        own(vec[6], local),
        own(vec[7], local),
        s_a[:, 3 * local :].T,
        vec[4],
        vec[2],
        vec[3],
        s_bc[:, :units],
        own(sums[8 * width :], units),
        s_bc[:, units:].T,
        vec[5],
    )


def solution(mesh):
    token = P(None, "dp", None, None)
    weight, turned = P("dp", "mp"), P("mp", "dp")
    return jax.shard_map(
        block_step,
        mesh=mesh,
        in_specs=(token, token, P(None, "dp"), P(), P(), weight, P("mp"), P("mp"), turned)
        + (P(), P(), P(), weight, P("mp"), turned, P()),
        out_specs=(token, token, P(), P(), weight, P("mp"), P("mp"), turned)
        + (P(), P(), P(), weight, P("mp"), turned, P()),
        check_vma=False,
    )
```

```python
import functools
import jax
import jax.numpy as jnp
from jax import lax
from jax.experimental import pallas as pl
from jax.experimental.pallas import tpu as pltpu
from jax.sharding import PartitionSpec as P


HEAD_DIM = 64
NORM_EPS = 1e-06
SLOT_ROWS = 200
ROWS = 1024
BF = jnp.bfloat16
F32 = jnp.float32
NT = (((1,), (1,)), ((), ()))
NN = (((1,), (0,)), ((), ()))


def dot(a, b, dims=NN):
    return lax.dot_general(a, b, dims, preferred_element_type=F32)


def norm_stats(values):
    center = jnp.mean(values, axis=-1, keepdims=True)
    offset = values - center
    spread = jnp.mean(offset * offset, axis=-1, keepdims=True)
    scale_inv = lax.rsqrt(spread + NORM_EPS)
    return offset * scale_inv, scale_inv


def norm_back(upstream, normal, scale_inv, gain_vec):
    scaled = upstream * gain_vec
    return scale_inv * (
        scaled
        - jnp.mean(scaled, axis=-1, keepdims=True)
        - normal * jnp.mean(scaled * normal, axis=-1, keepdims=True)
    )


def colsum(values):
    return jnp.sum(values, axis=0, keepdims=True)


def call(body, outs, ins, in_specs=None, out_specs=None, grid=None, scratch=(), flops=0, nbytes=0, limit=60, **kw):
    full = lambda a: pl.BlockSpec(a.shape, (lambda *_: (0,) * len(a.shape)))
    if in_specs is None:
        in_specs = [None] * len(ins)
    if out_specs is None:
        out_specs = [None] * len(outs)
    in_specs = [full(a) if s is None else s for a, s in zip(ins, in_specs)]
    out_specs = [full(a) if s is None else s for a, s in zip(outs, out_specs)]
    nbytes = sum(a.size * a.dtype.itemsize for a in ins) + sum(a.size * a.dtype.itemsize for a in outs)
    return pl.pallas_call(
        body,
        out_shape=tuple(outs),
        grid=(1,) if grid is None else grid,
        in_specs=in_specs,
        out_specs=tuple(out_specs),
        scratch_shapes=list(scratch),
        compiler_params=pltpu.CompilerParams(vmem_limit_bytes=limit * 1024 * 1024),
        cost_estimate=pl.CostEstimate(flops=flops, bytes_accessed=nbytes, transcendentals=0),
        **kw,
    )(*ins)


def sds(shape, dtype):
    return jax.ShapeDtypeStruct(shape, dtype)


def loop(n, fn, unroll=1):
    lax.fori_loop(0, n, lambda i, c: (fn(i), c)[1], 0, unroll=unroll)


def cut(i, size):
    return pl.ds(pl.multiple_of(i * size, size), size)


def prep_body(info_ref, in_ref, out_ref):
    out_ref[...] = jnp.zeros_like(out_ref)
    _, slots, length, _ = in_ref.shape
    for i in range(slots):

        @pl.when(i < info_ref[1])
        def _():
            out_ref[i * SLOT_ROWS : i * SLOT_ROWS + length, :] = in_ref[0, i]


def place(info_ref, refs, dst_ref, group=0, cols=slice(None), into=slice(None)):
    if len(refs) == 1:
        parts, _, sub, _ = refs[0].shape
        dst_ref[:, into] = refs[0][:, group, :, cols].reshape(parts * sub, -1)
        return
    for n, ref in enumerate(refs):
        sub = ref.shape[1]
        rows = pl.ds(pl.multiple_of(info_ref[2 + n] * sub, sub), sub)
        dst_ref[rows, into] = ref[group, :, cols]


def qkv_body(info_ref, x_ref, gain_ref, shift_ref, bias_ref, *refs):
    h_ref, qkv_ref, wq_ref, wo_ref = refs[-4:]
    chunks = refs[:-4]
    width = x_ref.shape[1]
    groups = chunks[0].shape[0 if len(chunks) > 1 else 1]
    local = width // groups

    def columns(s, dst_ref):
        for j in range(groups):
            place(info_ref, chunks, dst_ref, j, slice(s * local, (s + 1) * local), slice(j * local, (j + 1) * local))

    step = pl.program_id(0)

    @pl.when(step == 0)
    def _():
        def norm(i):
            rows = cut(i, 128)
            normal, _ = norm_stats(x_ref[rows, :].astype(F32))
            h_ref[rows, :] = (normal * gain_ref[...] + shift_ref[...]).astype(BF)

        loop(ROWS // 128, norm, 2)
        columns(3, wo_ref)

    for s in range(3):
        pl.when(step == s)(functools.partial(columns, s, wq_ref))
    qkv_ref[...] = (dot(h_ref[...], wq_ref[...]) + bias_ref[...]).astype(BF)


def half_masks():
    low_half = lax.broadcasted_iota(jnp.int32, (SLOT_ROWS, 2 * HEAD_DIM), 1) < HEAD_DIM
    return low_half, ~low_half


def attend_body(slots, length, q_ref, k_ref, v_ref, o_ref, p_ref, s_ref):
    masks = half_masks()
    tile = length // 8 * 8
    valid = lax.broadcasted_iota(jnp.int32, (SLOT_ROWS - tile, SLOT_ROWS), 0) < length - tile
    rows = [slice(i * SLOT_ROWS, (i + 1) * SLOT_ROWS) for i in range(slots)]

    def scores(i):
        q = q_ref[rows[i], :] * jnp.bfloat16(0.125)
        k = k_ref[rows[i], :]
        for h in range(2):
            s_ref[h, i] = dot(jnp.where(masks[h], k, jnp.zeros_like(k)), q, NT)

    def softmax(i):
        for h in range(2):
            s_ref[h, i, tile:] = jnp.where(valid, s_ref[h, i, tile:], -1e30)
            s = s_ref[h, i]
            e = jnp.exp(s - jnp.max(s, axis=0, keepdims=True))
            p_ref[h, i] = (e * (1.0 / jnp.sum(e, axis=0, keepdims=True))).astype(BF)

    def mix(i):
        v_t = v_ref[rows[i], :].T
        mixed = [dot(v_t[h * HEAD_DIM : (h + 1) * HEAD_DIM], p_ref[h, i]) for h in range(2)]
        o_ref[rows[i], :] = jnp.concatenate(mixed, axis=0).T.astype(BF)

    for i in range(slots):
        scores(i)
    for i in range(slots):
        softmax(i)
    for i in range(slots):
        mix(i)
    tail = slots * SLOT_ROWS
    o_ref[tail:, :] = jnp.zeros((ROWS - tail, 2 * HEAD_DIM), BF)


def mix_body(x_ref, o_ref, wo_ref, bias_ref, gain_ref, shift_ref, mid_ref, h_ref):
    mid_ref[...] = dot(o_ref[...], wo_ref[...], NT)

    def norm(i):
        rows = cut(i, 128)
        mid = x_ref[rows, :].astype(F32) + (mid_ref[rows, :] + bias_ref[...])
        mid_ref[rows, :] = mid
        normal, _ = norm_stats(mid)
        h_ref[rows, :] = (normal * gain_ref[...] + shift_ref[...]).astype(BF)

    loop(mid_ref.shape[0] // 128, norm)


def hidden_body(n_chunks, info_ref, halves_ref, h_ref, bias_ref, dy_ref, *refs):
    chunks, outs = refs[:n_chunks], refs[n_chunks:-6]
    act_ref, du_ref, sum_ref, *grads = outs
    wb_ref, wc_ref, ht_ref, dyt_ref, gb_ref, gc_ref = refs[-6:]
    cols = wb_ref.shape[1]

    @pl.when(pl.program_id(0) == 0)
    def _():
        ht_ref[...] = h_ref[...].T
        dyt_ref[...] = dy_ref[...].T

    place(info_ref, chunks, wb_ref, 0, slice(0, cols))
    place(info_ref, chunks, wc_ref, 0, slice(cols, 2 * cols))

    def chunk(i, total):
        rows = cut(i, 256)
        u = dot(h_ref[rows, :], wb_ref[...]) + bias_ref[...]
        half = 0.5 * (1.0 + lax.erf(u * 0.7071067811865476))
        act_ref[rows, :] = (u * half).astype(BF)
        slope = half + u * jnp.exp(-0.5 * u * u) * 0.3989422804014327
        du = dot(dy_ref[rows, :], wc_ref[...]) * slope
        du_ref[rows, :] = du.astype(BF)
        return total + colsum(du)

    total = lax.fori_loop(0, ROWS // 256, chunk, jnp.zeros((1, cols), F32), unroll=2)
    sum_ref[...] = jnp.broadcast_to(total, sum_ref.shape)
    gc_ref[...] = dot(dyt_ref[...], act_ref[...]).astype(BF)
    gb_ref[...] = dot(ht_ref[...], du_ref[...]).astype(BF)
    for piece, g_ref in enumerate((gb_ref, gc_ref)):
        lanes = slice(piece * cols, (piece + 1) * cols)
        if len(grads) == 1:
            parts, _, sub, _ = grads[0].shape
            grads[0][:, 0, :, lanes] = g_ref[...].reshape(parts, sub, cols)
            continue
        for n, ref in enumerate(grads):
            sub = ref.shape[1]
            ref[0, :, lanes] = g_ref[pl.ds(pl.multiple_of(halves_ref[2 + n] * sub, sub), sub), :]


def wide_dot(info_ref, left_ref, refs, buf_ref):
    groups, _, cols = buf_ref.shape

    @pl.when(pl.program_id(0) == 0)
    def _():
        for j in range(groups):
            place(info_ref, refs, buf_ref.at[j], j)

    return sum(dot(left_ref[:, j * cols : (j + 1) * cols], buf_ref[j], NT) for j in range(groups))


def down_body(info_ref, act_ref, mid_ref, bias_ref, *refs):
    out_ref, buf_ref = refs[-2:]
    value = mid_ref[...] + wide_dot(info_ref, act_ref, refs[:-2], buf_ref) + bias_ref[...]
    rows = out_ref.shape[0]
    row = pl.program_id(0) * rows + lax.broadcasted_iota(jnp.int32, (rows, 1), 0)
    out_ref[...] = jnp.where(row < info_ref[1] * SLOT_ROWS, value, 0.0).astype(BF)


def weave_body(length, info_ref, a_ref, b_ref, c_ref, d_ref, *refs):
    o_ref = refs[-1]

    def part(start, n, keep):
        x = jnp.concatenate([r[start : start + n, :] for r in (a_ref, b_ref, c_ref, d_ref)], axis=0)
        row = lax.broadcasted_iota(jnp.int32, (4 * n, 4 * n), 0)
        col = lax.broadcasted_iota(jnp.int32, (4 * n, 4 * n), 1)
        take = jnp.where(lax.bitwise_xor(row % 4, info_ref[0]) * n + row // 4 == col, 1.0, 0.0).astype(BF)
        y = dot(take, x).astype(BF).reshape(n, 4, x.shape[1])
        o_ref[0, start : start + keep] = y[:keep]

    full = length // 64 * 64
    for start in range(0, full, 64):
        part(start, 64, 64)
    part(full, 8, length - full)


def add_rows(sums_ref, rows):
    @pl.when(pl.program_id(0) == 0)
    def _():
        sums_ref[...] = jnp.zeros_like(sums_ref)

    for n, value in enumerate(rows):
        sums_ref[n : n + 1, :] += colsum(value)


def mid_back_body(info_ref, dy_ref, du_ref, mid_ref, gain_ref, *refs):
    dmid_ref, dlow_ref, sums_ref, buf_ref = refs[-4:]
    dh = wide_dot(info_ref, du_ref, refs[:-4], buf_ref)
    normal, scale_inv = norm_stats(mid_ref[...])
    dy = dy_ref[...].astype(F32)
    dmid = dy + norm_back(dh, normal, scale_inv, gain_ref[...])
    dmid_ref[...] = dmid
    dlow_ref[...] = dmid.astype(BF)
    add_rows(sums_ref, (dh * normal, dh, dmid, dy))


def out_back_body(dlow_ref, wo_ref, do_ref):
    do_ref[...] = dot(dlow_ref[...], wo_ref[...]).astype(BF)


def attend_back_body(slots, q_ref, k_ref, v_ref, p_ref, do_ref, o_ref, dqkvo_ref, dp_ref, ds_ref):
    dqkvo_ref[3] = o_ref[...]
    masks = half_masks()
    rows = [slice(i * SLOT_ROWS, (i + 1) * SLOT_ROWS) for i in range(slots)]

    def upstream(i):
        v = v_ref[rows[i], :]
        do = do_ref[rows[i], :]
        for h in range(2):
            dp_ref[h, i] = dot(jnp.where(masks[h], v, jnp.zeros_like(v)), do, NT)
        dv = [dot(p_ref[h, i], do) for h in range(2)]
        dqkvo_ref[2, rows[i], :] = jnp.where(masks[0], *dv).astype(BF)

    def softmax_back(i):
        for h in range(2):
            p = p_ref[h, i].astype(F32)
            dp = dp_ref[h, i]
            ds_ref[h, i] = (p * (dp - jnp.sum(p * dp, axis=0, keepdims=True))).astype(BF)

    def downstream(i):
        q = q_ref[rows[i], :] * jnp.bfloat16(0.125)
        k_t = (k_ref[rows[i], :] * jnp.bfloat16(0.125)).T
        dk = [dot(ds_ref[h, i], q) for h in range(2)]
        dqkvo_ref[1, rows[i], :] = jnp.where(masks[0], *dk).astype(BF)
        dq = [dot(k_t[h * HEAD_DIM : (h + 1) * HEAD_DIM], ds_ref[h, i]) for h in range(2)]
        dqkvo_ref[0, rows[i], :] = jnp.concatenate(dq, axis=0).T.astype(BF)

    for i in range(slots):
        upstream(i)
    for i in range(slots):
        softmax_back(i)
    for i in range(slots):
        downstream(i)
    tail = slots * SLOT_ROWS
    dqkvo_ref[:3, tail:, :] = jnp.zeros((3, ROWS - tail, 2 * HEAD_DIM), BF)


def outer_body(info_ref, h_ref, d_ref, dlow_ref, *refs):
    grads, sums_ref, t_ref, g_ref = refs[:-3], refs[-3], refs[-2], refs[-1]
    width = h_ref.shape[1]
    step = pl.program_id(0)

    @pl.when(step == 0)
    def _():
        t_ref[...] = h_ref[...].T
        sums_ref[...] = jnp.zeros_like(sums_ref)

    @pl.when(step == 3)
    def _():
        t_ref[...] = dlow_ref[...].T

    g_ref[...] = dot(t_ref[...], d_ref[0]).astype(BF)
    for n, s in enumerate((0, 2)):

        @pl.when(step == s)
        def _(n=n):
            sums_ref[n : n + 1, :] = colsum(d_ref[0].astype(F32))

    def store(s):
        if len(grads) == 1:
            parts, groups, sub, _ = grads[0].shape
            local = width // groups
            for j in range(groups):
                block = g_ref[:, j * local : (j + 1) * local].reshape(parts, sub, local)
                grads[0][:, j, :, s * local : (s + 1) * local] = block
            return
        for n, ref in enumerate(grads):
            groups, sub, _ = ref.shape
            local = width // groups
            rows = g_ref[pl.ds(pl.multiple_of(info_ref[2 + n] * sub, sub), sub), :]
            for j in range(groups):
                ref[j, :, s * local : (s + 1) * local] = rows[:, j * local : (j + 1) * local]

    for s in range(4):
        pl.when(step == s)(functools.partial(store, s))


def input_back_body(x_ref, d_ref, wq_ref, dmid_ref, gain_ref, out_ref, sums_ref):
    width = x_ref.shape[1]
    dh = sum(dot(d_ref[s], wq_ref[:, s * width : (s + 1) * width], NT) for s in range(3))
    normal, scale_inv = norm_stats(x_ref[...].astype(F32))
    out_ref[...] = (dmid_ref[...] + norm_back(dh, normal, scale_inv, gain_ref[...])).astype(BF)
    add_rows(sums_ref, (dh * normal, dh))


def finish_body(mine_ref, other_ref, qkv_ref, out_ref):
    total = mine_ref[...] + other_ref[...].astype(F32)
    cols = qkv_ref.shape[1]
    qkv_ref[...] = total[:, :cols]
    out_ref[...] = total[:, cols:].T


def block_step(
    inputs, cotangent, counts, norm_gain, norm_shift, qkv_weight, query_bias, value_bias,
    out_weight, out_bias, mlp_gain, mlp_shift, hidden_weight, hidden_bias, down_weight, down_bias,
):
    _, slots, length, width = inputs.shape
    sub = qkv_weight.shape[0]
    local = qkv_weight.shape[1] // 3
    units = hidden_weight.shape[1]
    parts, groups = width // sub, width // local
    ff = units * groups
    axes = ("dp", "mp")
    mine = lax.axis_index("mp")
    ring = sub % 32 == 0

    cycle = list(range(0, parts, 2)) + list(range(parts - 1, 0, -2))
    at = lax.axis_index("dp")
    here = jnp.where(at % 2 == 0, at // 2, parts - 1 - at // 2)
    far = parts // 2
    mp_swap = lambda a, bit: lax.ppermute(a, "mp", [(j, j ^ bit) for j in range(groups)])
    dp_swap = lambda a, bit: lax.ppermute(a, "dp", [(d, d ^ bit) for d in range(parts)])

    def hop(a, odd=True):
        pairs = []
        for p in range(parts):
            for j in range(groups):
                if j % 2 == 0:
                    pairs.append((cycle[p] * groups + j, cycle[(p + 1) % parts] * groups + j))
                elif odd:
                    pairs.append((cycle[p] * groups + j, cycle[(p - 1) % parts] * groups + j))
        return lax.ppermute(a, axes, pairs)

    even = mine % 2 == 0
    row = lambda v: v.reshape(1, -1)
    live = lax.dynamic_index_in_dim(counts, mine, 0, keepdims=False)[0]

    def info_of(offsets):
        spots = here + offsets + 2 * parts
        spots = spots - parts * (spots // parts)
        return jnp.concatenate([info, jnp.where(spots < far, 2 * spots, 2 * (parts - spots) - 1)])

    smem = pl.BlockSpec(memory_space=pltpu.SMEM)
    info = jnp.stack([mine, live])

    mm = 2 * ROWS * width * width
    t_bf = lambda n: sds((ROWS, n), BF)
    t_f = lambda n: sds((ROWS, n), F32)
    block = lambda shape: pl.BlockSpec(shape, lambda i, info: (0,) * len(shape))
    mine_block = pl.BlockSpec((1, slots, length, width), lambda i, info: (info[0], 0, 0, 0))

    def prep(array, count):
        return pl.pallas_call(
            prep_body,
            out_shape=t_bf(width),
            grid_spec=pltpu.PrefetchScalarGridSpec(
                num_scalar_prefetch=1, grid=(1,), in_specs=[mine_block], out_specs=block((ROWS, width))
            ),
            compiler_params=pltpu.CompilerParams(vmem_limit_bytes=24 * 1024 * 1024),
            cost_estimate=pl.CostEstimate(flops=0, bytes_accessed=4 * ROWS * width, transcendentals=0),
        )(jnp.stack([mine, count]), array)

    x = prep(inputs, jnp.int32(slots))
    dy = prep(cotangent, live)

    def scatter_ring(halves):
        got = [mp_swap(halves[far], 1)]
        got += [mp_swap(send, 1) for send in halves[far + 1 :]]

        def term(n):
            return halves[n].astype(F32) + got[n].astype(F32)

        total = term(0)
        for k in range(1, far):
            moved = hop(total.astype(BF))
            total = term(k) + moved.astype(F32)
        total = total.astype(BF)
        last = hop(total, False)
        total = jnp.where(even, last, total).reshape(2, 2, sub, -1)
        split = lambda a, b, first: (jnp.where(first, a, b), jnp.where(first, b, a))
        mine_half, other_half = split(total[:, 0], total[:, 1], even)
        other_half = mp_swap(other_half, 1)
        total = mine_half.astype(F32) + other_half.astype(F32)
        mine_half, other_half = split(total[0], total[1], mine < 2)
        other_half = mp_swap(other_half.astype(BF), 2)
        return mine_half, other_half

    to_right = jnp.arange(far, 0, -1, dtype=jnp.int32)
    to_left = jnp.arange(1 - far, 1, dtype=jnp.int32)
    halves_info = info_of(
        jnp.concatenate([jnp.where(even, to_right, to_left), jnp.where(even, to_left, to_right)])
    )
    halves = lambda n: [sds((groups, sub, n), BF)] * (2 * far)

    shard_bc = jnp.concatenate([hidden_weight, down_weight.T], axis=1)
    shard_a = jnp.concatenate([qkv_weight, out_weight.T], axis=1)
    vectors = jnp.concatenate([query_bias, value_bias, hidden_bias])

    def chip_chunk(shard):
        two = jnp.stack([shard, mp_swap(shard, 2)])
        near = mp_swap(two, 1)
        rel = [two[0], near[0], two[1], near[1]]
        rel = [jnp.where(even, rel[j], rel[j ^ 1]) for j in range(groups)]
        return jnp.stack([jnp.where(mine < 2, rel[j], rel[j ^ 2]) for j in range(groups)])

    def gather_ring(start, between):
        chunks, held = [start], start
        for k in range(1, far):
            held = hop(held)
            held = between(k, held)
            chunks += [held, mp_swap(held, 1)]
        half = hop(jnp.where(even, held[: groups // 2], held[groups // 2 :]))
        other = mp_swap(half, 1)
        first, second = jnp.where(even, half, other), jnp.where(even, other, half)
        return chunks + [jnp.concatenate([first, second])], half

    biases = chip_chunk(row(vectors))[:, 0]
    qb, vb, hb = (biases[:, a:b].reshape(-1) for a, b in ((0, local), (local, 2 * local), (2 * local, None)))
    bias_row = row(jnp.concatenate([qb, jnp.zeros_like(qb), vb]))

    if ring:
        offsets = [0]
        for k in range(1, far):
            offsets += [-k, k]
        ring_info = info_of(jnp.array(offsets + [far], jnp.int32) * jnp.where(even, 1, -1))
        start_bc = chip_chunk(shard_bc)
        prepared = [(x, bias_row)]

        def between(k, held):
            if k == 2:
                held, prepared[0] = lax.optimization_barrier((held, prepared[0]))
            return held

        chunks, _ = gather_ring(chip_chunk(shard_a), between)
        ((x, bias_row),) = prepared
        bc, _ = gather_ring(start_bc, lambda k, held: held)
        piece = lambda n: [pl.BlockSpec((groups, sub, units), lambda i: (0, 0, n))] * len(bc)
    else:
        ring_info = info
        wa = lax.all_gather(shard_a, axes, axis=0, tiled=False).reshape(parts, groups, sub, 4 * local)
        bc = [lax.all_gather(shard_bc, axes, axis=0, tiled=False).reshape(parts, groups, sub, 2 * units)]
        piece = lambda n: [pl.BlockSpec((parts, groups, sub, units), lambda i: (0, 0, 0, n))]
    third = lambda n: pl.BlockSpec((n, width), lambda i: (0, i))
    chunks = chunks if ring else [wa]
    h1, qkv, wq, wo = call(
        qkv_body,
        [t_bf(width), t_bf(3 * width), sds((width, 3 * width), BF), sds((width, width), BF)],
        [ring_info, x, row(norm_gain), row(norm_shift), bias_row] + chunks,
        [smem, None, None, None, third(1)] + [None] * len(chunks),
        [None, third(ROWS), third(width), None],
        (3,),
        flops=3 * mm,
    )
    pair = 2 * HEAD_DIM
    pairs = width // pair
    head = lambda s: pl.BlockSpec((ROWS, pair), lambda i: (0, s * pairs + i))
    p_spec = pl.BlockSpec((2, slots, SLOT_ROWS, SLOT_ROWS), lambda i: (i, 0, 0, 0))
    p_shape = sds((2 * pairs, slots, SLOT_ROWS, SLOT_ROWS), BF)
    mixed, probs = call(
        functools.partial(attend_body, slots, length),
        [t_bf(width), p_shape],
        [qkv, qkv, qkv],
        [head(0), head(1), head(2)],
        [head(0), p_spec],
        (pairs,),
        scratch=[pltpu.VMEM((2, slots, SLOT_ROWS, SLOT_ROWS), F32)],
        flops=mm,
    )
    rows256 = pl.BlockSpec((256, width), lambda i: (i, 0))
    middle, h2 = call(
        mix_body,
        [t_f(width), t_bf(width)],
        [x, mixed, wo, row(out_bias), row(mlp_gain), row(mlp_shift)],
        [rows256, rows256, None, None, None, None],
        [rows256, rows256],
        (ROWS // 256,),
        flops=mm,
    )
    tcols = pl.BlockSpec((ROWS, units), lambda i: (0, i))
    vcols = lambda n: pl.BlockSpec((n, units), lambda i: (0, i))
    group_buf = lambda n: pltpu.VMEM((n, width, units), BF)
    both = [
        pl.BlockSpec((1, sub, 2 * units), lambda i: (i, 0, 0))
        if ring
        else pl.BlockSpec((parts, 1, sub, 2 * units), lambda i: (0, i, 0, 0))
    ]
    grad_shapes = halves(2 * units) if ring else [sds((parts, groups, sub, 2 * units), BF)]
    act, du, sum_hidden, *halves_bc = call(
        functools.partial(hidden_body, len(bc)),
        [t_bf(ff), t_bf(ff), sds((8, ff), F32)] + grad_shapes,
        [ring_info, halves_info if ring else info, h2, row(hb), dy] + bc,
        [smem, smem, None, vcols(1), None] + both * len(bc),
        [tcols, tcols, vcols(8)] + both * len(grad_shapes),
        (groups,),
        scratch=[pltpu.VMEM((width, units), BF)] * 2
        + [pltpu.VMEM((width, ROWS), BF)] * 2
        + [pltpu.VMEM((width, units), BF)] * 2,
        flops=16 * mm,
    )
    g_bc = halves_bc[0]
    if ring:
        s_bc, other = scatter_ring(halves_bc)
        s_bc = s_bc + other.astype(F32)
    else:
        s_bc = lax.psum_scatter(
            g_bc.reshape(parts * groups, sub, 2 * units), axes, scatter_dimension=0, tiled=False
        ).astype(F32)

    own_shape = sds((slots * SLOT_ROWS, width), BF)

    def cross(own):
        crossed = mp_swap(own, 2)
        near = mp_swap(own, 1)
        return [own, near, crossed, mp_swap(crossed, 1)]

    def weave(parts_of):
        image = pl.BlockSpec((SLOT_ROWS, width), lambda i: (i, 0))
        (woven,) = call(
            functools.partial(weave_body, length),
            [sds((slots, length, groups, width), BF)],
            [info, *parts_of],
            [smem] + [image] * 4,
            [pl.BlockSpec((1, length, groups, width), lambda i: (i, 0, 0, 0))],
            (slots,),
            flops=mm,
            limit=24,
        )
        return woven.transpose(2, 0, 1, 3)

    down_info = jnp.concatenate([info, ring_info[2:]])
    act_late, _ = lax.optimization_barrier((act, g_bc))
    wide256 = pl.BlockSpec((256, ff), lambda i: (i, 0))
    (own_out,) = call(
        down_body,
        [own_shape],
        [down_info, act_late, middle, row(down_bias)] + bc,
        [smem, wide256, rows256, None] + piece(1),
        [rows256],
        (ROWS // 256,),
        scratch=[group_buf(groups)],
        flops=4 * mm,
    )
    all_out = weave(cross(own_out))
    du, _ = lax.optimization_barrier((du, own_out))

    dmid, dlow, sums_mid = call(
        mid_back_body,
        [t_f(width), t_bf(width), sds((8, width), F32)],
        [ring_info, dy, du, middle, row(mlp_gain)] + bc,
        [smem, rows256, wide256, rows256, None] + piece(0),
        [rows256, rows256, None],
        (ROWS // 256,),
        scratch=[group_buf(groups)],
        flops=4 * mm,
    )
    (do,) = call(out_back_body, [t_bf(width)], [dlow, wo], flops=mm)
    (dqkvo,) = call(
        functools.partial(attend_back_body, slots),
        [sds((4, ROWS, width), BF)],
        [qkv, qkv, qkv, probs, do, mixed],
        [head(0), head(1), head(2), p_spec, head(0), head(0)],
        [pl.BlockSpec((4, ROWS, pair), lambda i: (0, 0, i))],
        (pairs,),
        scratch=[pltpu.VMEM((2, slots, SLOT_ROWS, SLOT_ROWS), dtype) for dtype in (F32, BF)],
        flops=2 * mm,
    )
    sum_shape = sds((8, width), F32)
    grad_shapes = halves(4 * local) if ring else [sds((parts, groups, sub, 4 * local), BF)]
    *halves_a, sums_qkv = call(
        outer_body,
        grad_shapes + [sum_shape],
        [halves_info if ring else info, h1, dqkvo, dlow],
        [smem, None, pl.BlockSpec((1, ROWS, width), lambda i: (i, 0, 0)), None],
        grid=(4,),
        scratch=[pltpu.VMEM((width, ROWS), BF), pltpu.VMEM((width, width), BF)],
        flops=4 * mm,
    )
    if ring:
        s_qkv, s_out = call(
            finish_body, [sds((sub, 3 * local), F32), sds((local, sub), F32)], scatter_ring(halves_a), limit=16
        )
    else:
        s_a = lax.psum_scatter(
            halves_a[0].reshape(parts * groups, sub, 4 * local), axes, scatter_dimension=0, tiled=False
        ).astype(F32)
        s_qkv, s_out = s_a[:, : 3 * local], s_a[:, 3 * local :].T
    own_grad, sums_in = call(
        input_back_body,
        [own_shape, sum_shape],
        [x, dqkvo, wq, dmid, row(norm_gain)],
        [rows256, pl.BlockSpec((3, 256, width), lambda i: (0, i, 0)), None, rows256, None],
        [rows256, None],
        (ROWS // 256,),
        flops=3 * mm,
    )
    all_grad = weave(cross(own_grad))

    sums = jnp.concatenate(
        [sums_in[:2].reshape(-1), sums_mid[:4].reshape(-1), sums_qkv[:2].reshape(-1), sum_hidden[0]]
    )
    steps = [(mp_swap, 1)] + [(dp_swap, 1 << n) for n in range(parts.bit_length() - 1)] + [(mp_swap, 2)]
    for swap, bit in steps:
        other = swap(sums, bit)
        sums = sums + other
    vec = [sums[n * width : (n + 1) * width] for n in range(8)]
    own = lambda v, n: lax.dynamic_slice_in_dim(v, mine * n, n, 0)
    return (
        all_out,
        all_grad,
        vec[0],
        vec[1],
        s_qkv,
        own(vec[6], local),
        own(vec[7], local),
        s_out,
        vec[4],
        vec[2],
        vec[3],
        s_bc[:, :units],
        own(sums[8 * width :], units),
        s_bc[:, units:].T,
        vec[5],
    )


def solution(mesh):
    token = P(None, "dp", None, None)
    weight, turned = P("dp", "mp"), P("mp", "dp")
    return jax.shard_map(
        block_step,
        mesh=mesh,
        in_specs=(token, token, P(None, "dp"), P(), P(), weight, P("mp"), P("mp"), turned)
        + (P(), P(), P(), weight, P("mp"), turned, P()),
        out_specs=(token, token, P(), P(), weight, P("mp"), P("mp"), turned)
        + (P(), P(), P(), weight, P("mp"), turned, P()),
        check_vma=False,
    )
```

```python
import functools
import jax
import jax.numpy as jnp
from jax import lax
from jax.experimental import pallas as pl
from jax.experimental.pallas import tpu as pltpu
from jax.sharding import PartitionSpec as P


HEAD_DIM = 64
NORM_EPS = 1e-06
SLOT_ROWS = 200
ROWS = 1024
BF = jnp.bfloat16
F32 = jnp.float32
NT = (((1,), (1,)), ((), ()))
NN = (((1,), (0,)), ((), ()))


def dot(a, b, dims=NN):
    return lax.dot_general(a, b, dims, preferred_element_type=F32)


def norm_stats(values):
    center = jnp.mean(values, axis=-1, keepdims=True)
    offset = values - center
    spread = jnp.mean(offset * offset, axis=-1, keepdims=True)
    scale_inv = lax.rsqrt(spread + NORM_EPS)
    return offset * scale_inv, scale_inv


def norm_back(upstream, normal, scale_inv, gain_vec):
    scaled = upstream * gain_vec
    return scale_inv * (
        scaled
        - jnp.mean(scaled, axis=-1, keepdims=True)
        - normal * jnp.mean(scaled * normal, axis=-1, keepdims=True)
    )


def colsum(values):
    return jnp.sum(values, axis=0, keepdims=True)


def call(body, outs, ins, in_specs=None, out_specs=None, grid=None, scratch=(), flops=0, nbytes=0, limit=60, **kw):
    full = lambda a: pl.BlockSpec(a.shape, (lambda *_: (0,) * len(a.shape)))
    if in_specs is None:
        in_specs = [None] * len(ins)
    if out_specs is None:
        out_specs = [None] * len(outs)
    in_specs = [full(a) if s is None else s for a, s in zip(ins, in_specs)]
    out_specs = [full(a) if s is None else s for a, s in zip(outs, out_specs)]
    nbytes = sum(a.size * a.dtype.itemsize for a in ins) + sum(a.size * a.dtype.itemsize for a in outs)
    return pl.pallas_call(
        body,
        out_shape=tuple(outs),
        grid=(1,) if grid is None else grid,
        in_specs=in_specs,
        out_specs=tuple(out_specs),
        scratch_shapes=list(scratch),
        compiler_params=pltpu.CompilerParams(vmem_limit_bytes=limit * 1024 * 1024),
        cost_estimate=pl.CostEstimate(flops=flops, bytes_accessed=nbytes, transcendentals=0),
        **kw,
    )(*ins)


def sds(shape, dtype):
    return jax.ShapeDtypeStruct(shape, dtype)


def loop(n, fn, unroll=1):
    lax.fori_loop(0, n, lambda i, c: (fn(i), c)[1], 0, unroll=unroll)


def cut(i, size):
    return pl.ds(pl.multiple_of(i * size, size), size)


def prep_body(info_ref, in_ref, out_ref):
    out_ref[...] = jnp.zeros_like(out_ref)
    _, slots, length, _ = in_ref.shape
    for i in range(slots):

        @pl.when(i < info_ref[1])
        def _():
            out_ref[i * SLOT_ROWS : i * SLOT_ROWS + length, :] = in_ref[0, i]


def place(info_ref, refs, dst_ref, group=0, cols=slice(None), into=slice(None)):
    if len(refs) == 1:
        parts, _, sub, _ = refs[0].shape
        dst_ref[:, into] = refs[0][:, group, :, cols].reshape(parts * sub, -1)
        return
    for n, ref in enumerate(refs):
        sub = ref.shape[1]
        rows = pl.ds(pl.multiple_of(info_ref[2 + n] * sub, sub), sub)
        dst_ref[rows, into] = ref[group, :, cols]


def qkv_body(info_ref, x_ref, gain_ref, shift_ref, bias_ref, *refs):
    h_ref, qkv_ref, wq_ref, wo_ref = refs[-4:]
    chunks = refs[:-4]
    width = x_ref.shape[1]
    groups = chunks[0].shape[0 if len(chunks) > 1 else 1]
    local = width // groups

    def columns(s, dst_ref):
        for j in range(groups):
            place(info_ref, chunks, dst_ref, j, slice(s * local, (s + 1) * local), slice(j * local, (j + 1) * local))

    step = pl.program_id(0)

    @pl.when(step == 0)
    def _():
        def norm(i):
            rows = cut(i, 128)
            normal, _ = norm_stats(x_ref[rows, :].astype(F32))
            h_ref[rows, :] = (normal * gain_ref[...] + shift_ref[...]).astype(BF)

        loop(ROWS // 128, norm, 2)
        columns(3, wo_ref)

    for s in range(3):
        pl.when(step == s)(functools.partial(columns, s, wq_ref))
    qkv_ref[...] = (dot(h_ref[...], wq_ref[...]) + bias_ref[...]).astype(BF)


def half_masks():
    low_half = lax.broadcasted_iota(jnp.int32, (SLOT_ROWS, 2 * HEAD_DIM), 1) < HEAD_DIM
    return low_half, ~low_half


def attend_body(slots, length, q_ref, k_ref, v_ref, o_ref, p_ref, s_ref):
    masks = half_masks()
    tile = length // 8 * 8
    valid = lax.broadcasted_iota(jnp.int32, (SLOT_ROWS - tile, SLOT_ROWS), 0) < length - tile
    rows = [slice(i * SLOT_ROWS, (i + 1) * SLOT_ROWS) for i in range(slots)]

    def scores(i):
        q = q_ref[rows[i], :] * jnp.bfloat16(0.125)
        k = k_ref[rows[i], :]
        for h in range(2):
            s_ref[h, i] = dot(jnp.where(masks[h], k, jnp.zeros_like(k)), q, NT)

    def softmax(i):
        for h in range(2):
            s_ref[h, i, tile:] = jnp.where(valid, s_ref[h, i, tile:], -1e30)
            s = s_ref[h, i]
            e = jnp.exp(s - jnp.max(s, axis=0, keepdims=True))
            p_ref[h, i] = (e * (1.0 / jnp.sum(e, axis=0, keepdims=True))).astype(BF)

    def mix(i):
        v_t = v_ref[rows[i], :].T
        mixed = [dot(v_t[h * HEAD_DIM : (h + 1) * HEAD_DIM], p_ref[h, i]) for h in range(2)]
        o_ref[rows[i], :] = jnp.concatenate(mixed, axis=0).T.astype(BF)

    for i in range(slots):
        scores(i)
    for i in range(slots):
        softmax(i)
    for i in range(slots):
        mix(i)
    tail = slots * SLOT_ROWS
    o_ref[tail:, :] = jnp.zeros((ROWS - tail, 2 * HEAD_DIM), BF)


def mix_body(x_ref, o_ref, wo_ref, bias_ref, gain_ref, shift_ref, mid_ref, h_ref):
    mid_ref[...] = dot(o_ref[...], wo_ref[...], NT)

    def norm(i):
        rows = cut(i, 128)
        mid = x_ref[rows, :].astype(F32) + (mid_ref[rows, :] + bias_ref[...])
        mid_ref[rows, :] = mid
        normal, _ = norm_stats(mid)
        h_ref[rows, :] = (normal * gain_ref[...] + shift_ref[...]).astype(BF)

    loop(mid_ref.shape[0] // 128, norm)


def hidden_body(n_chunks, info_ref, halves_ref, h_ref, bias_ref, dy_ref, *refs):
    chunks, outs = refs[:n_chunks], refs[n_chunks:-6]
    act_ref, du_ref, sum_ref, *grads = outs
    wb_ref, wc_ref, ht_ref, dyt_ref, gb_ref, gc_ref = refs[-6:]
    cols = wb_ref.shape[1]

    @pl.when(pl.program_id(0) == 0)
    def _():
        ht_ref[...] = h_ref[...].T
        dyt_ref[...] = dy_ref[...].T

    place(info_ref, chunks, wb_ref, 0, slice(0, cols))
    place(info_ref, chunks, wc_ref, 0, slice(cols, 2 * cols))

    def chunk(i, total):
        rows = cut(i, 256)
        u = dot(h_ref[rows, :], wb_ref[...]) + bias_ref[...]
        half = 0.5 * (1.0 + lax.erf(u * 0.7071067811865476))
        act_ref[rows, :] = (u * half).astype(BF)
        slope = half + u * jnp.exp(-0.5 * u * u) * 0.3989422804014327
        du = dot(dy_ref[rows, :], wc_ref[...]) * slope
        du_ref[rows, :] = du.astype(BF)
        return total + colsum(du)

    total = lax.fori_loop(0, ROWS // 256, chunk, jnp.zeros((1, cols), F32), unroll=2)
    sum_ref[...] = jnp.broadcast_to(total, sum_ref.shape)
    gc_ref[...] = dot(dyt_ref[...], act_ref[...]).astype(BF)
    gb_ref[...] = dot(ht_ref[...], du_ref[...]).astype(BF)
    for piece, g_ref in enumerate((gb_ref, gc_ref)):
        lanes = slice(piece * cols, (piece + 1) * cols)
        if len(grads) == 1:
            parts, _, sub, _ = grads[0].shape
            grads[0][:, 0, :, lanes] = g_ref[...].reshape(parts, sub, cols)
            continue
        for n, ref in enumerate(grads):
            sub = ref.shape[1]
            ref[0, :, lanes] = g_ref[pl.ds(pl.multiple_of(halves_ref[2 + n] * sub, sub), sub), :]


def wide_dot(info_ref, left_ref, refs, buf_ref):
    groups, _, cols = buf_ref.shape

    @pl.when(pl.program_id(0) == 0)
    def _():
        for j in range(groups):
            place(info_ref, refs, buf_ref.at[j], j)

    return sum(dot(left_ref[:, j * cols : (j + 1) * cols], buf_ref[j], NT) for j in range(groups))


def down_body(info_ref, act_ref, mid_ref, bias_ref, *refs):
    out_ref, buf_ref = refs[-2:]
    value = mid_ref[...] + wide_dot(info_ref, act_ref, refs[:-2], buf_ref) + bias_ref[...]
    rows = out_ref.shape[0]
    row = pl.program_id(0) * rows + lax.broadcasted_iota(jnp.int32, (rows, 1), 0)
    out_ref[...] = jnp.where(row < info_ref[1] * SLOT_ROWS, value, 0.0).astype(BF)


def weave_body(length, info_ref, a_ref, b_ref, c_ref, d_ref, *refs):
    o_ref = refs[-1]

    def part(start, n, keep):
        x = jnp.concatenate([r[start : start + n, :] for r in (a_ref, b_ref, c_ref, d_ref)], axis=0)
        row = lax.broadcasted_iota(jnp.int32, (4 * n, 4 * n), 0)
        col = lax.broadcasted_iota(jnp.int32, (4 * n, 4 * n), 1)
        take = jnp.where(lax.bitwise_xor(row % 4, info_ref[0]) * n + row // 4 == col, 1.0, 0.0).astype(BF)
        y = dot(take, x).astype(BF).reshape(n, 4, x.shape[1])
        o_ref[0, start : start + keep] = y[:keep]

    full = length // 64 * 64
    for start in range(0, full, 64):
        part(start, 64, 64)
    part(full, 8, length - full)


def add_rows(sums_ref, rows):
    @pl.when(pl.program_id(0) == 0)
    def _():
        sums_ref[...] = jnp.zeros_like(sums_ref)

    for n, value in enumerate(rows):
        sums_ref[n : n + 1, :] += colsum(value)


def mid_back_body(info_ref, dy_ref, du_ref, mid_ref, gain_ref, *refs):
    dmid_ref, dlow_ref, sums_ref, buf_ref = refs[-4:]
    dh = wide_dot(info_ref, du_ref, refs[:-4], buf_ref)
    normal, scale_inv = norm_stats(mid_ref[...])
    dy = dy_ref[...].astype(F32)
    dmid = dy + norm_back(dh, normal, scale_inv, gain_ref[...])
    dmid_ref[...] = dmid
    dlow_ref[...] = dmid.astype(BF)
    add_rows(sums_ref, (dh * normal, dh, dmid, dy))


def out_back_body(dlow_ref, wo_ref, do_ref):
    do_ref[...] = dot(dlow_ref[...], wo_ref[...]).astype(BF)


def attend_back_body(slots, q_ref, k_ref, v_ref, p_ref, do_ref, dqkv_ref, dp_ref, ds_ref):
    masks = half_masks()
    rows = [slice(i * SLOT_ROWS, (i + 1) * SLOT_ROWS) for i in range(slots)]

    def upstream(i):
        v = v_ref[rows[i], :]
        do = do_ref[rows[i], :]
        for h in range(2):
            dp_ref[h, i] = dot(jnp.where(masks[h], v, jnp.zeros_like(v)), do, NT)
        dv = [dot(p_ref[h, i], do) for h in range(2)]
        dqkv_ref[2, rows[i], :] = jnp.where(masks[0], *dv).astype(BF)

    def softmax_back(i):
        for h in range(2):
            p = p_ref[h, i].astype(F32)
            dp = dp_ref[h, i]
            ds_ref[h, i] = (p * (dp - jnp.sum(p * dp, axis=0, keepdims=True))).astype(BF)

    def downstream(i):
        q = q_ref[rows[i], :] * jnp.bfloat16(0.125)
        k_t = (k_ref[rows[i], :] * jnp.bfloat16(0.125)).T
        dk = [dot(ds_ref[h, i], q) for h in range(2)]
        dqkv_ref[1, rows[i], :] = jnp.where(masks[0], *dk).astype(BF)
        dq = [dot(k_t[h * HEAD_DIM : (h + 1) * HEAD_DIM], ds_ref[h, i]) for h in range(2)]
        dqkv_ref[0, rows[i], :] = jnp.concatenate(dq, axis=0).T.astype(BF)

    for i in range(slots):
        upstream(i)
    for i in range(slots):
        softmax_back(i)
    for i in range(slots):
        downstream(i)
    tail = slots * SLOT_ROWS
    dqkv_ref[:, tail:, :] = jnp.zeros((3, ROWS - tail, 2 * HEAD_DIM), BF)


def outer_body(info_ref, h_ref, d_ref, dlow_ref, o_ref, *refs):
    grads, sums_ref, g_ref = refs[:-2], refs[-2], refs[-1]
    width = h_ref.shape[1]
    groups = g_ref.shape[0]
    local = width // groups
    sums_ref[0:1, :] = colsum(d_ref[0].astype(F32))
    sums_ref[1:2, :] = colsum(d_ref[2].astype(F32))
    h_t = h_ref[...].T
    for s in range(4):
        g = (dot(h_t, d_ref[s]) if s < 3 else dot(dlow_ref[...].T, o_ref[...])).astype(BF)
        for j in range(groups):
            g_ref[j, :, s * local : (s + 1) * local] = g[:, j * local : (j + 1) * local]
    if len(grads) == 1:
        parts, _, sub, cols = grads[0].shape
        for j in range(groups):
            grads[0][:, j] = g_ref[j].reshape(parts, sub, cols)
        return
    for n, ref in enumerate(grads):
        sub = ref.shape[1]
        rows = pl.ds(pl.multiple_of(info_ref[2 + n] * sub, sub), sub)
        for j in range(groups):
            ref[j] = g_ref[j, rows, :]


def input_back_body(x_ref, d_ref, wq_ref, dmid_ref, gain_ref, out_ref, sums_ref):
    width = x_ref.shape[1]
    dh = sum(dot(d_ref[s], wq_ref[:, s * width : (s + 1) * width], NT) for s in range(3))
    normal, scale_inv = norm_stats(x_ref[...].astype(F32))
    out_ref[...] = (dmid_ref[...] + norm_back(dh, normal, scale_inv, gain_ref[...])).astype(BF)
    add_rows(sums_ref, (dh * normal, dh))


def finish_body(mine_ref, other_ref, qkv_ref, out_ref):
    total = mine_ref[...] + other_ref[...].astype(F32)
    cols = qkv_ref.shape[1]
    qkv_ref[...] = total[:, :cols]
    out_ref[...] = total[:, cols:].T


def block_step(
    inputs, cotangent, counts, norm_gain, norm_shift, qkv_weight, query_bias, value_bias,
    out_weight, out_bias, mlp_gain, mlp_shift, hidden_weight, hidden_bias, down_weight, down_bias,
):
    _, slots, length, width = inputs.shape
    sub = qkv_weight.shape[0]
    local = qkv_weight.shape[1] // 3
    units = hidden_weight.shape[1]
    parts, groups = width // sub, width // local
    ff = units * groups
    axes = ("dp", "mp")
    mine = lax.axis_index("mp")
    ring = sub % 32 == 0

    cycle = list(range(0, parts, 2)) + list(range(parts - 1, 0, -2))
    at = lax.axis_index("dp")
    here = jnp.where(at % 2 == 0, at // 2, parts - 1 - at // 2)
    far = parts // 2
    mp_swap = lambda a, bit: lax.ppermute(a, "mp", [(j, j ^ bit) for j in range(groups)])
    dp_swap = lambda a, bit: lax.ppermute(a, "dp", [(d, d ^ bit) for d in range(parts)])

    def hop(a, odd=True):
        pairs = []
        for p in range(parts):
            for j in range(groups):
                if j % 2 == 0:
                    pairs.append((cycle[p] * groups + j, cycle[(p + 1) % parts] * groups + j))
                elif odd:
                    pairs.append((cycle[p] * groups + j, cycle[(p - 1) % parts] * groups + j))
        return lax.ppermute(a, axes, pairs)

    even = mine % 2 == 0
    row = lambda v: v.reshape(1, -1)
    live = lax.dynamic_index_in_dim(counts, mine, 0, keepdims=False)[0]

    def info_of(offsets):
        spots = here + offsets + 2 * parts
        spots = spots - parts * (spots // parts)
        return jnp.concatenate([info, jnp.where(spots < far, 2 * spots, 2 * (parts - spots) - 1)])

    smem = pl.BlockSpec(memory_space=pltpu.SMEM)
    info = jnp.stack([mine, live])

    mm = 2 * ROWS * width * width
    t_bf = lambda n: sds((ROWS, n), BF)
    t_f = lambda n: sds((ROWS, n), F32)
    block = lambda shape: pl.BlockSpec(shape, lambda i, info: (0,) * len(shape))
    mine_block = pl.BlockSpec((1, slots, length, width), lambda i, info: (info[0], 0, 0, 0))

    def prep(array, count):
        return pl.pallas_call(
            prep_body,
            out_shape=t_bf(width),
            grid_spec=pltpu.PrefetchScalarGridSpec(
                num_scalar_prefetch=1, grid=(1,), in_specs=[mine_block], out_specs=block((ROWS, width))
            ),
            compiler_params=pltpu.CompilerParams(vmem_limit_bytes=24 * 1024 * 1024),
            cost_estimate=pl.CostEstimate(flops=0, bytes_accessed=4 * ROWS * width, transcendentals=0),
        )(jnp.stack([mine, count]), array)

    x = prep(inputs, jnp.int32(slots))
    dy = prep(cotangent, live)

    def scatter_ring(halves):
        got = [mp_swap(halves[far], 1)]
        got += [mp_swap(send, 1) for send in halves[far + 1 :]]

        def term(n):
            return halves[n].astype(F32) + got[n].astype(F32)

        total = term(0)
        for k in range(1, far):
            moved = hop(total.astype(BF))
            total = term(k) + moved.astype(F32)
        total = total.astype(BF)
        last = hop(total, False)
        total = jnp.where(even, last, total)
        total = total.reshape(2, 2, sub, -1)
        split = lambda a, b, first: (jnp.where(first, a, b), jnp.where(first, b, a))
        mine_half, other_half = split(total[:, 0], total[:, 1], even)
        other_half = mp_swap(other_half, 1)
        total = mine_half.astype(F32) + other_half.astype(F32)
        mine_half, other_half = split(total[0], total[1], mine < 2)
        other_half = mp_swap(other_half.astype(BF), 2)
        return mine_half, other_half

    to_right = jnp.arange(far, 0, -1, dtype=jnp.int32)
    to_left = jnp.arange(1 - far, 1, dtype=jnp.int32)
    halves_info = info_of(
        jnp.concatenate([jnp.where(even, to_right, to_left), jnp.where(even, to_left, to_right)])
    )
    halves = lambda n: [sds((groups, sub, n), BF)] * (2 * far)

    shard_bc = jnp.concatenate([hidden_weight, down_weight.T], axis=1)
    shard_a = jnp.concatenate([qkv_weight, out_weight.T], axis=1)
    vectors = jnp.concatenate([query_bias, value_bias, hidden_bias])

    def chip_chunk(shard):
        two = jnp.stack([shard, mp_swap(shard, 2)])
        near = mp_swap(two, 1)
        rel = [two[0], near[0], two[1], near[1]]
        rel = [jnp.where(even, rel[j], rel[j ^ 1]) for j in range(groups)]
        return jnp.stack([jnp.where(mine < 2, rel[j], rel[j ^ 2]) for j in range(groups)])

    def gather_ring(start, between):
        chunks, held = [start], start
        for k in range(1, far):
            held = hop(held)
            held = between(k, held)
            chunks += [held, mp_swap(held, 1)]
        half = hop(jnp.where(even, held[: groups // 2], held[groups // 2 :]))
        other = mp_swap(half, 1)
        first, second = jnp.where(even, half, other), jnp.where(even, other, half)
        return chunks + [jnp.concatenate([first, second])], half

    biases = chip_chunk(row(vectors))[:, 0]
    qb, vb, hb = (biases[:, a:b].reshape(-1) for a, b in ((0, local), (local, 2 * local), (2 * local, None)))
    bias_row = row(jnp.concatenate([qb, jnp.zeros_like(qb), vb]))

    if ring:
        offsets = [0]
        for k in range(1, far):
            offsets += [-k, k]
        ring_info = info_of(jnp.array(offsets + [far], jnp.int32) * jnp.where(even, 1, -1))
        start_bc = chip_chunk(shard_bc)
        prepared = [(x, bias_row)]

        def between(k, held):
            if k == 2:
                held, prepared[0] = lax.optimization_barrier((held, prepared[0]))
            return held

        chunks, _ = gather_ring(chip_chunk(shard_a), between)
        ((x, bias_row),) = prepared
        bc, _ = gather_ring(start_bc, lambda k, held: held)
        piece = lambda n: [pl.BlockSpec((groups, sub, units), lambda i: (0, 0, n))] * len(bc)
    else:
        ring_info = info
        wa = lax.all_gather(shard_a, axes, axis=0, tiled=False).reshape(parts, groups, sub, 4 * local)
        bc = [lax.all_gather(shard_bc, axes, axis=0, tiled=False).reshape(parts, groups, sub, 2 * units)]
        piece = lambda n: [pl.BlockSpec((parts, groups, sub, units), lambda i: (0, 0, 0, n))]
    third = lambda n: pl.BlockSpec((n, width), lambda i: (0, i))
    chunks = chunks if ring else [wa]
    h1, qkv, wq, wo = call(
        qkv_body,
        [t_bf(width), t_bf(3 * width), sds((width, 3 * width), BF), sds((width, width), BF)],
        [ring_info, x, row(norm_gain), row(norm_shift), bias_row] + chunks,
        [smem, None, None, None, third(1)] + [None] * len(chunks),
        [None, third(ROWS), third(width), None],
        (3,),
        flops=3 * mm,
    )
    pair = 2 * HEAD_DIM
    pairs = width // pair
    head = lambda s: pl.BlockSpec((ROWS, pair), lambda i: (0, s * pairs + i))
    p_spec = pl.BlockSpec((2, slots, SLOT_ROWS, SLOT_ROWS), lambda i: (i, 0, 0, 0))
    p_shape = sds((2 * pairs, slots, SLOT_ROWS, SLOT_ROWS), BF)
    mixed, probs = call(
        functools.partial(attend_body, slots, length),
        [t_bf(width), p_shape],
        [qkv, qkv, qkv],
        [head(0), head(1), head(2)],
        [head(0), p_spec],
        (pairs,),
        scratch=[pltpu.VMEM((2, slots, SLOT_ROWS, SLOT_ROWS), F32)],
        flops=mm,
    )
    rows256 = pl.BlockSpec((256, width), lambda i: (i, 0))
    middle, h2 = call(
        mix_body,
        [t_f(width), t_bf(width)],
        [x, mixed, wo, row(out_bias), row(mlp_gain), row(mlp_shift)],
        [rows256, rows256, None, None, None, None],
        [rows256, rows256],
        (ROWS // 256,),
        flops=mm,
    )
    tcols = pl.BlockSpec((ROWS, units), lambda i: (0, i))
    vcols = lambda n: pl.BlockSpec((n, units), lambda i: (0, i))
    group_buf = lambda n: pltpu.VMEM((n, width, units), BF)
    both = [
        pl.BlockSpec((1, sub, 2 * units), lambda i: (i, 0, 0))
        if ring
        else pl.BlockSpec((parts, 1, sub, 2 * units), lambda i: (0, i, 0, 0))
    ]
    grad_shapes = halves(2 * units) if ring else [sds((parts, groups, sub, 2 * units), BF)]
    act, du, sum_hidden, *halves_bc = call(
        functools.partial(hidden_body, len(bc)),
        [t_bf(ff), t_bf(ff), sds((8, ff), F32)] + grad_shapes,
        [ring_info, halves_info if ring else info, h2, row(hb), dy] + bc,
        [smem, smem, None, vcols(1), None] + both * len(bc),
        [tcols, tcols, vcols(8)] + both * len(grad_shapes),
        (groups,),
        scratch=[pltpu.VMEM((width, units), BF)] * 2
        + [pltpu.VMEM((width, ROWS), BF)] * 2
        + [pltpu.VMEM((width, units), BF)] * 2,
        flops=16 * mm,
    )
    g_bc = halves_bc[0]
    if ring:
        s_bc, other = scatter_ring(halves_bc)
        s_bc = s_bc + other.astype(F32)
    else:
        s_bc = lax.psum_scatter(
            g_bc.reshape(parts * groups, sub, 2 * units), axes, scatter_dimension=0, tiled=False
        ).astype(F32)

    own_shape = sds((slots * SLOT_ROWS, width), BF)

    def cross(own):
        crossed = mp_swap(own, 2)
        near = mp_swap(own, 1)
        return [own, near, crossed, mp_swap(crossed, 1)]

    def weave(parts_of):
        image = pl.BlockSpec((SLOT_ROWS, width), lambda i: (i, 0))
        (woven,) = call(
            functools.partial(weave_body, length),
            [sds((slots, length, groups, width), BF)],
            [info, *parts_of],
            [smem] + [image] * 4,
            [pl.BlockSpec((1, length, groups, width), lambda i: (i, 0, 0, 0))],
            (slots,),
            flops=mm,
            limit=24,
        )
        return woven.transpose(2, 0, 1, 3)

    down_info = jnp.concatenate([info, ring_info[2:]])
    act_late, _ = lax.optimization_barrier((act, g_bc))
    wide256 = pl.BlockSpec((256, ff), lambda i: (i, 0))
    (own_out,) = call(
        down_body,
        [own_shape],
        [down_info, act_late, middle, row(down_bias)] + bc,
        [smem, wide256, rows256, None] + piece(1),
        [rows256],
        (ROWS // 256,),
        scratch=[group_buf(groups)],
        flops=4 * mm,
    )
    all_out = weave(cross(own_out))
    du, _ = lax.optimization_barrier((du, own_out))

    dmid, dlow, sums_mid = call(
        mid_back_body,
        [t_f(width), t_bf(width), sds((8, width), F32)],
        [ring_info, dy, du, middle, row(mlp_gain)] + bc,
        [smem, rows256, wide256, rows256, None] + piece(0),
        [rows256, rows256, None],
        (ROWS // 256,),
        scratch=[group_buf(groups)],
        flops=4 * mm,
    )
    (do,) = call(out_back_body, [t_bf(width)], [dlow, wo], flops=mm)
    (dqkv,) = call(
        functools.partial(attend_back_body, slots),
        [sds((3, ROWS, width), BF)],
        [qkv, qkv, qkv, probs, do],
        [head(0), head(1), head(2), p_spec, head(0)],
        [pl.BlockSpec((3, ROWS, pair), lambda i: (0, 0, i))],
        (pairs,),
        scratch=[pltpu.VMEM((2, slots, SLOT_ROWS, SLOT_ROWS), dtype) for dtype in (F32, BF)],
        flops=2 * mm,
    )
    sum_shape = sds((8, width), F32)
    grad_shapes = halves(4 * local) if ring else [sds((parts, groups, sub, 4 * local), BF)]
    *halves_a, sums_qkv = call(
        outer_body,
        grad_shapes + [sum_shape],
        [halves_info if ring else info, h1, dqkv, dlow, mixed],
        [smem, None, None, None, None],
        scratch=[pltpu.VMEM((groups, width, width), BF)],
        flops=4 * mm,
    )
    if ring:
        s_qkv, s_out = call(
            finish_body, [sds((sub, 3 * local), F32), sds((local, sub), F32)], scatter_ring(halves_a), limit=16
        )
    else:
        s_a = lax.psum_scatter(
            halves_a[0].reshape(parts * groups, sub, 4 * local), axes, scatter_dimension=0, tiled=False
        ).astype(F32)
        s_qkv, s_out = s_a[:, : 3 * local], s_a[:, 3 * local :].T
    own_grad, sums_in = call(
        input_back_body,
        [own_shape, sum_shape],
        [x, dqkv, wq, dmid, row(norm_gain)],
        [rows256, pl.BlockSpec((3, 256, width), lambda i: (0, i, 0)), None, rows256, None],
        [rows256, None],
        (ROWS // 256,),
        flops=3 * mm,
    )
    all_grad = weave(cross(own_grad))

    sums = jnp.concatenate(
        [sums_in[:2].reshape(-1), sums_mid[:4].reshape(-1), sums_qkv[:2].reshape(-1), sum_hidden[0]]
    )
    steps = [(mp_swap, 1)] + [(dp_swap, 1 << n) for n in range(parts.bit_length() - 1)] + [(mp_swap, 2)]
    for swap, bit in steps:
        other = swap(sums, bit)
        sums = sums + other
    vec = [sums[n * width : (n + 1) * width] for n in range(8)]
    own = lambda v, n: lax.dynamic_slice_in_dim(v, mine * n, n, 0)
    return (
        all_out,
        all_grad,
        vec[0],
        vec[1],
        s_qkv,
        own(vec[6], local),
        own(vec[7], local),
        s_out,
        vec[4],
        vec[2],
        vec[3],
        s_bc[:, :units],
        own(sums[8 * width :], units),
        s_bc[:, units:].T,
        vec[5],
    )


def solution(mesh):
    token = P(None, "dp", None, None)
    weight, turned = P("dp", "mp"), P("mp", "dp")
    return jax.shard_map(
        block_step,
        mesh=mesh,
        in_specs=(token, token, P(None, "dp"), P(), P(), weight, P("mp"), P("mp"), turned)
        + (P(), P(), P(), weight, P("mp"), turned, P()),
        out_specs=(token, token, P(), P(), weight, P("mp"), P("mp"), turned)
        + (P(), P(), P(), weight, P("mp"), turned, P()),
        check_vma=False,
    )
```
